512 devices in a mesh: ctx: 64 (over z, y_hi, core), dp: 8 (over y_lo, x).
Axes of the slice: x: 4, y: 8 (y_hi: 4, y_lo: 2; y = y_hi * 2 + y_lo), z: 8, core: 2. Of those that a mesh axis runs over, the one named last changes fastest.
Arguments:
- queries: bfloat16 [8, 8192, 512], P('dp', 'ctx'), may hold values from -8 to 8
- keys: bfloat16 [8, 8192, 128], P('dp', 'ctx'), may hold values from -8 to 8
- values: bfloat16 [8, 8192, 128], P('dp', 'ctx'), may hold values from -6 to 6
- grad_out: bfloat16 [8, 8192, 512], P('dp', 'ctx'), may hold values from -60 to 60
- doc_starts: int32 [8, 8], P('dp'), may hold values from 0 to 8064, as said below
Outputs:
- attended: bfloat16 [8, 8192, 512], P('dp', 'ctx')
- grad_queries: bfloat16 [8, 8192, 512], P('dp', 'ctx')
- grad_keys: bfloat16 [8, 8192, 128], P('dp', 'ctx')
- grad_values: bfloat16 [8, 8192, 128], P('dp', 'ctx')
The draws below stay inside these ranges and needn't reach their ends.
Inputs may be any that keep to these rules, and one draw needn't show every extreme that they name: `doc_starts`: row b lists the first positions of the 8 documents packed in sequence b: the first is 0, they rise strictly, all are multiples of 128, and in some sequence the last document has exactly 128 tokens.
All inputs are finite; a program needn't handle non-finite values.
Results may differ from the reference program's by a relative error of at most 0.034.
Values may be sent and summed in bfloat16 or wider, within the bound.
No kernel may reach another device: no remote copies, remote signals or barrier semaphores. Data moves between devices by JAX's collectives and lax.ppermute only.
A program may use at most 64 MiB of HBM per device.

```python
import jax
import jax.numpy as jnp
from jax import lax

HD = 128
HQ = 4
TOK_DEV = 128
DOCS = 8
ALIGN = 128
SEQ = 8192
BATCH = 8
N_CTX = 64


def draw_queries(key, part):
    shape = (BATCH, SEQ, HQ * HD)
    base = jnp.clip(jax.random.normal(jax.random.fold_in(key, 1), shape, jnp.float32), -3.0, 3.0)
    return jnp.clip(base, -8.0, 8.0).astype(jnp.bfloat16)


def draw_keys(key, part):
    shape = (BATCH, SEQ, HD)
    base = jnp.clip(jax.random.normal(jax.random.fold_in(key, 11), shape, jnp.float32), -3.0, 3.0)
    return jnp.clip(base, -8.0, 8.0).astype(jnp.bfloat16)


def draw_grad_out(key, part):
    shape = (BATCH, SEQ, HQ * HD)
    blocks = SEQ // TOK_DEV
    seq_ramp = 1.0 + 0.75 * (jnp.arange(SEQ) // TOK_DEV).astype(jnp.float32) / (blocks - 1)
    batch_ramp = 1.0 + 0.75 * jnp.arange(BATCH).astype(jnp.float32) / max(BATCH - 1, 1)
    row_scale = jnp.exp(jax.random.uniform(jax.random.fold_in(key, 21), (BATCH, SEQ, 1), jnp.float32, 0.0, jnp.log(3.0)))
    ramp = seq_ramp[None, :, None] * batch_ramp[:, None, None]
    base = jnp.clip(jax.random.normal(jax.random.fold_in(key, 22), shape, jnp.float32), -3.0, 3.0)
    return jnp.clip(base * row_scale * ramp, -60.0, 60.0).astype(jnp.bfloat16)


def draw_doc_starts(key, part):
    count = SEQ // ALIGN

    def one_row(index):
        row_key = jax.random.fold_in(key, 100 + index)
        order = jax.random.permutation(row_key, count - 2) + 1
        last = jnp.where(index == 0, count - 1, order[DOCS - 2])
        chosen = jnp.sort(jnp.concatenate([order[:DOCS - 2], last[None]]))
        return jnp.concatenate([jnp.zeros((1,), jnp.int32), chosen.astype(jnp.int32)]) * ALIGN
    return jax.vmap(one_row)(jnp.arange(BATCH, dtype=jnp.int32)).astype(jnp.int32)


def shard_levels(own_key, dims, shards, low, top_value):
    def one(dim, shards_of):
        steps = jax.random.uniform(jax.random.fold_in(jax.random.fold_in(own_key, 6), dim), (shards_of,), jnp.float32, low / len(shards), top_value / len(shards))
        return jnp.repeat(jnp.exp(steps), dims[dim] // shards_of).reshape((-1,) + (1,) * (len(dims) - dim - 1))

    loudness = one(*shards[0])
    for cut in shards[1:]:
        loudness = loudness * one(*cut)
    return loudness


def normal_values(key, dims, spread, limit, split=(), kind=jnp.bfloat16):
    drawn = spread * jax.random.normal(key, dims, jnp.float32)
    if split:
        drawn = drawn * shard_levels(key, dims, split, -0.22, 0.18)
    return jnp.clip(drawn, -limit, limit).astype(kind)


def setup_inputs(seed: int = 0) -> dict:
    arg_keys = jax.random.split(jax.random.key(seed), 6)
    return {
        "queries": draw_queries(jax.random.fold_in(arg_keys[5], 71), 0),
        "keys": draw_keys(jax.random.fold_in(arg_keys[5], 71), 0),
        "values": normal_values(arg_keys[2], (BATCH, SEQ, HD), 1.0, 6.0, ((0, 8), (1, 64))),
        "grad_out": draw_grad_out(jax.random.fold_in(arg_keys[5], 71), 0),
        "doc_starts": draw_doc_starts(jax.random.fold_in(arg_keys[5], 71), 0),
    }


masked_floor = -1e+30

def zig_positions(index, tok, nctx):
    block = index // tok
    rest = index % tok
    half = tok // 2
    return jnp.where(rest < half, block * half + rest, (2 * nctx - 1 - block) * half + rest - half).astype(jnp.int32)

def doc_number(positions, starts):
    return (lax.optimization_barrier(jnp.sum((starts[None, :] <= positions[:, None]).astype(jnp.int32), axis=1)) - 1).astype(jnp.int32)

def seq_grads(queries, keys, values, grad_out, starts):
    scale = 1.0 / jnp.sqrt(jnp.float32(HD))
    positions = zig_positions(jnp.arange(SEQ, dtype=jnp.int32), TOK_DEV, N_CTX)
    docs = doc_number(positions, starts)
    query3 = queries.reshape(SEQ, HQ, HD).astype(jnp.float32)
    grad3 = grad_out.reshape(SEQ, HQ, HD).astype(jnp.float32)
    key_blocks = keys.reshape(N_CTX, TOK_DEV, HD)
    value_blocks = values.reshape(N_CTX, TOK_DEV, HD)
    pos_blocks = positions.reshape(N_CTX, TOK_DEV)
    doc_blocks = docs.reshape(N_CTX, TOK_DEV)

    def mask_of(kpos, kdoc):
        return ((kpos[None, :] <= positions[:, None]) & (kdoc[None, :] == docs[:, None]))[:, None, :]

    def logits_of(key_block):
        return jnp.einsum('qhd,kd->qhk', query3, key_block.astype(jnp.float32)) * scale

    def forward_step(carry, item):
        acc, run_max, run_sum = carry
        key_block, value_block, kpos, kdoc = item
        allowed = mask_of(kpos, kdoc)
        logits = logits_of(key_block)
        block_max = lax.optimization_barrier(jnp.max(jnp.where(allowed, logits, masked_floor), axis=2))
        expd = jnp.where(allowed, jnp.exp(logits - block_max[:, :, None]), 0.0)
        part = jnp.einsum('qhk,kd->qhd', expd.astype(jnp.bfloat16).astype(jnp.float32), value_block.astype(jnp.float32))
        new_max = jnp.maximum(run_max, block_max)
        old_w = jnp.exp(run_max - new_max)
        new_w = jnp.exp(block_max - new_max)
        acc = acc * old_w[:, :, None] + part * new_w[:, :, None]
        run_sum = run_sum * old_w + lax.optimization_barrier(jnp.sum(expd, axis=2)) * new_w
        return ((acc, new_max, run_sum), None)
    init = (jnp.zeros((SEQ, HQ, HD), jnp.float32), jnp.full((SEQ, HQ), masked_floor, jnp.float32), jnp.zeros((SEQ, HQ), jnp.float32))
    (acc, run_max, run_sum), _ = lax.scan(forward_step, init, (key_blocks, value_blocks, pos_blocks, doc_blocks))
    attended = (acc / run_sum[:, :, None]).astype(jnp.bfloat16)
    log_total = run_max + jnp.log(run_sum)
    delta = lax.optimization_barrier(jnp.sum(grad3 * attended.astype(jnp.float32), axis=2))

    def backward_step(grad_q, item):
        key_block, value_block, kpos, kdoc = item
        allowed = mask_of(kpos, kdoc)
        logits = logits_of(key_block)
        prob = jnp.where(allowed, jnp.exp(logits - log_total[:, :, None]), 0.0)
        grad_value = jnp.einsum('qhk,qhd->kd', prob.astype(jnp.bfloat16).astype(jnp.float32), grad3)
        grad_prob = jnp.einsum('qhd,kd->qhk', grad3, value_block.astype(jnp.float32))
        grad_logit = (prob * (grad_prob - delta[:, :, None]) * scale).astype(jnp.bfloat16).astype(jnp.float32)
        grad_q = grad_q + jnp.einsum('qhk,kd->qhd', grad_logit, key_block.astype(jnp.float32))
        grad_key = jnp.einsum('qhk,qhd->kd', grad_logit, query3)
        return (grad_q, (grad_key, grad_value))
    grad_q, (grad_k, grad_v) = lax.scan(backward_step, jnp.zeros((SEQ, HQ, HD), jnp.float32), (key_blocks, value_blocks, pos_blocks, doc_blocks))
    return (attended.reshape(SEQ, HQ * HD), grad_q.reshape(SEQ, HQ * HD), grad_k.reshape(SEQ, HD), grad_v.reshape(SEQ, HD))

def reference(queries, keys, values, grad_out, doc_starts):
    attended, grad_q, grad_k, grad_v = lax.map(lambda items: seq_grads(*items), (queries, keys, values, grad_out, doc_starts))
    total = jnp.sum(grad_q * grad_q) + jnp.sum(grad_k * grad_k) + jnp.sum(grad_v * grad_v)
    count = BATCH * SEQ * (HQ * HD + 2 * HD)
    factor = 1.0 / jnp.sqrt(total / count + 1e-06)
    return (attended, (grad_q * factor).astype(jnp.bfloat16), (grad_k * factor).astype(jnp.bfloat16), (grad_v * factor).astype(jnp.bfloat16))
```

```python
import functools
import math

import jax
import jax.numpy as jnp
from jax import lax
from jax.experimental import pallas as pl
from jax.experimental.pallas import tpu as pltpu
from jax.sharding import PartitionSpec as P

FLOOR = -1e30
GROUP = 4


def dot(a, b, ca, cb):
    return lax.dot_general(a, b, (((ca,), (cb,)), ((), ())), preferred_element_type=jnp.float32)


def attend_kernel(nctx, heads, info, q_ref, do_ref, kv_ref, att_ref, dq_ref, sq_ref, dkv_ref, s_scr):
    tok = q_ref.shape[1]
    half = tok // 2
    width = kv_ref.shape[2] // 2
    cols = heads * half
    tile = GROUP * half
    runs = 2 * nctx
    scale = 1.0 / math.sqrt(width)
    log2_scale = scale * math.log2(math.e)
    me = info[0]

    dkv_ref[...] = jnp.zeros_like(dkv_ref)

    row = lax.broadcasted_iota(jnp.int32, (tile, 1), 0)
    row_run = row // half
    row_rest = row % half
    col_rest = lax.broadcasted_iota(jnp.int32, (1, cols), 1) % half
    squares = jnp.float32(0.0)

    def stacked(ref, r0):
        return jnp.concatenate(
            [ref[0, r0 : r0 + half, h * width : (h + 1) * width] for h in range(heads)], axis=0
        )

    for side in (0, 1):
        r0 = side * half
        run = me if side == 0 else runs - 1 - me
        first = info[1 + side]
        query_pos = run * half + col_rest
        first_pos = first * half
        q2 = stacked(q_ref, r0)
        do2 = stacked(do_ref, r0)

        if side == 0:
            regions = [(0, first // GROUP, me // GROUP + 1)]
        else:
            regions = [
                (0, jnp.minimum(first // GROUP, nctx // GROUP), jnp.int32(nctx // GROUP)),
                (1, me // GROUP, (runs - 1 - jnp.maximum(first, nctx)) // GROUP + 1),
            ]

        def over(body, carry):
            for part, low, high in regions:
                carry = lax.fori_loop(low, high, functools.partial(body, part), carry)
            return carry

        def rows_of(part, t):
            return pl.ds(pl.multiple_of(part * nctx * half + t * tile, tile), tile)

        def block_of(part, t, lo, hi):
            return (
                pl.ds(t * GROUP, GROUP),
                slice(part * half, (part + 1) * half),
                slice(lo, hi),
            )

        def key_tile(part, t):
            return kv_ref[block_of(part, t, 0, width)].reshape(tile, width)

        def value_tile(part, t):
            return kv_ref[block_of(part, t, width, 2 * width)].reshape(tile, width)

        def scores(part, t, biggest):
            s = dot(key_tile(part, t), q2, 1, 1)
            block_run = t * GROUP + row_run
            key_run = block_run if part == 0 else runs - 1 - block_run
            key_pos = key_run * half + row_rest
            key_pos = jnp.where(key_pos >= first_pos, key_pos, jnp.int32(2**30))
            s = jnp.where(key_pos <= query_pos, s, FLOOR)
            s_scr[rows_of(part, t), :] = s
            return jnp.maximum(biggest, jnp.max(s.reshape(tile // 8, 8, cols), axis=0))

        biggest = over(scores, jnp.full((8, cols), FLOOR, jnp.float32))
        top = jnp.max(biggest, axis=0, keepdims=True)

        def forward(part, t, carry):
            total, acc = carry
            rows = rows_of(part, t)
            e = jnp.exp2((s_scr[rows, :] - top) * log2_scale)
            s_scr[rows, :] = e
            total = total + jnp.sum(e.reshape(tile // 8, 8, cols), axis=0)
            acc = acc + dot(value_tile(part, t), e.astype(jnp.bfloat16), 0, 0)
            return total, acc

        total, acc = over(
            forward, (jnp.zeros((8, cols), jnp.float32), jnp.zeros((width, cols), jnp.float32))
        )
        inverse = 1.0 / jnp.sum(total, axis=0, keepdims=True)
        att_t = acc * inverse
        att = att_t.T.astype(jnp.bfloat16)
        for h in range(heads):
            att_ref[0, r0 : r0 + half, h * width : (h + 1) * width] = att[h * half : (h + 1) * half]
        do_t = do2.astype(jnp.float32).T
        delta = jnp.sum(do_t * att_t.astype(jnp.bfloat16).astype(jnp.float32), axis=0, keepdims=True)

        def backward(part, t, dq_t):
            rows = rows_of(part, t)
            p = s_scr[rows, :] * inverse
            dp = dot(value_tile(part, t), do2, 1, 1)
            ds = (p * (dp - delta)).astype(jnp.bfloat16)
            dv = dot(p.astype(jnp.bfloat16), do2, 1, 0)
            dk = dot(ds, q2, 1, 0) * scale
            for lo, new in ((0, dk), (width, dv)):
                where = block_of(part, t, lo, lo + width)
                new = new.reshape(GROUP, half, width)
                if side == 1 and part == 0:
                    new = new + dkv_ref[where].astype(jnp.float32)
                dkv_ref[where] = new.astype(dkv_ref.dtype)
            return dq_t + dot(key_tile(part, t), ds, 0, 0)

        dq_t = over(backward, jnp.zeros((width, cols), jnp.float32)) * scale
        squares = squares + jnp.sum(dq_t * dq_t)
        dq = dq_t.T
        for h in range(heads):
            dq_ref[0, r0 : r0 + half, h * width : (h + 1) * width] = dq[h * half : (h + 1) * half]

    sq_ref[0, 0] = squares


def attend(info, queries, grad_out, kv, nctx):
    tok = queries.shape[1]
    width = kv.shape[2] // 2
    heads = queries.shape[2] // width
    vmem = pl.BlockSpec(memory_space=pltpu.VMEM)
    smem = pl.BlockSpec(memory_space=pltpu.SMEM)
    return pl.pallas_call(
        functools.partial(attend_kernel, nctx, heads),
        out_shape=(
            jax.ShapeDtypeStruct(queries.shape, jnp.bfloat16),
            jax.ShapeDtypeStruct(queries.shape, jnp.float32),
            jax.ShapeDtypeStruct((1, 1), jnp.float32),
            jax.ShapeDtypeStruct(kv.shape, jnp.bfloat16),
        ),
        in_specs=[smem, vmem, vmem, vmem],
        out_specs=(vmem, vmem, smem, vmem),
        scratch_shapes=[pltpu.VMEM((nctx * tok, heads * tok // 2), jnp.float32)],
        compiler_params=pltpu.CompilerParams(vmem_limit_bytes=48 * 1024 * 1024),
    )(info, queries, grad_out, kv)


def per_device(queries, keys, values, grad_out, doc_starts):
    tok = queries.shape[1]
    width = keys.shape[2]
    nctx = lax.axis_size("ctx")
    ndata = lax.axis_size("dp")
    half = tok // 2
    me = lax.axis_index("ctx")
    starts = doc_starts[0] // half
    low_first = jnp.max(jnp.where(starts <= me, starts, 0))
    high_first = jnp.max(jnp.where(starts <= 2 * nctx - 1 - me, starts, 0))
    info = jnp.stack([me, low_first, high_first]).astype(jnp.int32)

    kv = jnp.concatenate([keys, values], axis=2)
    kv = lax.all_gather(kv, "ctx", axis=0, tiled=True)
    attended, query_raw, squares, partial = attend(info, queries, grad_out, kv, nctx)
    raw = lax.psum_scatter(partial, "ctx", scatter_dimension=0, tiled=True).astype(jnp.float32)
    total = lax.psum(jnp.sum(raw * raw) + squares[0, 0], ("ctx", "dp"))
    count = float(ndata * nctx * tok * (queries.shape[2] + 2 * width))
    factor = lax.rsqrt(total / count + 1e-06)
    out_query = (query_raw * factor).astype(jnp.bfloat16)
    scaled = (raw * factor).astype(jnp.bfloat16)
    return attended, out_query, scaled[:, :, :width], scaled[:, :, width:]


def solution(mesh):
    spec = P("dp", "ctx", None)
    return jax.shard_map(
        per_device,
        mesh=mesh,
        in_specs=(spec, spec, spec, spec, P("dp", None)),
        out_specs=(spec, spec, spec, spec),
        check_vma=False,
    )
```

```python
import functools
import math

import jax
import jax.numpy as jnp
from jax import lax
from jax.experimental import pallas as pl
from jax.experimental.pallas import tpu as pltpu
from jax.sharding import Mesh
from jax.sharding import PartitionSpec as P

FLOOR = -1e30
NZ, NY, NC = 8, 4, 2
FIELDS = 6
VMEM = pl.BlockSpec(memory_space=pltpu.VMEM)
SMEM = pl.BlockSpec(memory_space=pltpu.SMEM)
PARAMS = pltpu.CompilerParams(vmem_limit_bytes=40 * 1024 * 1024)


def dot(a, b, ca, cb):
    return lax.dot_general(a, b, (((ca,), (cb,)), ((), ())), preferred_element_type=jnp.float32)


def visits(doc_starts, tok, z, y, c):
    nctx = NZ * NY * NC
    half = tok // 2
    source = jnp.repeat((y + jnp.arange(NY, dtype=jnp.int32)) % NY, 2)
    upper = jnp.tile(jnp.arange(2, dtype=jnp.int32), NY)
    base = (z * NY + source) * NC + c
    run = jnp.where(upper == 1, 2 * nctx - 1 - base, base)
    starts = doc_starts // half
    first = jnp.max(jnp.where(starts[None, :] <= run[:, None], starts[None, :], 0), axis=1) // 2
    last = run // 2
    low0 = (first - y + NY - 1) // NY
    high0 = jnp.minimum((last - y + NY) // NY, NZ)
    low1 = (nctx - 1 - y - last + NY - 1) // NY
    high1 = jnp.minimum((nctx - 1 - y - first + NY) // NY, NZ)
    count0 = jnp.maximum(high0 - low0, 0)
    count1 = jnp.maximum(high1 - low1, 0)
    table = jnp.stack([run, upper * NY + source, low0, count0, low1, count1], axis=1)
    own = jnp.stack([y, c]).astype(jnp.int32)
    return jnp.concatenate([table.reshape(-1).astype(jnp.int32), own])


class Tile:
    def __init__(self, info, mine_ref, other_ref, heads):
        self.info, self.mine, self.other = info, mine_ref, other_ref
        self.half = mine_ref.shape[1] // 2
        self.width = mine_ref.shape[2] // 2
        self.cols = heads * self.half
        self.keys = 2 * self.half
        self.runs = 2 * NZ * NY * NC
        self.y = info[2 * NY * FIELDS]
        self.c = info[2 * NY * FIELDS + 1]
        row = lax.broadcasted_iota(jnp.int32, (self.keys, 1), 0)
        self.row_core = jnp.where(row < self.half, self.c, 1 - self.c)
        self.row_rest = row % self.half
        self.col_rest = lax.broadcasted_iota(jnp.int32, (1, self.cols), 1) % self.half

    def field(self, j, n):
        return self.info[j * FIELDS + n]

    def count(self, j):
        return self.field(j, 3) + self.field(j, 5)

    def place(self, j, i):
        lower = self.field(j, 3)
        part = (i >= lower).astype(jnp.int32)
        z = jnp.where(part == 1, self.field(j, 4) + i - lower, self.field(j, 2) + i)
        return z, part

    def rows(self, part):
        return pl.ds(pl.multiple_of(part * self.half, self.half), self.half)

    def block(self, place, second):
        z, part = place
        lanes = slice(self.width * second, self.width * (second + 1))
        return jnp.concatenate(
            [self.mine[z, self.rows(part), lanes], self.other[z, self.rows(part), lanes]], axis=0
        )

    def allowed(self, j, place):
        z, part = place
        run = (z * NY + self.y) * NC + self.row_core
        run = jnp.where(part == 1, self.runs - 1 - run, run)
        return run * self.half + self.row_rest <= self.field(j, 0) * self.half + self.col_rest


def stack_heads(refs, out_ref, lane0, half, width, heads):
    for k, ref in enumerate(refs):
        for side in (0, 1):
            for h in range(heads):
                out_ref[2 * k + side, h * half : (h + 1) * half, :] = ref[
                    0, side * half : (side + 1) * half, lane0 + h * width : lane0 + (h + 1) * width
                ]


def forward_kernel(heads, info, a0, a1, a2, a3, mine, other, u_ref, stats_ref, q_scr, do_scr, s_scr, st_scr):
    tile = Tile(info, mine, other, heads)
    half, width, cols = tile.half, tile.width, tile.cols
    log2_scale = math.log2(math.e) / math.sqrt(width)
    stack_heads((a0, a1, a2, a3), q_scr, 0, half, width, heads)
    stack_heads((a0, a1, a2, a3), do_scr, heads * width, half, width, heads)

    def one_run(j, _):
        q2 = q_scr[j]
        count = tile.count(j)

        def scores(i, biggest):
            place = tile.place(j, i)
            s = dot(tile.block(place, 0), q2, 1, 1)
            s = jnp.where(tile.allowed(j, place), s, FLOOR)
            s_scr[i] = s
            return jnp.maximum(biggest, jnp.max(s.reshape(tile.keys // 8, 8, cols), axis=0))

        biggest = lax.fori_loop(0, count, scores, jnp.full((8, cols), FLOOR, jnp.float32))
        top = jnp.max(biggest, axis=0, keepdims=True)

        def sums(i, carry):
            total, acc = carry
            e = jnp.exp2((s_scr[i] - top) * log2_scale)
            total = total + jnp.sum(e.reshape(tile.keys // 8, 8, cols), axis=0)
            values = tile.block(tile.place(j, i), 1)
            return total, acc + dot(values, e.astype(jnp.bfloat16), 0, 0)

        total, acc = lax.fori_loop(
            0, count, sums, (jnp.zeros((8, cols), jnp.float32), jnp.zeros((width, cols), jnp.float32))
        )
        u_ref[j] = acc
        row = pl.ds(tile.field(j, 1), 1)
        st_scr[0, row, :] = top
        st_scr[1, row, :] = jnp.sum(total, axis=0, keepdims=True)
        st_scr[2, row, :] = jnp.sum(acc * do_scr[j].astype(jnp.float32).T, axis=0, keepdims=True)
        return 0

    lax.fori_loop(0, 2 * NY, one_run, 0)
    for k in range(NY):
        stats_ref[k] = st_scr[...]


def backward_kernel(
    heads, info, a0, a1, a2, a3, mine, other, u_ref, stats,
    o0, o1, o2, o3, dmine, dother, q_scr, do_scr, dacc, att_scr, dq_scr, st_scr,
):
    tile = Tile(info, mine, other, heads)
    half, width, cols = tile.half, tile.width, tile.cols
    scale = 1.0 / math.sqrt(width)
    log2_scale = scale * math.log2(math.e)
    stack_heads((a0, a1, a2, a3), q_scr, 0, half, width, heads)
    stack_heads((a0, a1, a2, a3), do_scr, heads * width, half, width, heads)
    dmine[...] = jnp.zeros_like(dmine)
    dacc[...] = jnp.zeros_like(dacc)

    tops = [stats[k, 0] for k in range(NY)]
    top = functools.reduce(jnp.maximum, tops)
    weights = [jnp.exp2((t - top) * log2_scale) for t in tops]
    den = sum(w * stats[k, 1] for k, w in enumerate(weights))
    inverse = 1.0 / den
    st_scr[0] = top * log2_scale + jnp.log2(den)
    st_scr[1] = sum(w * stats[k, 2] for k, w in enumerate(weights)) * inverse
    st_scr[2] = jnp.exp2((stats[tile.y, 0] - top) * log2_scale) * inverse

    def one_run(j, _):
        q2 = q_scr[j]
        do2 = do_scr[j]
        row = pl.ds(tile.field(j, 1), 1)
        lse2 = st_scr[0, row, :]
        delta = st_scr[1, row, :]
        att_scr[j] = (u_ref[j] * st_scr[2, row, :]).T.astype(jnp.bfloat16)

        def visit(i, dq_t):
            place = tile.place(j, i)
            keys = tile.block(place, 0)
            s = dot(keys, q2, 1, 1)
            s = jnp.where(tile.allowed(j, place), s, FLOOR)
            p = jnp.exp2(s * log2_scale - lse2)
            dp = dot(tile.block(place, 1), do2, 1, 1)
            ds = (p * (dp - delta)).astype(jnp.bfloat16)
            dk = dot(ds, q2, 1, 0)
            dv = dot(p.astype(jnp.bfloat16), do2, 1, 0)
            z, part = place
            rows = tile.rows(part)
            dmine[z, rows, :width] += dk[:half]
            dmine[z, rows, width:] += dv[:half]
            dacc[z, rows, :width] += dk[half:]
            dacc[z, rows, width:] += dv[half:]
            return dq_t + dot(keys, ds, 0, 0)

        dq_t = lax.fori_loop(0, tile.count(j), visit, jnp.zeros((width, cols), jnp.float32))
        dq_scr[j] = (dq_t * scale).T.astype(jnp.bfloat16)
        return 0

    lax.fori_loop(0, 2 * NY, one_run, 0)
    dmine[:, :, :width] = dmine[:, :, :width] * scale
    dother[:, :, :width] = (dacc[:, :, :width] * scale).astype(dother.dtype)
    dother[:, :, width:] = dacc[:, :, width:].astype(dother.dtype)
    for k, out in enumerate((o0, o1, o2, o3)):
        for side in (0, 1):
            for h in range(heads):
                where = slice(side * half, (side + 1) * half)
                part = slice(h * half, (h + 1) * half)
                lanes = slice(h * width, (h + 1) * width)
                out[0, where, lanes] = att_scr[2 * k + side, part, :]
                lanes = slice((heads + h) * width, (heads + h + 1) * width)
                out[0, where, lanes] = dq_scr[2 * k + side, part, :]


def combine_kernel(o0, o1, o2, o3, dkv, att_ref, dq_ref, dkv_ref, sq_ref):
    wide = att_ref.shape[2]
    parts = [o[0].astype(jnp.float32) for o in (o0, o1, o2, o3)]
    both = (parts[0] + parts[1]) + (parts[2] + parts[3])
    att_ref[0] = both[:, :wide].astype(att_ref.dtype)
    dq = both[:, wide:]
    dq_ref[0] = dq
    total = functools.reduce(jnp.add, [dkv[k].astype(jnp.float32) for k in range(NZ)])
    dkv_ref[0] = total
    squares = jnp.sum(dq * dq) + jnp.sum(total * total)
    sq_ref[...] = jnp.full(sq_ref.shape, squares, jnp.float32)


def scale_kernel(count, sums, dq, dkv, oq, ok, ov):
    lanes = sums.shape[2]
    total = sums[0]
    for k in range(1, sums.shape[0]):
        total = total + sums[k]
    factor = lax.rsqrt(total / count + 1e-06)
    for h in range(dq.shape[2] // lanes):
        at = slice(h * lanes, (h + 1) * lanes)
        oq[0, :, at] = (dq[0, :, at] * factor).astype(oq.dtype)
    width = ok.shape[2]
    ok[0] = (dkv[0, :, :width] * factor).astype(ok.dtype)
    ov[0] = (dkv[0, :, width:] * factor).astype(ov.dtype)


def turn(x, axis, size, by):
    return lax.ppermute(x, axis, [(i, (i + by) % size) for i in range(size)])


def per_device(queries, keys, values, grad_out, doc_starts):
    tok = queries.shape[1]
    wide = queries.shape[2]
    width = keys.shape[2]
    heads = wide // width
    half = tok // 2
    cols = heads * half
    z, y, c = (lax.axis_index(a) for a in ("z", "y", "core"))
    info = visits(doc_starts[0], tok, z, y, c)

    asked = jnp.concatenate([queries, grad_out], axis=2)
    around = [asked] + [turn(asked, "y", NY, -k) for k in range(1, NY)]
    kv = jnp.concatenate([keys, values], axis=2)
    mine = lax.all_to_all(jnp.broadcast_to(kv, (NZ, tok, 2 * width)), "z", 0, 0, tiled=True)
    other = turn(mine, "core", NC, 1)

    f32, bf16 = jnp.float32, jnp.bfloat16
    shape = jax.ShapeDtypeStruct
    u, stats = pl.pallas_call(
        functools.partial(forward_kernel, heads),
        out_shape=(shape((2 * NY, width, cols), f32), shape((NY, 3, 2 * NY, cols), f32)),
        in_specs=[SMEM] + [VMEM] * 6,
        out_specs=(VMEM, VMEM),
        scratch_shapes=[
            pltpu.VMEM((2 * NY, cols, width), bf16),
            pltpu.VMEM((2 * NY, cols, width), bf16),
            pltpu.VMEM((2 * NZ, tok, cols), f32),
            pltpu.VMEM((3, 2 * NY, cols), f32),
        ],
        compiler_params=PARAMS,
    )(info, *around, mine, other)
    stats = lax.all_to_all(stats, "y", 0, 0, tiled=True)
    *sent, dmine, dother = pl.pallas_call(
        functools.partial(backward_kernel, heads),
        out_shape=[shape(asked.shape, bf16)] * NY
        + [shape(mine.shape, f32), shape(mine.shape, bf16)],
        in_specs=[SMEM] + [VMEM] * 8,
        out_specs=[VMEM] * (NY + 2),
        scratch_shapes=[
            pltpu.VMEM((2 * NY, cols, width), bf16),
            pltpu.VMEM((2 * NY, cols, width), bf16),
            pltpu.VMEM(mine.shape, f32),
            pltpu.VMEM((2 * NY, cols, width), bf16),
            pltpu.VMEM((2 * NY, cols, width), bf16),
            pltpu.VMEM((3, 2 * NY, cols), f32),
        ],
        compiler_params=PARAMS,
    )(info, *around, mine, other, u, stats)
    back = [sent[0]] + [turn(sent[k], "y", NY, k) for k in range(1, NY)]
    from_core = turn(dother, "core", NC, 1)
    pair = (dmine + from_core.astype(f32)).astype(bf16)
    pieces = lax.all_to_all(pair, "z", 0, 0, tiled=True)
    attended, dq, dkv, squares = pl.pallas_call(
        combine_kernel,
        out_shape=(
            shape(queries.shape, bf16),
            shape(queries.shape, f32),
            shape(kv.shape, f32),
            shape((NZ * NY, 1, 128), f32),
        ),
        in_specs=[VMEM] * 5,
        out_specs=(VMEM,) * 4,
        compiler_params=PARAMS,
    )(*back, pieces)
    squares = lax.all_to_all(squares, ("z", "y"), 0, 0, tiled=True)
    ndata = lax.axis_size("dp")
    squares = jnp.broadcast_to(jnp.sum(squares, axis=0, keepdims=True), (NC * ndata, 1, 128))
    squares = lax.all_to_all(squares, ("core", "dp"), 0, 0, tiled=True)
    count = float(ndata * NZ * NY * NC * tok * (wide + 2 * width))
    out_query, out_key, out_value = pl.pallas_call(
        functools.partial(scale_kernel, count),
        out_shape=(shape(queries.shape, bf16), shape(keys.shape, bf16), shape(values.shape, bf16)),
        in_specs=[VMEM] * 3,
        out_specs=(VMEM,) * 3,
        compiler_params=PARAMS,
    )(squares, dq, dkv)
    return attended, out_query, out_key, out_value


def solution(mesh):
    ndata = mesh.shape["dp"]
    fine = Mesh(mesh.devices.reshape(NZ, NY, NC, ndata), ("z", "y", "core", "dp"))
    spec = P("dp", ("z", "y", "core"), None)
    return jax.shard_map(
        per_device,
        mesh=fine,
        in_specs=(spec, spec, spec, spec, P("dp", None)),
        out_specs=(spec, spec, spec, spec),
        check_vma=False,
    )
```

```python
import functools
import math

import jax
import jax.numpy as jnp
from jax import lax
from jax.experimental import pallas as pl
from jax.experimental.pallas import tpu as pltpu
from jax.sharding import Mesh
from jax.sharding import PartitionSpec as P

FLOOR = -1e30
NZ, NY, NC = 8, 4, 2
FIELDS = 6
VMEM = pl.BlockSpec(memory_space=pltpu.VMEM)
SMEM = pl.BlockSpec(memory_space=pltpu.SMEM)
PARAMS = pltpu.CompilerParams(vmem_limit_bytes=40 * 1024 * 1024)


def dot(a, b, ca, cb):
    return lax.dot_general(a, b, (((ca,), (cb,)), ((), ())), preferred_element_type=jnp.float32)


def visits(doc_starts, tok, z, y, c):
    nctx = NZ * NY * NC
    half = tok // 2
    source = jnp.repeat((y + jnp.arange(NY, dtype=jnp.int32)) % NY, 2)
    upper = jnp.tile(jnp.arange(2, dtype=jnp.int32), NY)
    base = (z * NY + source) * NC + c
    run = jnp.where(upper == 1, 2 * nctx - 1 - base, base)
    starts = doc_starts // half
    first = jnp.max(jnp.where(starts[None, :] <= run[:, None], starts[None, :], 0), axis=1) // 2
    last = run // 2
    low0 = (first - y + NY - 1) // NY
    high0 = jnp.minimum((last - y + NY) // NY, NZ)
    low1 = (nctx - 1 - y - last + NY - 1) // NY
    high1 = jnp.minimum((nctx - 1 - y - first + NY) // NY, NZ)
    count0 = jnp.maximum(high0 - low0, 0)
    count1 = jnp.maximum(high1 - low1, 0)
    table = jnp.stack([run, upper * NY + source, low0, count0, low1, count1], axis=1)
    own = jnp.stack([y, c]).astype(jnp.int32)
    return jnp.concatenate([table.reshape(-1).astype(jnp.int32), own])


class Tile:
    def __init__(self, info, pairs_ref, heads):
        self.info, self.pairs = info, pairs_ref
        self.keys = pairs_ref.shape[1]
        self.half = self.keys // 2
        self.width = pairs_ref.shape[2] // 2
        self.cols = heads * self.half
        self.runs = 2 * NZ * NY * NC
        self.y = info[2 * NY * FIELDS]
        self.c = info[2 * NY * FIELDS + 1]
        row = lax.broadcasted_iota(jnp.int32, (self.keys, 1), 0)
        core = jnp.where(row < self.half, self.c, 1 - self.c)
        rest = row % self.half
        self.row_low = core * self.half + rest
        self.row_high = (self.runs - 1 - core) * self.half + rest
        self.col_rest = lax.broadcasted_iota(jnp.int32, (1, self.cols), 1) % self.half

    def field(self, j, n):
        return self.info[j * FIELDS + n]

    def count(self, j):
        return self.field(j, 3) + self.field(j, 5)

    def steps(self, j):
        return (self.count(j) + 1) // 2

    def blocks(self, j, i):
        def place(n):
            lower = self.field(j, 3)
            return jnp.where(n >= lower, self.field(j, 4) + NZ + n - lower, self.field(j, 2) + n)

        second = jnp.minimum(2 * i + 1, self.count(j) - 1)
        return place(2 * i), place(second)

    def allowed(self, j, i, blocks):
        parts = []
        for n, b in enumerate(blocks):
            step = NY * NC * self.half
            low = b * step + self.y * NC * self.half + self.row_low
            high = self.row_high - (b - NZ) * step - self.y * NC * self.half
            at = jnp.where(b >= NZ, high, low)
            if n:
                at = jnp.where(2 * i + 1 < self.count(j), at, jnp.int32(2**30))
            parts.append(at)
        return jnp.concatenate(parts, axis=0) <= self.field(j, 0) * self.half + self.col_rest


def two(ref, blocks, lanes, axis):
    return jnp.concatenate([ref[b, :, lanes] for b in blocks], axis=axis)


def gather_kernel(mine, other, pairs, turned):
    half = mine.shape[1] // 2
    width = mine.shape[2] // 2
    for b in range(2 * NZ):
        rows = slice((b // NZ) * half, (b // NZ + 1) * half)
        block = jnp.concatenate([mine[b % NZ, rows], other[b % NZ, rows]], axis=0)
        pairs[b] = block
        turned[b] = block.astype(jnp.float32).T.astype(turned.dtype)


def stack_heads(refs, out_ref, lane0, half, width, heads):
    for k, ref in enumerate(refs):
        for side in (0, 1):
            for h in range(heads):
                out_ref[2 * k + side, h * half : (h + 1) * half, :] = ref[
                    0, side * half : (side + 1) * half, lane0 + h * width : lane0 + (h + 1) * width
                ]


def forward_kernel(heads, info, a0, a1, a2, a3, pairs, turned, u_ref, stats_ref, q_scr, do_scr, s_scr, st_scr):
    tile = Tile(info, pairs, heads)
    half, width, cols = tile.half, tile.width, tile.cols
    log2_scale = math.log2(math.e) / math.sqrt(width)
    stack_heads((a0, a1, a2, a3), q_scr, 0, half, width, heads)
    stack_heads((a0, a1, a2, a3), do_scr, heads * width, half, width, heads)
    groups = 2 * tile.keys // 8

    def one_run(j, _):
        q2 = q_scr[j]
        steps = tile.steps(j)

        def scores(i, biggest):
            blocks = tile.blocks(j, i)
            s = dot(two(pairs, blocks, slice(0, width), 0), q2, 1, 1)
            s = jnp.where(tile.allowed(j, i, blocks), s, FLOOR)
            s_scr[i] = s
            return jnp.maximum(biggest, jnp.max(s.reshape(groups, 8, cols), axis=0))

        biggest = lax.fori_loop(0, steps, scores, jnp.full((8, cols), FLOOR, jnp.float32))
        top = jnp.max(biggest, axis=0, keepdims=True)

        def sums(i, carry):
            total, acc = carry
            e = jnp.exp2((s_scr[i] - top) * log2_scale)
            total = total + jnp.sum(e.reshape(groups, 8, cols), axis=0)
            values_t = jnp.concatenate([turned[b, width:, :] for b in tile.blocks(j, i)], axis=1)
            return total, acc + dot(values_t, e.astype(jnp.bfloat16), 1, 0)

        total, acc = lax.fori_loop(
            0, steps, sums, (jnp.zeros((8, cols), jnp.float32), jnp.zeros((width, cols), jnp.float32))
        )
        u_ref[j] = acc
        row = pl.ds(tile.field(j, 1), 1)
        st_scr[0, row, :] = top
        st_scr[1, row, :] = jnp.sum(total, axis=0, keepdims=True)
        st_scr[2, row, :] = jnp.sum(acc * do_scr[j].astype(jnp.float32).T, axis=0, keepdims=True)
        return 0

    lax.fori_loop(0, 2 * NY, one_run, 0)
    for k in range(NY):
        stats_ref[k] = st_scr[...]


def backward_kernel(
    heads, info, a0, a1, a2, a3, pairs, turned, u_ref, stats,
    o0, o1, o2, o3, dmine, dother, q_scr, do_scr, dacc, att_scr, dq_scr, st_scr,
):
    tile = Tile(info, pairs, heads)
    half, width, cols, keys = tile.half, tile.width, tile.cols, tile.keys
    scale = 1.0 / math.sqrt(width)
    log2_scale = scale * math.log2(math.e)
    stack_heads((a0, a1, a2, a3), q_scr, 0, half, width, heads)
    stack_heads((a0, a1, a2, a3), do_scr, heads * width, half, width, heads)
    dacc[...] = jnp.zeros_like(dacc)

    tops = [stats[k, 0] for k in range(NY)]
    top = functools.reduce(jnp.maximum, tops)
    weights = [jnp.exp2((t - top) * log2_scale) for t in tops]
    den = sum(w * stats[k, 1] for k, w in enumerate(weights))
    inverse = 1.0 / den
    st_scr[0] = top * log2_scale + jnp.log2(den)
    st_scr[1] = sum(w * stats[k, 2] for k, w in enumerate(weights)) * inverse
    st_scr[2] = jnp.exp2((stats[tile.y, 0] - top) * log2_scale) * inverse

    def one_run(j, _):
        q2 = q_scr[j]
        do2 = do_scr[j]
        row = pl.ds(tile.field(j, 1), 1)
        lse2 = st_scr[0, row, :]
        delta = st_scr[1, row, :]
        att_scr[j] = (u_ref[j] * st_scr[2, row, :]).T.astype(jnp.bfloat16)

        def visit(i, dq_t):
            blocks = tile.blocks(j, i)
            s = dot(two(pairs, blocks, slice(0, width), 0), q2, 1, 1)
            s = jnp.where(tile.allowed(j, i, blocks), s, FLOOR)
            p = jnp.exp2(s * log2_scale - lse2)
            dp = dot(two(pairs, blocks, slice(width, 2 * width), 0), do2, 1, 1)
            ds = (p * (dp - delta)).astype(jnp.bfloat16)
            dk = dot(ds, q2, 1, 0)
            dv = dot(p.astype(jnp.bfloat16), do2, 1, 0)
            for n, b in enumerate(blocks):
                dacc[b, :, :width] += dk[n * keys : (n + 1) * keys]
                dacc[b, :, width:] += dv[n * keys : (n + 1) * keys]
            keys_t = jnp.concatenate([turned[b, :width, :] for b in blocks], axis=1)
            return dq_t + dot(keys_t, ds, 1, 0)

        dq_t = lax.fori_loop(0, tile.steps(j), visit, jnp.zeros((width, cols), jnp.float32))
        dq_scr[j] = (dq_t * scale).T.astype(jnp.bfloat16)
        return 0

    lax.fori_loop(0, 2 * NY, one_run, 0)
    for b in range(2 * NZ):
        rows = slice((b // NZ) * half, (b // NZ + 1) * half)
        for out, part in ((dmine, slice(0, half)), (dother, slice(half, keys))):
            out[b % NZ, rows, :width] = (dacc[b, part, :width] * scale).astype(out.dtype)
            out[b % NZ, rows, width:] = dacc[b, part, width:].astype(out.dtype)
    for k, out in enumerate((o0, o1, o2, o3)):
        for side in (0, 1):
            for h in range(heads):
                where = slice(side * half, (side + 1) * half)
                part = slice(h * half, (h + 1) * half)
                lanes = slice(h * width, (h + 1) * width)
                out[0, where, lanes] = att_scr[2 * k + side, part, :]
                lanes = slice((heads + h) * width, (heads + h + 1) * width)
                out[0, where, lanes] = dq_scr[2 * k + side, part, :]


def combine_kernel(o0, o1, o2, o3, dkv, att_ref, dq_ref, dkv_ref, sq_ref):
    wide = att_ref.shape[2]
    parts = [o[0].astype(jnp.float32) for o in (o0, o1, o2, o3)]
    both = (parts[0] + parts[1]) + (parts[2] + parts[3])
    att_ref[0] = both[:, :wide].astype(att_ref.dtype)
    dq = both[:, wide:]
    dq_ref[0] = dq
    total = functools.reduce(jnp.add, [dkv[k].astype(jnp.float32) for k in range(NZ)])
    dkv_ref[0] = total
    squares = jnp.sum(dq * dq) + jnp.sum(total * total)
    sq_ref[...] = jnp.full(sq_ref.shape, squares, jnp.float32)


def scale_kernel(count, sums, dq, dkv, oq, ok, ov):
    lanes = sums.shape[2]
    total = sums[0]
    for k in range(1, sums.shape[0]):
        total = total + sums[k]
    factor = lax.rsqrt(total / count + 1e-06)
    for h in range(dq.shape[2] // lanes):
        at = slice(h * lanes, (h + 1) * lanes)
        oq[0, :, at] = (dq[0, :, at] * factor).astype(oq.dtype)
    width = ok.shape[2]
    ok[0] = (dkv[0, :, :width] * factor).astype(ok.dtype)
    ov[0] = (dkv[0, :, width:] * factor).astype(ov.dtype)


def spread_kernel(keys, values, copies):
    width = keys.shape[2]
    for k in range(copies.shape[0]):
        copies[k, :, :width] = keys[0]
        copies[k, :, width:] = values[0]


def join_kernel(left, right, *outs):
    wide = left.shape[2]
    for out in outs:
        out[:, :, :wide] = left[...]
        out[:, :, wide:] = right[...]


def turn(x, axis, size, by):
    return lax.ppermute(x, axis, [(i, (i + by) % size) for i in range(size)])


def per_device(queries, keys, values, grad_out, doc_starts):
    tok = queries.shape[1]
    wide = queries.shape[2]
    width = keys.shape[2]
    heads = wide // width
    half = tok // 2
    cols = heads * half
    z, y, c = (lax.axis_index(a) for a in ("z", "y", "core"))
    info = visits(doc_starts[0], tok, z, y, c)

    copies = pl.pallas_call(spread_kernel, out_shape=jax.ShapeDtypeStruct((NZ, tok, 2 * width), keys.dtype), in_specs=[VMEM] * 2, out_specs=VMEM, compiler_params=PARAMS)(keys, values)
    mine = lax.all_to_all(copies, "z", 0, 0, tiled=True)
    asked, *ask = pl.pallas_call(join_kernel, out_shape=[jax.ShapeDtypeStruct((1, tok, 2 * wide), keys.dtype)] * NY, in_specs=[VMEM] * 2, out_specs=[VMEM] * NY, compiler_params=PARAMS)(queries, grad_out)
    mine = lax.all_to_all(copies, "z", 0, 0, tiled=True)
    around = [asked] + [turn(ask[k - 1], "y", NY, -k) for k in range(1, NY)]
    other = turn(mine, "core", NC, 1)

    f32, bf16 = jnp.float32, jnp.bfloat16
    shape = jax.ShapeDtypeStruct
    pairs, turned = pl.pallas_call(
        gather_kernel,
        out_shape=(shape((2 * NZ, tok, 2 * width), bf16), shape((2 * NZ, 2 * width, tok), bf16)),
        in_specs=[VMEM] * 2,
        out_specs=(VMEM,) * 2,
        compiler_params=PARAMS,
    )(mine, other)
    u, stats = pl.pallas_call(
        functools.partial(forward_kernel, heads),
        out_shape=(shape((2 * NY, width, cols), f32), shape((NY, 3, 2 * NY, cols), f32)),
        in_specs=[SMEM] + [VMEM] * 6,
        out_specs=(VMEM, VMEM),
        scratch_shapes=[
            pltpu.VMEM((2 * NY, cols, width), bf16),
            pltpu.VMEM((2 * NY, cols, width), bf16),
            pltpu.VMEM((NZ, 2 * tok, cols), f32),
            pltpu.VMEM((3, 2 * NY, cols), f32),
        ],
        compiler_params=PARAMS,
    )(info, *around, pairs, turned)
    stats = lax.all_to_all(stats, "y", 0, 0, tiled=True)
    *sent, dmine, dother = pl.pallas_call(
        functools.partial(backward_kernel, heads),
        out_shape=[shape(asked.shape, bf16)] * NY
        + [shape(mine.shape, f32), shape(mine.shape, bf16)],
        in_specs=[SMEM] + [VMEM] * 8,
        out_specs=[VMEM] * (NY + 2),
        scratch_shapes=[
            pltpu.VMEM((2 * NY, cols, width), bf16),
            pltpu.VMEM((2 * NY, cols, width), bf16),
            pltpu.VMEM((2 * NZ, tok, 2 * width), f32),
            pltpu.VMEM((2 * NY, cols, width), bf16),
            pltpu.VMEM((2 * NY, cols, width), bf16),
            pltpu.VMEM((3, 2 * NY, cols), f32),
        ],
        compiler_params=PARAMS,
    )(info, *around, pairs, turned, u, stats)
    back = [sent[0]] + [turn(sent[k], "y", NY, k) for k in range(1, NY)]
    from_core = turn(dother, "core", NC, 1)
    pair = (dmine + from_core.astype(f32)).astype(bf16)
    pieces = lax.all_to_all(pair, "z", 0, 0, tiled=True)
    attended, dq, dkv, squares = pl.pallas_call(
        combine_kernel,
        out_shape=(
            shape(queries.shape, bf16),
            shape(queries.shape, f32),
            shape((1, tok, 2 * width), f32),
            shape((NZ * NY, 1, 128), f32),
        ),
        in_specs=[VMEM] * 5,
        out_specs=(VMEM,) * 4,
        compiler_params=PARAMS,
    )(*back, pieces)
    squares = lax.all_to_all(squares, ("z", "y"), 0, 0, tiled=True)
    ndata = lax.axis_size("dp")
    squares = jnp.broadcast_to(jnp.sum(squares, axis=0, keepdims=True), (NC * ndata, 1, 128))
    squares = lax.all_to_all(squares, ("core", "dp"), 0, 0, tiled=True)
    count = float(ndata * NZ * NY * NC * tok * (wide + 2 * width))
    out_query, out_key, out_value = pl.pallas_call(
        functools.partial(scale_kernel, count),
        out_shape=(shape(queries.shape, bf16), shape(keys.shape, bf16), shape(values.shape, bf16)),
        in_specs=[VMEM] * 3,
        out_specs=(VMEM,) * 3,
        compiler_params=PARAMS,
    )(squares, dq, dkv)
    return attended, out_query, out_key, out_value


def solution(mesh):
    ndata = mesh.shape["dp"]
    fine = Mesh(mesh.devices.reshape(NZ, NY, NC, ndata), ("z", "y", "core", "dp"))
    spec = P("dp", ("z", "y", "core"), None)
    return jax.shard_map(
        per_device,
        mesh=fine,
        in_specs=(spec, spec, spec, spec, P("dp", None)),
        out_specs=(spec, spec, spec, spec),
        check_vma=False,
    )
```

```python
import functools
import math

import jax
import jax.numpy as jnp
from jax import lax
from jax.experimental import pallas as pl
from jax.experimental.pallas import tpu as pltpu
from jax.sharding import Mesh
from jax.sharding import PartitionSpec as P

FLOOR = -1e30
NZ, NY, NC = 8, 4, 2
FIELDS = 6
VMEM = pl.BlockSpec(memory_space=pltpu.VMEM)
SMEM = pl.BlockSpec(memory_space=pltpu.SMEM)
PARAMS = pltpu.CompilerParams(vmem_limit_bytes=40 * 1024 * 1024)


def dot(a, b, ca, cb):
    return lax.dot_general(a, b, (((ca,), (cb,)), ((), ())), preferred_element_type=jnp.float32)


def visits(doc_starts, tok, z, y, c):
    nctx = NZ * NY * NC
    half = tok // 2
    source = jnp.repeat((y + jnp.arange(NY, dtype=jnp.int32)) % NY, 2)
    upper = jnp.tile(jnp.arange(2, dtype=jnp.int32), NY)
    base = (z * NY + source) * NC + c
    run = jnp.where(upper == 1, 2 * nctx - 1 - base, base)
    starts = doc_starts // half
    first = jnp.max(jnp.where(starts[None, :] <= run[:, None], starts[None, :], 0), axis=1) // 2
    last = run // 2
    low0 = (first - y + NY - 1) // NY
    high0 = jnp.minimum((last - y + NY) // NY, NZ)
    low1 = (nctx - 1 - y - last + NY - 1) // NY
    high1 = jnp.minimum((nctx - 1 - y - first + NY) // NY, NZ)
    count0 = jnp.maximum(high0 - low0, 0)
    count1 = jnp.maximum(high1 - low1, 0)
    table = jnp.stack([run, upper * NY + source, low0, count0, low1, count1], axis=1)
    own = jnp.stack([y, c]).astype(jnp.int32)
    return jnp.concatenate([table.reshape(-1).astype(jnp.int32), own])


class Tile:
    def __init__(self, info, pairs_ref, heads):
        self.info, self.pairs = info, pairs_ref
        self.keys = pairs_ref.shape[1]
        self.half = self.keys // 2
        self.width = pairs_ref.shape[2] // 2
        self.cols = heads * self.half
        self.runs = 2 * NZ * NY * NC
        self.y = info[2 * NY * FIELDS]
        self.c = info[2 * NY * FIELDS + 1]
        row = lax.broadcasted_iota(jnp.int32, (self.keys, 1), 0)
        core = jnp.where(row < self.half, self.c, 1 - self.c)
        rest = row % self.half
        self.row_low = core * self.half + rest
        self.row_high = (self.runs - 1 - core) * self.half + rest
        self.col_rest = lax.broadcasted_iota(jnp.int32, (1, self.cols), 1) % self.half

    def field(self, j, n):
        return self.info[j * FIELDS + n]

    def count(self, j):
        return self.field(j, 3) + self.field(j, 5)

    def steps(self, j):
        return (self.count(j) + 1) // 2

    def blocks(self, j, i):
        def place(n):
            lower = self.field(j, 3)
            return jnp.where(n >= lower, self.field(j, 4) + NZ + n - lower, self.field(j, 2) + n)

        second = jnp.minimum(2 * i + 1, self.count(j) - 1)
        return place(2 * i), place(second)

    def allowed(self, j, i, blocks):
        parts = []
        for n, b in enumerate(blocks):
            step = NY * NC * self.half
            low = b * step + self.y * NC * self.half + self.row_low
            high = self.row_high - (b - NZ) * step - self.y * NC * self.half
            at = jnp.where(b >= NZ, high, low)
            if n:
                at = jnp.where(2 * i + 1 < self.count(j), at, jnp.int32(2**30))
            parts.append(at)
        return jnp.concatenate(parts, axis=0) <= self.field(j, 0) * self.half + self.col_rest


def two(ref, blocks, lanes, axis):
    return jnp.concatenate([ref[b, :, lanes] for b in blocks], axis=axis)


def gather_kernel(mine, other, pairs, turned):
    half = mine.shape[1] // 2
    width = mine.shape[2] // 2
    for b in range(2 * NZ):
        rows = slice((b // NZ) * half, (b // NZ + 1) * half)
        block = jnp.concatenate([mine[b % NZ, rows], other[b % NZ, rows]], axis=0)
        pairs[b] = block
        turned[b] = block.astype(jnp.float32).T.astype(turned.dtype)


def heads_of(ref, side, second, half, width, heads):
    rows = pl.ds(pl.multiple_of(side * half, half), half)
    lanes = [(heads * second + h) * width for h in range(heads)]
    return jnp.concatenate([ref[0, rows, at : at + width] for at in lanes], axis=0)


def forward_kernel(heads, ks, before, info, *refs):
    asked, refs = refs[: len(ks)], refs[len(ks) :]
    pairs, turned = refs[:2]
    earlier = refs[2 : 2 + before]
    u_ref, stats_ref, s_scr, st_scr = refs[2 + before :]
    tile = Tile(info, pairs, heads)
    half, width, cols = tile.half, tile.width, tile.cols
    log2_scale = math.log2(math.e) / math.sqrt(width)
    groups = 2 * tile.keys // 8
    st_scr[...] = sum([e[...] for e in earlier], jnp.zeros(st_scr.shape, jnp.float32))

    def one_run(n, k, side):
        j = 2 * k + side
        q2 = heads_of(asked[n], side, 0, half, width, heads)
        steps = tile.steps(j)

        def scores(i, biggest):
            blocks = tile.blocks(j, i)
            s = dot(two(pairs, blocks, slice(0, width), 0), q2, 1, 1)
            s = jnp.where(tile.allowed(j, i, blocks), s, FLOOR)
            s_scr[i] = s
            return jnp.maximum(biggest, jnp.max(s.reshape(groups, 8, cols), axis=0))

        biggest = lax.fori_loop(0, steps, scores, jnp.full((8, cols), FLOOR, jnp.float32))
        top = jnp.max(biggest, axis=0, keepdims=True)

        def sums(i, carry):
            total, acc = carry
            e = jnp.exp2((s_scr[i] - top) * log2_scale)
            total = total + jnp.sum(e.reshape(groups, 8, cols), axis=0)
            values_t = jnp.concatenate([turned[b, width:, :] for b in tile.blocks(j, i)], axis=1)
            return total, acc + dot(values_t, e.astype(jnp.bfloat16), 1, 0)

        total, acc = lax.fori_loop(
            0, steps, sums, (jnp.zeros((8, cols), jnp.float32), jnp.zeros((width, cols), jnp.float32))
        )
        u_ref[2 * n + side] = acc
        row = pl.ds(tile.field(j, 1), 1)
        do_t = heads_of(asked[n], side, 1, half, width, heads).astype(jnp.float32).T
        st_scr[0, row, :] = top
        st_scr[1, row, :] = jnp.sum(total, axis=0, keepdims=True)
        st_scr[2, row, :] = jnp.sum(acc * do_t, axis=0, keepdims=True)

    for n, k in enumerate(ks):
        lax.fori_loop(0, 2, lambda side, _, n=n, k=k: (one_run(n, k, side), 0)[1], 0)
    if before:
        for k in range(NY):
            stats_ref[k] = st_scr[...]
    else:
        stats_ref[...] = st_scr[...]


def backward_kernel(heads, ks, info, *refs):
    asked, refs = refs[: len(ks)], refs[len(ks) :]
    us, refs = refs[: len(ks)], refs[len(ks) :]
    pairs, turned, stats = refs[:3]
    refs = refs[3:]
    *outs, dmine, dother, dacc, st_scr = refs
    tile = Tile(info, pairs, heads)
    half, width, cols, keys = tile.half, tile.width, tile.cols, tile.keys
    scale = 1.0 / math.sqrt(width)
    log2_scale = scale * math.log2(math.e)
    dacc[...] = jnp.zeros_like(dacc)

    tops = [stats[k, 0] for k in range(NY)]
    top = functools.reduce(jnp.maximum, tops)
    weights = [jnp.exp2((t - top) * log2_scale) for t in tops]
    den = sum(w * stats[k, 1] for k, w in enumerate(weights))
    inverse = 1.0 / den
    st_scr[0] = top * log2_scale + jnp.log2(den)
    st_scr[1] = sum(w * stats[k, 2] for k, w in enumerate(weights)) * inverse
    st_scr[2] = jnp.exp2((stats[tile.y, 0] - top) * log2_scale) * inverse

    def one_run(n, k, side):
        j = 2 * k + side
        q2 = heads_of(asked[n], side, 0, half, width, heads)
        do2 = heads_of(asked[n], side, 1, half, width, heads)
        row = pl.ds(tile.field(j, 1), 1)
        lse2 = st_scr[0, row, :]
        delta = st_scr[1, row, :]

        def visit(i, dq_t):
            blocks = tile.blocks(j, i)
            s = dot(two(pairs, blocks, slice(0, width), 0), q2, 1, 1)
            s = jnp.where(tile.allowed(j, i, blocks), s, FLOOR)
            p = jnp.exp2(s * log2_scale - lse2)
            dp = dot(two(pairs, blocks, slice(width, 2 * width), 0), do2, 1, 1)
            ds = (p * (dp - delta)).astype(jnp.bfloat16)
            dk = dot(ds, q2, 1, 0)
            dv = dot(p.astype(jnp.bfloat16), do2, 1, 0)
            for m, b in enumerate(blocks):
                dacc[b, :, :width] += dk[m * keys : (m + 1) * keys]
                dacc[b, :, width:] += dv[m * keys : (m + 1) * keys]
            keys_t = jnp.concatenate([turned[b, :width, :] for b in blocks], axis=1)
            return dq_t + dot(keys_t, ds, 1, 0)

        dq_t = lax.fori_loop(0, tile.steps(j), visit, jnp.zeros((width, cols), jnp.float32))
        att = (us[n][side] * st_scr[2, row, :]).T.astype(jnp.bfloat16)
        dq = (dq_t * scale).T.astype(jnp.bfloat16)
        rows = pl.ds(pl.multiple_of(side * half, half), half)
        for second, whole in ((0, att), (1, dq)):
            for h in range(heads):
                at = (heads * second + h) * width
                outs[n][0, rows, at : at + width] = whole[h * half : (h + 1) * half]

    for n, k in enumerate(ks):
        lax.fori_loop(0, 2, lambda side, _, n=n, k=k: (one_run(n, k, side), 0)[1], 0)
    for b in range(2 * NZ):
        rows = slice((b // NZ) * half, (b // NZ + 1) * half)
        for out, part in ((dmine, slice(0, half)), (dother, slice(half, keys))):
            out[b % NZ, rows, :width] = (dacc[b, part, :width] * scale).astype(out.dtype)
            out[b % NZ, rows, width:] = dacc[b, part, width:].astype(out.dtype)


def combine_kernel(o0, o1, o2, o3, dkv, att_ref, dq_ref, dkv_ref, sq_ref):
    wide = att_ref.shape[2]
    parts = [o[0].astype(jnp.float32) for o in (o0, o1, o2, o3)]
    both = (parts[0] + parts[1]) + (parts[2] + parts[3])
    att_ref[0] = both[:, :wide].astype(att_ref.dtype)
    dq = both[:, wide:]
    dq_ref[0] = dq
    total = functools.reduce(jnp.add, [dkv[k].astype(jnp.float32) for k in range(NZ)])
    dkv_ref[0] = total
    squares = jnp.sum(dq * dq) + jnp.sum(total * total)
    sq_ref[...] = jnp.full(sq_ref.shape, squares, jnp.float32)


def scale_kernel(count, sums, dq, dkv, oq, ok, ov):
    lanes = sums.shape[2]
    total = sums[0]
    for k in range(1, sums.shape[0]):
        total = total + sums[k]
    factor = lax.rsqrt(total / count + 1e-06)
    for h in range(dq.shape[2] // lanes):
        at = slice(h * lanes, (h + 1) * lanes)
        oq[0, :, at] = (dq[0, :, at] * factor).astype(oq.dtype)
    width = ok.shape[2]
    ok[0] = (dkv[0, :, :width] * factor).astype(ok.dtype)
    ov[0] = (dkv[0, :, width:] * factor).astype(ov.dtype)


def spread_kernel(keys, values, copies):
    width = keys.shape[2]
    for k in range(copies.shape[0]):
        copies[k, :, :width] = keys[0]
        copies[k, :, width:] = values[0]


def join_kernel(left, right, *outs):
    wide = left.shape[2]
    for out in outs:
        out[:, :, :wide] = left[...]
        out[:, :, wide:] = right[...]


def turn(x, axis, size, by):
    return lax.ppermute(x, axis, [(i, (i + by) % size) for i in range(size)])


def per_device(queries, keys, values, grad_out, doc_starts):
    tok = queries.shape[1]
    wide = queries.shape[2]
    width = keys.shape[2]
    heads = wide // width
    half = tok // 2
    cols = heads * half
    z, y, c = (lax.axis_index(a) for a in ("z", "y", "core"))
    info = visits(doc_starts[0], tok, z, y, c)

    copies = pl.pallas_call(spread_kernel, out_shape=jax.ShapeDtypeStruct((NZ, tok, 2 * width), keys.dtype), in_specs=[VMEM] * 2, out_specs=VMEM, compiler_params=PARAMS)(keys, values)
    mine = lax.all_to_all(copies, "z", 0, 0, tiled=True)
    asked, *ask = pl.pallas_call(join_kernel, out_shape=[jax.ShapeDtypeStruct((1, tok, 2 * wide), keys.dtype)] * NY, in_specs=[VMEM] * 2, out_specs=[VMEM] * NY, compiler_params=PARAMS)(queries, grad_out)
    mine = lax.all_to_all(copies, "z", 0, 0, tiled=True)
    around = {k: turn(ask[k - 1], "y", NY, -k) for k in (2, 1, 3)}
    around[0] = asked
    other = turn(mine, "core", NC, 1)

    f32, bf16 = jnp.float32, jnp.bfloat16
    shape = jax.ShapeDtypeStruct
    pairs, turned = pl.pallas_call(
        gather_kernel,
        out_shape=(shape((2 * NZ, tok, 2 * width), bf16), shape((2 * NZ, 2 * width, tok), bf16)),
        in_specs=[VMEM] * 2,
        out_specs=(VMEM,) * 2,
        compiler_params=PARAMS,
    )(mine, other)
    stat = (3, 2 * NY, cols)

    def forward(ks, earlier):
        return pl.pallas_call(
            functools.partial(forward_kernel, heads, ks, len(earlier)),
            out_shape=(
                shape((2 * len(ks), width, cols), f32),
                shape((NY,) + stat if earlier else stat, f32),
            ),
            in_specs=[SMEM] + [VMEM] * (len(ks) + 2 + len(earlier)),
            out_specs=(VMEM, VMEM),
            scratch_shapes=[pltpu.VMEM((NZ, 2 * tok, cols), f32), pltpu.VMEM(stat, f32)],
            compiler_params=PARAMS,
        )(info, *[around[k] for k in ks], pairs, turned, *earlier)

    u0, stats0 = forward((0,), [])
    u1, stats1 = forward((1,), [])
    u3, stats3 = forward((3,), [])
    u2, stats = forward((2,), [stats0, stats1, stats3])
    stats = lax.all_to_all(stats, "y", 0, 0, tiled=True)
    *sent, dmine, dother = pl.pallas_call(
        functools.partial(backward_kernel, heads, tuple(range(NY))),
        out_shape=[shape(asked.shape, bf16)] * NY
        + [shape(mine.shape, f32), shape(mine.shape, bf16)],
        in_specs=[SMEM] + [VMEM] * (2 * NY + 3),
        out_specs=[VMEM] * (NY + 2),
        scratch_shapes=[pltpu.VMEM((2 * NZ, tok, 2 * width), f32), pltpu.VMEM(stat, f32)],
        compiler_params=PARAMS,
    )(info, *[around[k] for k in range(NY)], u0, u1, u2, u3, pairs, turned, stats)
    back = [sent[0]] + [turn(sent[k], "y", NY, k) for k in range(1, NY)]
    from_core = turn(dother, "core", NC, 1)
    pair = (dmine + from_core.astype(f32)).astype(bf16)
    pieces = lax.all_to_all(pair, "z", 0, 0, tiled=True)
    attended, dq, dkv, squares = pl.pallas_call(
        combine_kernel,
        out_shape=(
            shape(queries.shape, bf16),
            shape(queries.shape, f32),
            shape((1, tok, 2 * width), f32),
            shape((NZ * NC, 1, 128), f32),
        ),
        in_specs=[VMEM] * 5,
        out_specs=(VMEM,) * 4,
        compiler_params=PARAMS,
    )(*back, pieces)
    squares = lax.all_to_all(squares, ("z", "core"), 0, 0, tiled=True)
    ndata = lax.axis_size("dp")
    squares = jnp.broadcast_to(jnp.sum(squares, axis=0, keepdims=True), (NY * ndata, 1, 128))
    squares = lax.all_to_all(squares, ("y", "dp"), 0, 0, tiled=True)
    count = float(ndata * NZ * NY * NC * tok * (wide + 2 * width))
    out_query, out_key, out_value = pl.pallas_call(
        functools.partial(scale_kernel, count),
        out_shape=(shape(queries.shape, bf16), shape(keys.shape, bf16), shape(values.shape, bf16)),
        in_specs=[VMEM] * 3,
        out_specs=(VMEM,) * 3,
        compiler_params=PARAMS,
    )(squares, dq, dkv)
    return attended, out_query, out_key, out_value


def solution(mesh):
    ndata = mesh.shape["dp"]
    fine = Mesh(mesh.devices.reshape(NZ, NY, NC, ndata), ("z", "y", "core", "dp"))
    spec = P("dp", ("z", "y", "core"), None)
    return jax.shard_map(
        per_device,
        mesh=fine,
        in_specs=(spec, spec, spec, spec, P("dp", None)),
        out_specs=(spec, spec, spec, spec),
        check_vma=False,
    )
```

```python
import functools
import math

import jax
import jax.numpy as jnp
from jax import lax
from jax.experimental import pallas as pl
from jax.experimental.pallas import tpu as pltpu
from jax.sharding import Mesh
from jax.sharding import PartitionSpec as P

FLOOR = -1e30
NZ, NY, NC = 8, 4, 2
FIELDS = 4
VMEM = pl.BlockSpec(memory_space=pltpu.VMEM)
SMEM = pl.BlockSpec(memory_space=pltpu.SMEM)
PARAMS = pltpu.CompilerParams(vmem_limit_bytes=40 * 1024 * 1024)


def dot(a, b, ca, cb):
    return lax.dot_general(a, b, (((ca,), (cb,)), ((), ())), preferred_element_type=jnp.float32)


FIELDS = 4
VMEM = pl.BlockSpec(memory_space=pltpu.VMEM)
SMEM = pl.BlockSpec(memory_space=pltpu.SMEM)
PARAMS = pltpu.CompilerParams(vmem_limit_bytes=40 * 1024 * 1024)


def dot(a, b, ca, cb):
    return lax.dot_general(a, b, (((ca,), (cb,)), ((), ())), preferred_element_type=jnp.float32)


def visits(doc_starts, tok, z, y, c):
    nctx = NZ * NY * NC
    half = tok // 2
    source = jnp.tile((y + jnp.arange(NY, dtype=jnp.int32)) % NY, 2)
    upper = jnp.repeat(jnp.arange(2, dtype=jnp.int32), NY)
    base = (z * NY + source) * NC + c
    run = jnp.where(upper == 1, 2 * nctx - 1 - base, base)
    starts = doc_starts // half
    begin = jnp.max(jnp.where(starts[None, :] <= run[:, None], starts[None, :], 0), axis=1)
    first = jnp.min(begin.reshape(2, NY), axis=1) // 2
    last = jnp.max(run.reshape(2, NY), axis=1) // 2
    low0 = (first - y + NY - 1) // NY
    high0 = jnp.minimum((last - y + NY) // NY, NZ)
    low1 = (nctx - 1 - y - last + NY - 1) // NY
    high1 = jnp.minimum((nctx - 1 - y - first + NY) // NY, NZ)
    count0 = jnp.maximum(high0 - low0, 0)
    count1 = jnp.maximum(high1 - low1, 0)
    sides = jnp.stack([low0, count0, low1, count1], axis=1).reshape(-1)
    runs = jnp.stack([run, begin, upper * NY + source], axis=1).reshape(-1)
    own = jnp.stack([y, c])
    return jnp.concatenate([sides, runs, own]).astype(jnp.int32)


class Tile:
    def __init__(self, info, pairs_ref, heads):
        self.info, self.pairs = info, pairs_ref
        self.keys = pairs_ref.shape[1]
        self.half = self.keys // 2
        self.width = pairs_ref.shape[2] // 2
        self.cols = heads * self.half
        self.runs = 2 * NZ * NY * NC
        own = 2 * FIELDS + 2 * NY * 3
        self.y = info[own]
        self.c = info[own + 1]
        row = lax.broadcasted_iota(jnp.int32, (self.keys, 1), 0)
        core = jnp.where(row < self.half, self.c, 1 - self.c)
        rest = row % self.half
        self.row_low = core * self.half + rest
        self.row_high = (self.runs - 1 - core) * self.half + rest
        self.col_rest = lax.broadcasted_iota(jnp.int32, (1, self.cols), 1) % self.half

    def field(self, side, n):
        return self.info[side * FIELDS + n]

    def run(self, side, k, n):
        return self.info[2 * FIELDS + (side * NY + k) * 3 + n]

    def row(self, side, k):
        return pl.ds(self.run(side, k, 2), 1)

    def count(self, side):
        return self.field(side, 1) + self.field(side, 3)

    def steps(self, side):
        return (self.count(side) + 1) // 2

    def columns(self, side):
        own = [self.run(side, k, 0) * self.half + self.col_rest for k in range(NY)]
        first = [jnp.full((1, self.cols), self.run(side, k, 1) * self.half) for k in range(NY)]
        return jnp.concatenate(own, axis=1), jnp.concatenate(first, axis=1)

    def blocks(self, side, i):
        def place(n):
            lower = self.field(side, 1)
            return jnp.where(
                n >= lower, self.field(side, 2) + NZ + n - lower, self.field(side, 0) + n
            )

        second = jnp.minimum(2 * i + 1, self.count(side) - 1)
        return place(2 * i), place(second)

    def positions(self, side, i, blocks):
        parts = []
        for n, b in enumerate(blocks):
            step = NY * NC * self.half
            low = b * step + self.y * NC * self.half + self.row_low
            high = self.row_high - (b - NZ) * step - self.y * NC * self.half
            at = jnp.where(b >= NZ, high, low)
            if n:
                at = jnp.where(2 * i + 1 < self.count(side), at, jnp.int32(2**30))
            parts.append(at)
        return jnp.concatenate(parts, axis=0)


def two(ref, blocks, lanes, axis):
    return jnp.concatenate([ref[b, :, lanes] for b in blocks], axis=axis)


def gather_kernel(mine, other, pairs, turned):
    half = mine.shape[1] // 2
    width = mine.shape[2] // 2
    for b in range(2 * NZ):
        rows = slice((b // NZ) * half, (b // NZ + 1) * half)
        block = jnp.concatenate([mine[b % NZ, rows], other[b % NZ, rows]], axis=0)
        pairs[b] = block
        turned[b] = block.astype(jnp.float32).T.astype(turned.dtype)


def queries_of(refs, side, second, half, width, heads):
    rows = pl.ds(pl.multiple_of(side * half, half), half)
    lanes = [(heads * second + h) * width for h in range(heads)]
    return jnp.concatenate([r[0, rows, at : at + width] for r in refs for at in lanes], axis=0)


def forward_kernel(heads, info, a0, a1, a2, a3, pairs, turned, u_ref, stats_ref, s_scr, st_scr):
    tile = Tile(info, pairs, heads)
    half, width, cols = tile.half, tile.width, tile.cols
    log2_scale = math.log2(math.e) / math.sqrt(width)
    groups = 2 * tile.keys // 8
    asked = (a0, a1, a2, a3)

    def one_side(side, _):
        queries = queries_of(asked, side, 0, half, width, heads)
        own, first = tile.columns(side)
        steps = tile.steps(side)

        def scores(i, biggest):
            blocks = tile.blocks(side, i)
            at = tile.positions(side, i, blocks)
            s = dot(two(pairs, blocks, slice(0, width), 0), queries, 1, 1)
            s = jnp.where((at <= own) & (at >= first), s, FLOOR)
            s_scr[i] = s
            return jnp.maximum(biggest, jnp.max(s.reshape(groups, 8, NY * cols), axis=0))

        biggest = lax.fori_loop(0, steps, scores, jnp.full((8, NY * cols), FLOOR, jnp.float32))
        top = jnp.max(biggest, axis=0, keepdims=True)
        u_ref[side] = jnp.zeros(u_ref.shape[1:], jnp.float32)

        def sums(i, total):
            e = jnp.exp2((s_scr[i] - top) * log2_scale)
            total = total + jnp.sum(e.reshape(groups, 8, NY * cols), axis=0)
            values_t = jnp.concatenate([turned[b, width:, :] for b in tile.blocks(side, i)], axis=1)
            u_ref[side] += dot(values_t, e.astype(jnp.bfloat16), 1, 0)
            return total

        total = lax.fori_loop(0, steps, sums, jnp.zeros((8, NY * cols), jnp.float32))
        total = jnp.sum(total, axis=0, keepdims=True)
        do_t = queries_of(asked, side, 1, half, width, heads).astype(jnp.float32).T
        seen = jnp.sum(u_ref[side] * do_t, axis=0, keepdims=True)
        for k in range(NY):
            for n, whole in enumerate((top, total, seen)):
                st_scr[n, tile.row(side, k), :] = whole[:, k * cols : (k + 1) * cols]
        return 0

    lax.fori_loop(0, 2, one_side, 0)
    for k in range(NY):
        stats_ref[k] = st_scr[...]


def backward_kernel(
    heads, info, a0, a1, a2, a3, u_ref, pairs, turned, stats,
    o0, o1, o2, o3, dmine, dother, dacc, dq_scr, st_scr,
):
    tile = Tile(info, pairs, heads)
    half, width, cols, keys = tile.half, tile.width, tile.cols, tile.keys
    scale = 1.0 / math.sqrt(width)
    log2_scale = scale * math.log2(math.e)
    asked = (a0, a1, a2, a3)
    dacc[...] = jnp.zeros_like(dacc)

    tops = [stats[k, 0] for k in range(NY)]
    top = functools.reduce(jnp.maximum, tops)
    weights = [jnp.exp2((t - top) * log2_scale) for t in tops]
    den = sum(w * stats[k, 1] for k, w in enumerate(weights))
    inverse = 1.0 / den
    st_scr[0] = top * log2_scale + jnp.log2(den)
    st_scr[1] = sum(w * stats[k, 2] for k, w in enumerate(weights)) * inverse
    st_scr[2] = jnp.exp2((stats[tile.y, 0] - top) * log2_scale) * inverse

    def one_side(side, _):
        queries = queries_of(asked, side, 0, half, width, heads)
        grads = queries_of(asked, side, 1, half, width, heads)
        own, first = tile.columns(side)
        lse2, delta, share = (
            jnp.concatenate([st_scr[n, tile.row(side, k), :] for k in range(NY)], axis=1)
            for n in range(3)
        )
        dq_scr[...] = jnp.zeros_like(dq_scr)

        def visit(i, _):
            blocks = tile.blocks(side, i)
            at = tile.positions(side, i, blocks)
            s = dot(two(pairs, blocks, slice(0, width), 0), queries, 1, 1)
            s = jnp.where((at <= own) & (at >= first), s, FLOOR)
            p = jnp.exp2(s * log2_scale - lse2)
            dp = dot(two(pairs, blocks, slice(width, 2 * width), 0), grads, 1, 1)
            ds = (p * (dp - delta)).astype(jnp.bfloat16)
            dk = dot(ds, queries, 1, 0)
            dv = dot(p.astype(jnp.bfloat16), grads, 1, 0)
            for m, b in enumerate(blocks):
                dacc[b, :, :width] += dk[m * keys : (m + 1) * keys]
                dacc[b, :, width:] += dv[m * keys : (m + 1) * keys]
            keys_t = jnp.concatenate([turned[b, :width, :] for b in blocks], axis=1)
            dq_scr[...] += dot(keys_t, ds, 1, 0)
            return 0

        lax.fori_loop(0, tile.steps(side), visit, 0)
        att = (u_ref[side] * share).T.astype(jnp.bfloat16)
        dq = (dq_scr[...] * scale).T.astype(jnp.bfloat16)
        rows = pl.ds(pl.multiple_of(side * half, half), half)
        for second, whole in ((0, att), (1, dq)):
            for k, out in enumerate((o0, o1, o2, o3)):
                for h in range(heads):
                    at = (heads * second + h) * width
                    out[0, rows, at : at + width] = whole[k * cols + h * half : k * cols + (h + 1) * half]
        return 0

    lax.fori_loop(0, 2, one_side, 0)
    for b in range(2 * NZ):
        rows = slice((b // NZ) * half, (b // NZ + 1) * half)
        for out, part in ((dmine, slice(0, half)), (dother, slice(half, keys))):
            out[b % NZ, rows, :width] = (dacc[b, part, :width] * scale).astype(out.dtype)
            out[b % NZ, rows, width:] = dacc[b, part, width:].astype(out.dtype)


def combine_kernel(o0, o1, o2, o3, dkv, att_ref, dq_ref, dkv_ref, sq_ref):
    wide = att_ref.shape[2]
    parts = [o[0].astype(jnp.float32) for o in (o0, o1, o2, o3)]
    both = (parts[0] + parts[1]) + (parts[2] + parts[3])
    att_ref[0] = both[:, :wide].astype(att_ref.dtype)
    dq = both[:, wide:]
    dq_ref[0] = dq
    total = functools.reduce(jnp.add, [dkv[k].astype(jnp.float32) for k in range(NZ)])
    dkv_ref[0] = total
    squares = jnp.sum(dq * dq) + jnp.sum(total * total)
    sq_ref[...] = jnp.full(sq_ref.shape, squares, jnp.float32)


def scale_kernel(count, sums, dq, dkv, oq, ok, ov):
    lanes = sums.shape[2]
    total = sums[0]
    for k in range(1, sums.shape[0]):
        total = total + sums[k]
    factor = lax.rsqrt(total / count + 1e-06)
    for h in range(dq.shape[2] // lanes):
        at = slice(h * lanes, (h + 1) * lanes)
        oq[0, :, at] = (dq[0, :, at] * factor).astype(oq.dtype)
    width = ok.shape[2]
    ok[0] = (dkv[0, :, :width] * factor).astype(ok.dtype)
    ov[0] = (dkv[0, :, width:] * factor).astype(ov.dtype)


def spread_kernel(keys, values, copies):
    width = keys.shape[2]
    for k in range(copies.shape[0]):
        copies[k, :, :width] = keys[0]
        copies[k, :, width:] = values[0]


def join_kernel(left, right, *outs):
    wide = left.shape[2]
    for out in outs:
        out[:, :, :wide] = left[...]
        out[:, :, wide:] = right[...]


def turn(x, axis, size, by):
    return lax.ppermute(x, axis, [(i, (i + by) % size) for i in range(size)])


def per_device(queries, keys, values, grad_out, doc_starts):
    tok = queries.shape[1]
    wide = queries.shape[2]
    width = keys.shape[2]
    heads = wide // width
    half = tok // 2
    cols = heads * half
    z, y, c = (lax.axis_index(a) for a in ("z", "y", "core"))
    info = visits(doc_starts[0], tok, z, y, c)

    copies = pl.pallas_call(spread_kernel, out_shape=jax.ShapeDtypeStruct((NZ, tok, 2 * width), keys.dtype), in_specs=[VMEM] * 2, out_specs=VMEM, compiler_params=PARAMS)(keys, values)
    mine = lax.all_to_all(copies, "z", 0, 0, tiled=True)
    asked, *ask = pl.pallas_call(join_kernel, out_shape=[jax.ShapeDtypeStruct((1, tok, 2 * wide), keys.dtype)] * NY, in_specs=[VMEM] * 2, out_specs=[VMEM] * NY, compiler_params=PARAMS)(queries, grad_out)
    mine = lax.all_to_all(copies, "z", 0, 0, tiled=True)
    around = {k: turn(ask[k - 1], "y", NY, -k) for k in (2, 1, 3)}
    around[0] = asked
    other = turn(mine, "core", NC, 1)

    f32, bf16 = jnp.float32, jnp.bfloat16
    shape = jax.ShapeDtypeStruct
    pairs, turned = pl.pallas_call(
        gather_kernel,
        out_shape=(shape((2 * NZ, tok, 2 * width), bf16), shape((2 * NZ, 2 * width, tok), bf16)),
        in_specs=[VMEM] * 2,
        out_specs=(VMEM,) * 2,
        compiler_params=PARAMS,
    )(mine, other)
    stat = (3, 2 * NY, cols)

    asks = [around[k] for k in range(NY)]
    u, stats = pl.pallas_call(
        functools.partial(forward_kernel, heads),
        out_shape=(shape((2, width, NY * cols), f32), shape((NY,) + stat, f32)),
        in_specs=[SMEM] + [VMEM] * (NY + 2),
        out_specs=(VMEM, VMEM),
        scratch_shapes=[pltpu.VMEM((NZ, 2 * tok, NY * cols), f32), pltpu.VMEM(stat, f32)],
        compiler_params=PARAMS,
    )(info, *asks, pairs, turned)
    stats = lax.all_to_all(stats, "y", 0, 0, tiled=True)
    *sent, dmine, dother = pl.pallas_call(
        functools.partial(backward_kernel, heads),
        out_shape=[shape(asked.shape, bf16)] * NY
        + [shape(mine.shape, f32), shape(mine.shape, bf16)],
        in_specs=[SMEM] + [VMEM] * (NY + 4),
        out_specs=[VMEM] * (NY + 2),
        scratch_shapes=[
            pltpu.VMEM((2 * NZ, tok, 2 * width), f32),
            pltpu.VMEM((width, NY * cols), f32),
            pltpu.VMEM(stat, f32),
        ],
        compiler_params=PARAMS,
    )(info, *asks, u, pairs, turned, stats)
    back = [sent[0]] + [turn(sent[k], "y", NY, k) for k in range(1, NY)]
    from_core = turn(dother, "core", NC, 1)
    pair = (dmine + from_core.astype(f32)).astype(bf16)
    pieces = lax.all_to_all(pair, "z", 0, 0, tiled=True)
    attended, dq, dkv, squares = pl.pallas_call(
        combine_kernel,
        out_shape=(
            shape(queries.shape, bf16),
            shape(queries.shape, f32),
            shape((1, tok, 2 * width), f32),
            shape((NZ * NC, 1, 128), f32),
        ),
        in_specs=[VMEM] * 5,
        out_specs=(VMEM,) * 4,
        compiler_params=PARAMS,
    )(*back, pieces)
    squares = lax.all_to_all(squares, ("z", "core"), 0, 0, tiled=True)
    ndata = lax.axis_size("dp")
    squares = jnp.broadcast_to(jnp.sum(squares, axis=0, keepdims=True), (NY * ndata, 1, 128))
    squares = lax.all_to_all(squares, ("y", "dp"), 0, 0, tiled=True)
    count = float(ndata * NZ * NY * NC * tok * (wide + 2 * width))
    out_query, out_key, out_value = pl.pallas_call(
        functools.partial(scale_kernel, count),
        out_shape=(shape(queries.shape, bf16), shape(keys.shape, bf16), shape(values.shape, bf16)),
        in_specs=[VMEM] * 3,
        out_specs=(VMEM,) * 3,
        compiler_params=PARAMS,
    )(squares, dq, dkv)
    return attended, out_query, out_key, out_value


def solution(mesh):
    ndata = mesh.shape["dp"]
    fine = Mesh(mesh.devices.reshape(NZ, NY, NC, ndata), ("z", "y", "core", "dp"))
    spec = P("dp", ("z", "y", "core"), None)
    return jax.shard_map(
        per_device,
        mesh=fine,
        in_specs=(spec, spec, spec, spec, P("dp", None)),
        out_specs=(spec, spec, spec, spec),
        check_vma=False,
    )
```

```python
import functools
import math

import jax
import jax.numpy as jnp
from jax import lax
from jax.experimental import pallas as pl
from jax.experimental.pallas import tpu as pltpu
from jax.sharding import Mesh
from jax.sharding import PartitionSpec as P

FLOOR = -1e30
NZ, NY, NC = 8, 4, 2
FIELDS = 4
VMEM = pl.BlockSpec(memory_space=pltpu.VMEM)
SMEM = pl.BlockSpec(memory_space=pltpu.SMEM)
PARAMS = pltpu.CompilerParams(vmem_limit_bytes=40 * 1024 * 1024)


def dot(a, b, ca, cb):
    return lax.dot_general(a, b, (((ca,), (cb,)), ((), ())), preferred_element_type=jnp.float32)


FIELDS = 4
VMEM = pl.BlockSpec(memory_space=pltpu.VMEM)
SMEM = pl.BlockSpec(memory_space=pltpu.SMEM)
PARAMS = pltpu.CompilerParams(vmem_limit_bytes=40 * 1024 * 1024)


def dot(a, b, ca, cb):
    return lax.dot_general(a, b, (((ca,), (cb,)), ((), ())), preferred_element_type=jnp.float32)


def visits(doc_starts, tok, z, y, c):
    nctx = NZ * NY * NC
    half = tok // 2
    source = jnp.tile((y + jnp.arange(NY, dtype=jnp.int32)) % NY, 2)
    upper = jnp.repeat(jnp.arange(2, dtype=jnp.int32), NY)
    base = (z * NY + source) * NC + c
    run = jnp.where(upper == 1, 2 * nctx - 1 - base, base)
    starts = doc_starts // half
    begin = jnp.max(jnp.where(starts[None, :] <= run[:, None], starts[None, :], 0), axis=1)
    first = jnp.min(begin.reshape(2, NY), axis=1) // 2
    last = jnp.max(run.reshape(2, NY), axis=1) // 2
    low0 = (first - y + NY - 1) // NY
    high0 = jnp.minimum((last - y + NY) // NY, NZ)
    low1 = (nctx - 1 - y - last + NY - 1) // NY
    high1 = jnp.minimum((nctx - 1 - y - first + NY) // NY, NZ)
    count0 = jnp.maximum(high0 - low0, 0)
    count1 = jnp.maximum(high1 - low1, 0)
    sides = jnp.stack([low0, count0, low1, count1], axis=1).reshape(-1)
    runs = jnp.stack([run, begin, upper * NY + source], axis=1).reshape(-1)
    own = jnp.stack([y, c])
    return jnp.concatenate([sides, runs, own]).astype(jnp.int32)


class Tile:
    def __init__(self, info, pairs_ref, heads):
        self.info, self.pairs = info, pairs_ref
        self.keys = pairs_ref.shape[1]
        self.half = self.keys // 2
        self.width = pairs_ref.shape[2] // 2
        self.cols = heads * self.half
        self.runs = 2 * NZ * NY * NC
        own = 2 * FIELDS + 2 * NY * 3
        self.y = info[own]
        self.c = info[own + 1]
        row = lax.broadcasted_iota(jnp.int32, (self.keys, 1), 0)
        core = jnp.where(row < self.half, self.c, 1 - self.c)
        rest = row % self.half
        self.row_low = core * self.half + rest
        self.row_high = (self.runs - 1 - core) * self.half + rest
        self.col_rest = lax.broadcasted_iota(jnp.int32, (1, self.cols), 1) % self.half

    def field(self, side, n):
        return self.info[side * FIELDS + n]

    def run(self, side, k, n):
        return self.info[2 * FIELDS + (side * NY + k) * 3 + n]

    def row(self, side, k):
        return pl.ds(self.run(side, k, 2), 1)

    def count(self, side):
        return self.field(side, 1) + self.field(side, 3)

    def steps(self, side):
        return (self.count(side) + 1) // 2

    def columns(self, side):
        own = [self.run(side, k, 0) * self.half + self.col_rest for k in range(NY)]
        first = [jnp.full((1, self.cols), self.run(side, k, 1) * self.half) for k in range(NY)]
        return jnp.concatenate(own, axis=1), jnp.concatenate(first, axis=1)

    def blocks(self, side, i):
        def place(n):
            lower = self.field(side, 1)
            return jnp.where(
                n >= lower, self.field(side, 2) + NZ + n - lower, self.field(side, 0) + n
            )

        second = jnp.minimum(2 * i + 1, self.count(side) - 1)
        return place(2 * i), place(second)

    def positions(self, side, i, blocks):
        parts = []
        for n, b in enumerate(blocks):
            step = NY * NC * self.half
            low = b * step + self.y * NC * self.half + self.row_low
            high = self.row_high - (b - NZ) * step - self.y * NC * self.half
            at = jnp.where(b >= NZ, high, low)
            if n:
                at = jnp.where(2 * i + 1 < self.count(side), at, jnp.int32(2**30))
            parts.append(at)
        return jnp.concatenate(parts, axis=0)


def two(ref, blocks, lanes, axis):
    return jnp.concatenate([ref[b, :, lanes] for b in blocks], axis=axis)


def gather_kernel(mine, other, pairs, turned):
    half = mine.shape[1] // 2
    width = mine.shape[2] // 2
    for b in range(2 * NZ):
        rows = slice((b // NZ) * half, (b // NZ + 1) * half)
        block = jnp.concatenate([mine[b % NZ, rows], other[b % NZ, rows]], axis=0)
        pairs[b] = block
        turned[b] = block.astype(jnp.float32).T.astype(turned.dtype)


def queries_of(refs, side, second, half, width, heads):
    rows = pl.ds(pl.multiple_of(side * half, half), half)
    lanes = [(heads * second + h) * width for h in range(heads)]
    return jnp.concatenate([r[0, rows, at : at + width] for r in refs for at in lanes], axis=0)


def forward_kernel(heads, info, a0, a1, a2, a3, pairs, turned, u_ref, stats_ref, s_scr, st_scr):
    tile = Tile(info, pairs, heads)
    half, width, cols = tile.half, tile.width, tile.cols
    log2_scale = math.log2(math.e) / math.sqrt(width)
    groups = 2 * tile.keys // 8
    asked = (a0, a1, a2, a3)

    def one_side(side, _):
        queries = queries_of(asked, side, 0, half, width, heads)
        own, first = tile.columns(side)
        steps = tile.steps(side)

        def scores(i, biggest):
            blocks = tile.blocks(side, i)
            at = tile.positions(side, i, blocks)
            s = dot(two(pairs, blocks, slice(0, width), 0), queries, 1, 1)
            s = jnp.where((at <= own) & (at >= first), s, FLOOR)
            s_scr[i] = s
            return jnp.maximum(biggest, jnp.max(s.reshape(groups, 8, NY * cols), axis=0))

        biggest = lax.fori_loop(0, steps, scores, jnp.full((8, NY * cols), FLOOR, jnp.float32))
        top = jnp.max(biggest, axis=0, keepdims=True)
        u_ref[side] = jnp.zeros(u_ref.shape[1:], jnp.float32)

        def sums(i, total):
            e = jnp.exp2((s_scr[i] - top) * log2_scale)
            total = total + jnp.sum(e.reshape(groups, 8, NY * cols), axis=0)
            values_t = jnp.concatenate([turned[b, width:, :] for b in tile.blocks(side, i)], axis=1)
            u_ref[side] += dot(values_t, e.astype(jnp.bfloat16), 1, 0)
            return total

        total = lax.fori_loop(0, steps, sums, jnp.zeros((8, NY * cols), jnp.float32))
        total = jnp.sum(total, axis=0, keepdims=True)
        do_t = queries_of(asked, side, 1, half, width, heads).astype(jnp.float32).T
        seen = jnp.sum(u_ref[side] * do_t, axis=0, keepdims=True)
        for k in range(NY):
            for n, whole in enumerate((top, total, seen)):
                st_scr[n, tile.row(side, k), :] = whole[:, k * cols : (k + 1) * cols]
        return 0

    lax.fori_loop(0, 2, one_side, 0)
    for k in range(NY):
        stats_ref[k] = st_scr[...]


def backward_kernel(
    heads, info, a0, a1, a2, a3, u_ref, pairs, turned, stats,
    t0, t1, t2, t3, o0, o1, o2, o3, dmine, dother, dacc, dq_scr, st_scr,
):
    tile = Tile(info, pairs, heads)
    half, width, cols, keys = tile.half, tile.width, tile.cols, tile.keys
    scale = 1.0 / math.sqrt(width)
    log2_scale = scale * math.log2(math.e)
    asked = (a0, a1, a2, a3)
    dacc[...] = jnp.zeros_like(dacc)

    tops = [stats[k, 0] for k in range(NY)]
    top = functools.reduce(jnp.maximum, tops)
    weights = [jnp.exp2((t - top) * log2_scale) for t in tops]
    den = sum(w * stats[k, 1] for k, w in enumerate(weights))
    inverse = 1.0 / den
    st_scr[0] = top * log2_scale + jnp.log2(den)
    st_scr[1] = sum(w * stats[k, 2] for k, w in enumerate(weights)) * inverse
    st_scr[2] = jnp.exp2((stats[tile.y, 0] - top) * log2_scale) * inverse

    def one_side(side, _):
        queries = queries_of(asked, side, 0, half, width, heads)
        grads = queries_of(asked, side, 1, half, width, heads)
        own, first = tile.columns(side)
        lse2, delta, share = (
            jnp.concatenate([st_scr[n, tile.row(side, k), :] for k in range(NY)], axis=1)
            for n in range(3)
        )
        dq_scr[...] = jnp.zeros_like(dq_scr)

        def visit(i, _):
            blocks = tile.blocks(side, i)
            at = tile.positions(side, i, blocks)
            s = dot(two(pairs, blocks, slice(0, width), 0), queries, 1, 1)
            s = jnp.where((at <= own) & (at >= first), s, FLOOR)
            p = jnp.exp2(s * log2_scale - lse2)
            dp = dot(two(pairs, blocks, slice(width, 2 * width), 0), grads, 1, 1)
            ds = (p * (dp - delta)).astype(jnp.bfloat16)
            dk = dot(ds, queries, 1, 0)
            dv = dot(p.astype(jnp.bfloat16), grads, 1, 0)
            for m, b in enumerate(blocks):
                dacc[b, :, :width] += dk[m * keys : (m + 1) * keys]
                dacc[b, :, width:] += dv[m * keys : (m + 1) * keys]
            keys_t = jnp.concatenate([turned[b, :width, :] for b in blocks], axis=1)
            dq_scr[...] += dot(keys_t, ds, 1, 0)
            return 0

        lax.fori_loop(0, tile.steps(side), visit, 0)
        att = (u_ref[side] * share).T.astype(jnp.bfloat16)
        dq = (dq_scr[...] * scale).T.astype(jnp.bfloat16)
        rows = pl.ds(pl.multiple_of(side * half, half), half)
        for whole, outs in ((att, (t0, t1, t2, t3)), (dq, (o0, o1, o2, o3))):
            for k, out in enumerate(outs):
                for h in range(heads):
                    at = k * cols + h * half
                    out[0, rows, h * width : (h + 1) * width] = whole[at : at + half]
        return 0

    lax.fori_loop(0, 2, one_side, 0)
    for b in range(2 * NZ):
        rows = slice((b // NZ) * half, (b // NZ + 1) * half)
        for out, part in ((dmine, slice(0, half)), (dother, slice(half, keys))):
            out[b % NZ, rows, :width] = (dacc[b, part, :width] * scale).astype(out.dtype)
            out[b % NZ, rows, width:] = dacc[b, part, width:].astype(out.dtype)


def combine_kernel(o0, o1, o2, o3, dkv, dq_ref, dkv_ref, sq_ref):
    parts = [o[0].astype(jnp.float32) for o in (o0, o1, o2, o3)]
    dq = (parts[0] + parts[1]) + (parts[2] + parts[3])
    dq_ref[0] = dq
    total = functools.reduce(jnp.add, [dkv[k].astype(jnp.float32) for k in range(NZ)])
    dkv_ref[0] = total
    squares = jnp.sum(dq * dq) + jnp.sum(total * total)
    sq_ref[...] = jnp.full(sq_ref.shape, squares, jnp.float32)


def release_kernel(order, *refs):
    del order
    count = len(refs) // 2
    for a, b in zip(refs[:count], refs[count:]):
        b[...] = a[...]


def attended_kernel(a0, a1, a2, a3, out):
    parts = [a[...].astype(jnp.float32) for a in (a0, a1, a2, a3)]
    out[...] = ((parts[0] + parts[1]) + (parts[2] + parts[3])).astype(out.dtype)


def fold_kernel(parts, out):
    total = functools.reduce(jnp.add, [parts[k] for k in range(parts.shape[0])])
    for k in range(out.shape[0]):
        out[k] = total


def scale_kernel(count, sums, dq, dkv, oq, ok, ov):
    lanes = sums.shape[2]
    total = sums[0]
    for k in range(1, sums.shape[0]):
        total = total + sums[k]
    factor = lax.rsqrt(total / count + 1e-06)
    for h in range(dq.shape[2] // lanes):
        at = slice(h * lanes, (h + 1) * lanes)
        oq[0, :, at] = (dq[0, :, at] * factor).astype(oq.dtype)
    width = ok.shape[2]
    ok[0] = (dkv[0, :, :width] * factor).astype(ok.dtype)
    ov[0] = (dkv[0, :, width:] * factor).astype(ov.dtype)


def spread_kernel(keys, values, order, copies):
    del order
    width = keys.shape[2]
    for k in range(copies.shape[0]):
        copies[k, :, :width] = keys[0]
        copies[k, :, width:] = values[0]


def join_kernel(left, right, *outs):
    wide = left.shape[2]
    for out in outs:
        out[:, :, :wide] = left[...]
        out[:, :, wide:] = right[...]


def turn(x, axis, size, by):
    return lax.ppermute(x, axis, [(i, (i + by) % size) for i in range(size)])


def per_device(queries, keys, values, grad_out, doc_starts):
    tok = queries.shape[1]
    wide = queries.shape[2]
    width = keys.shape[2]
    heads = wide // width
    half = tok // 2
    cols = heads * half
    z, y, c = (lax.axis_index(a) for a in ("z", "y", "core"))
    info = visits(doc_starts[0], tok, z, y, c)

    block = jax.ShapeDtypeStruct((1, tok, 2 * wide), keys.dtype)
    far = pl.pallas_call(
        join_kernel,
        out_shape=[block],
        in_specs=[VMEM] * 2,
        out_specs=[VMEM],
        compiler_params=PARAMS,
    )(queries, grad_out)
    copies = pl.pallas_call(
        spread_kernel,
        out_shape=jax.ShapeDtypeStruct((NZ, tok, 2 * width), keys.dtype),
        in_specs=[VMEM] * 3,
        out_specs=VMEM,
        compiler_params=PARAMS,
    )(keys, values, far[0])
    asked, *near = pl.pallas_call(
        join_kernel,
        out_shape=[block] * (NY - 1),
        in_specs=[VMEM] * 2,
        out_specs=[VMEM] * (NY - 1),
        compiler_params=PARAMS,
    )(queries, grad_out)
    mine = lax.all_to_all(copies, "z", 0, 0, tiled=True)
    around = {0: asked, 1: turn(near[0], "y", NY, -1), 2: turn(far[0], "y", NY, -2), 3: turn(near[1], "y", NY, -3)}
    other = turn(mine, "core", NC, 1)

    f32, bf16 = jnp.float32, jnp.bfloat16
    shape = jax.ShapeDtypeStruct
    pairs, turned = pl.pallas_call(
        gather_kernel,
        out_shape=(shape((2 * NZ, tok, 2 * width), bf16), shape((2 * NZ, 2 * width, tok), bf16)),
        in_specs=[VMEM] * 2,
        out_specs=(VMEM,) * 2,
        compiler_params=PARAMS,
    )(mine, other)
    stat = (3, 2 * NY, cols)

    asks = [around[k] for k in range(NY)]
    u, stats = pl.pallas_call(
        functools.partial(forward_kernel, heads),
        out_shape=(shape((2, width, NY * cols), f32), shape((NY,) + stat, f32)),
        in_specs=[SMEM] + [VMEM] * (NY + 2),
        out_specs=(VMEM, VMEM),
        scratch_shapes=[pltpu.VMEM((NZ, 2 * tok, NY * cols), f32), pltpu.VMEM(stat, f32)],
        compiler_params=PARAMS,
    )(info, *asks, pairs, turned)
    stats = lax.all_to_all(stats, "y", 0, 0, tiled=True)
    *sent, dmine, dother = pl.pallas_call(
        functools.partial(backward_kernel, heads),
        out_shape=[shape(queries.shape, bf16)] * (2 * NY)
        + [shape(mine.shape, f32), shape(mine.shape, bf16)],
        in_specs=[SMEM] + [VMEM] * (NY + 4),
        out_specs=[VMEM] * (2 * NY + 2),
        scratch_shapes=[
            pltpu.VMEM((2 * NZ, tok, 2 * width), f32),
            pltpu.VMEM((width, NY * cols), f32),
            pltpu.VMEM(stat, f32),
        ],
        compiler_params=PARAMS,
    )(info, *asks, u, pairs, turned, stats)
    seen, sent = sent[:NY], sent[NY:]
    back = [sent[0]] + [turn(sent[k], "y", NY, k) for k in range(1, NY)]
    from_core = turn(dother, "core", NC, 1)
    pair = (dmine + from_core.astype(f32)).astype(bf16)
    pieces = lax.all_to_all(pair, "z", 0, 0, tiled=True)
    dq, dkv, squares = pl.pallas_call(
        combine_kernel,
        out_shape=[
            shape(queries.shape, f32),
            shape((1, tok, 2 * width), f32),
            shape((NZ * NC, 1, 128), f32),
        ],
        in_specs=[VMEM] * (NY + 1),
        out_specs=[VMEM] * 3,
        compiler_params=PARAMS,
    )(*back, pieces)
    released = pl.pallas_call(
        release_kernel,
        out_shape=[shape(queries.shape, bf16)] * (NY - 1),
        in_specs=[VMEM] * NY,
        out_specs=[VMEM] * (NY - 1),
        compiler_params=PARAMS,
    )(squares, *seen[1:])
    squares = lax.all_to_all(squares, ("z", "core"), 0, 0, tiled=True)
    home = [seen[0]] + [turn(released[k - 1], "y", NY, k) for k in range(1, NY)]
    ndata = lax.axis_size("dp")
    squares = pl.pallas_call(
        fold_kernel,
        out_shape=shape((NY * ndata, 1, 128), f32),
        in_specs=[VMEM],
        out_specs=VMEM,
        compiler_params=PARAMS,
        cost_estimate=pl.CostEstimate(flops=10**9, transcendentals=0, bytes_accessed=0),
    )(squares)
    squares = lax.all_to_all(squares, ("y", "dp"), 0, 0, tiled=True)
    attended = pl.pallas_call(
        attended_kernel,
        out_shape=shape(queries.shape, bf16),
        in_specs=[VMEM] * NY,
        out_specs=VMEM,
        compiler_params=PARAMS,
    )(*home)
    count = float(ndata * NZ * NY * NC * tok * (wide + 2 * width))
    out_query, out_key, out_value = pl.pallas_call(
        functools.partial(scale_kernel, count),
        out_shape=(shape(queries.shape, bf16), shape(keys.shape, bf16), shape(values.shape, bf16)),
        in_specs=[VMEM] * 3,
        out_specs=(VMEM,) * 3,
        compiler_params=PARAMS,
    )(squares, dq, dkv)
    return attended, out_query, out_key, out_value


def solution(mesh):
    ndata = mesh.shape["dp"]
    fine = Mesh(mesh.devices.reshape(NZ, NY, NC, ndata), ("z", "y", "core", "dp"))
    spec = P("dp", ("z", "y", "core"), None)
    return jax.shard_map(
        per_device,
        mesh=fine,
        in_specs=(spec, spec, spec, spec, P("dp", None)),
        out_specs=(spec, spec, spec, spec),
        check_vma=False,
    )
```

```python
import functools
import math

import jax
import jax.numpy as jnp
from jax import lax
from jax.experimental import pallas as pl
from jax.experimental.pallas import tpu as pltpu
from jax.sharding import Mesh
from jax.sharding import PartitionSpec as P

FLOOR = -1e30
NZ, NY, NC = 8, 4, 2
FIELDS = 4
VMEM = pl.BlockSpec(memory_space=pltpu.VMEM)
FAR = pl.BlockSpec(memory_space=pl.ANY)
SMEM = pl.BlockSpec(memory_space=pltpu.SMEM)
ALONE = pltpu.CompilerParams(vmem_limit_bytes=62 * 1024 * 1024)
PARAMS = pltpu.CompilerParams(vmem_limit_bytes=40 * 1024 * 1024)


def dot(a, b, ca, cb):
    return lax.dot_general(a, b, (((ca,), (cb,)), ((), ())), preferred_element_type=jnp.float32)


FIELDS = 4
VMEM = pl.BlockSpec(memory_space=pltpu.VMEM)
FAR = pl.BlockSpec(memory_space=pl.ANY)
SMEM = pl.BlockSpec(memory_space=pltpu.SMEM)
ALONE = pltpu.CompilerParams(vmem_limit_bytes=62 * 1024 * 1024)
PARAMS = pltpu.CompilerParams(vmem_limit_bytes=40 * 1024 * 1024)


def dot(a, b, ca, cb):
    return lax.dot_general(a, b, (((ca,), (cb,)), ((), ())), preferred_element_type=jnp.float32)


def visits(doc_starts, tok, z, y, c):
    nctx = NZ * NY * NC
    half = tok // 2
    source = jnp.tile((y + jnp.arange(NY, dtype=jnp.int32)) % NY, 2)
    upper = jnp.repeat(jnp.arange(2, dtype=jnp.int32), NY)
    base = (z * NY + source) * NC + c
    run = jnp.where(upper == 1, 2 * nctx - 1 - base, base)
    starts = doc_starts // half
    begin = jnp.max(jnp.where(starts[None, :] <= run[:, None], starts[None, :], 0), axis=1)
    first = jnp.min(begin.reshape(2, NY), axis=1) // 2
    last = jnp.max(run.reshape(2, NY), axis=1) // 2
    low0 = (first - y + NY - 1) // NY
    high0 = jnp.minimum((last - y + NY) // NY, NZ)
    low1 = (nctx - 1 - y - last + NY - 1) // NY
    high1 = jnp.minimum((nctx - 1 - y - first + NY) // NY, NZ)
    count0 = jnp.maximum(high0 - low0, 0)
    count1 = jnp.maximum(high1 - low1, 0)
    sides = jnp.stack([low0, count0, low1, count1], axis=1).reshape(-1)
    runs = jnp.stack([run, begin, upper * NY + source], axis=1).reshape(-1)
    own = jnp.stack([y, c])
    return jnp.concatenate([sides, runs, own]).astype(jnp.int32)


class Tile:
    def __init__(self, info, pairs_ref, heads):
        self.info, self.pairs = info, pairs_ref
        self.keys = pairs_ref.shape[1]
        self.half = self.keys // 2
        self.width = pairs_ref.shape[2] // 2
        self.cols = heads * self.half
        self.runs = 2 * NZ * NY * NC
        own = 2 * FIELDS + 2 * NY * 3
        self.y = info[own]
        self.c = info[own + 1]
        row = lax.broadcasted_iota(jnp.int32, (self.keys, 1), 0)
        core = jnp.where(row < self.half, self.c, 1 - self.c)
        rest = row % self.half
        self.row_low = core * self.half + rest
        self.row_high = (self.runs - 1 - core) * self.half + rest
        self.col_rest = lax.broadcasted_iota(jnp.int32, (1, self.cols), 1) % self.half

    def field(self, side, n):
        return self.info[side * FIELDS + n]

    def run(self, side, k, n):
        return self.info[2 * FIELDS + (side * NY + k) * 3 + n]

    def row(self, side, k):
        return pl.ds(self.run(side, k, 2), 1)

    def count(self, side):
        return self.field(side, 1) + self.field(side, 3)

    def steps(self, side):
        return (self.count(side) + 1) // 2

    def columns(self, side):
        own = [self.run(side, k, 0) * self.half + self.col_rest for k in range(NY)]
        first = [jnp.full((1, self.cols), self.run(side, k, 1) * self.half) for k in range(NY)]
        return jnp.concatenate(own, axis=1), jnp.concatenate(first, axis=1)

    def blocks(self, side, i):
        def place(n):
            lower = self.field(side, 1)
            return jnp.where(
                n >= lower, self.field(side, 2) + NZ + n - lower, self.field(side, 0) + n
            )

        second = jnp.minimum(2 * i + 1, self.count(side) - 1)
        return place(2 * i), place(second)

    def positions(self, side, i, blocks):
        parts = []
        for n, b in enumerate(blocks):
            step = NY * NC * self.half
            low = b * step + self.y * NC * self.half + self.row_low
            high = self.row_high - (b - NZ) * step - self.y * NC * self.half
            at = jnp.where(b >= NZ, high, low)
            if n:
                at = jnp.where(2 * i + 1 < self.count(side), at, jnp.int32(2**30))
            parts.append(at)
        return jnp.concatenate(parts, axis=0)


def two(ref, blocks, lanes, axis):
    return jnp.concatenate([ref[b, :, lanes] for b in blocks], axis=axis)


def gather_kernel(mine, other, pairs, turned):
    half = mine.shape[1] // 2
    width = mine.shape[2] // 2
    for b in range(2 * NZ):
        rows = slice((b // NZ) * half, (b // NZ + 1) * half)
        block = jnp.concatenate([mine[b % NZ, rows], other[b % NZ, rows]], axis=0)
        pairs[b] = block
        turned[b] = block.astype(jnp.float32).T.astype(turned.dtype)


def queries_of(refs, side, second, half, width, heads):
    rows = pl.ds(pl.multiple_of(side * half, half), half)
    lanes = [(heads * second + h) * width for h in range(heads)]
    return jnp.concatenate([r[0, rows, at : at + width] for r in refs for at in lanes], axis=0)


def forward_kernel(heads, info, a0, a1, a2, a3, pairs, turned, u_ref, stats_ref, s_scr, st_scr):
    tile = Tile(info, pairs, heads)
    half, width, cols = tile.half, tile.width, tile.cols
    log2_scale = math.log2(math.e) / math.sqrt(width)
    groups = 2 * tile.keys // 8
    asked = (a0, a1, a2, a3)

    def one_side(side, _):
        queries = queries_of(asked, side, 0, half, width, heads)
        own, first = tile.columns(side)
        steps = tile.steps(side)

        def scores(i, biggest):
            blocks = tile.blocks(side, i)
            at = tile.positions(side, i, blocks)
            s = dot(two(pairs, blocks, slice(0, width), 0), queries, 1, 1)
            s = jnp.where((at <= own) & (at >= first), s, FLOOR)
            s_scr[i] = s
            return jnp.maximum(biggest, jnp.max(s.reshape(groups, 8, NY * cols), axis=0))

        biggest = lax.fori_loop(0, steps, scores, jnp.full((8, NY * cols), FLOOR, jnp.float32))
        top = jnp.max(biggest, axis=0, keepdims=True)
        u_ref[side] = jnp.zeros(u_ref.shape[1:], jnp.float32)

        def sums(i, total):
            e = jnp.exp2((s_scr[i] - top) * log2_scale)
            total = total + jnp.sum(e.reshape(groups, 8, NY * cols), axis=0)
            values_t = jnp.concatenate([turned[b, width:, :] for b in tile.blocks(side, i)], axis=1)
            u_ref[side] += dot(values_t, e.astype(jnp.bfloat16), 1, 0)
            return total

        total = lax.fori_loop(0, steps, sums, jnp.zeros((8, NY * cols), jnp.float32))
        total = jnp.sum(total, axis=0, keepdims=True)
        do_t = queries_of(asked, side, 1, half, width, heads).astype(jnp.float32).T
        seen = jnp.sum(u_ref[side] * do_t, axis=0, keepdims=True)
        for k in range(NY):
            for n, whole in enumerate((top, total, seen)):
                st_scr[n, tile.row(side, k), :] = whole[:, k * cols : (k + 1) * cols]
        return 0

    lax.fori_loop(0, 2, one_side, 0)
    for k in range(NY):
        stats_ref[k] = st_scr[...]


def backward_kernel(
    heads, info, a0, a1, a2, a3, u_ref, pairs, turned, stats,
    t0, t1, t2, t3, o0, o1, o2, o3, dmine, dother, dacc, dq_scr, st_scr,
):
    tile = Tile(info, pairs, heads)
    half, width, cols, keys = tile.half, tile.width, tile.cols, tile.keys
    scale = 1.0 / math.sqrt(width)
    log2_scale = scale * math.log2(math.e)
    asked = (a0, a1, a2, a3)
    dacc[...] = jnp.zeros_like(dacc)

    tops = [stats[k, 0] for k in range(NY)]
    top = functools.reduce(jnp.maximum, tops)
    weights = [jnp.exp2((t - top) * log2_scale) for t in tops]
    den = sum(w * stats[k, 1] for k, w in enumerate(weights))
    inverse = 1.0 / den
    st_scr[0] = top * log2_scale + jnp.log2(den)
    st_scr[1] = sum(w * stats[k, 2] for k, w in enumerate(weights)) * inverse
    st_scr[2] = jnp.exp2((stats[tile.y, 0] - top) * log2_scale) * inverse

    def one_side(side, _):
        queries = queries_of(asked, side, 0, half, width, heads)
        grads = queries_of(asked, side, 1, half, width, heads)
        own, first = tile.columns(side)
        lse2, delta, share = (
            jnp.concatenate([st_scr[n, tile.row(side, k), :] for k in range(NY)], axis=1)
            for n in range(3)
        )
        dq_scr[...] = jnp.zeros_like(dq_scr)

        def visit(i, _):
            blocks = tile.blocks(side, i)
            at = tile.positions(side, i, blocks)
            s = dot(two(pairs, blocks, slice(0, width), 0), queries, 1, 1)
            s = jnp.where((at <= own) & (at >= first), s, FLOOR)
            p = jnp.exp2(s * log2_scale - lse2)
            dp = dot(two(pairs, blocks, slice(width, 2 * width), 0), grads, 1, 1)
            ds = (p * (dp - delta)).astype(jnp.bfloat16)
            dk = dot(ds, queries, 1, 0)
            dv = dot(p.astype(jnp.bfloat16), grads, 1, 0)
            for m, b in enumerate(blocks):
                dacc[b, :, :width] += dk[m * keys : (m + 1) * keys]
                dacc[b, :, width:] += dv[m * keys : (m + 1) * keys]
            keys_t = jnp.concatenate([turned[b, :width, :] for b in blocks], axis=1)
            dq_scr[...] += dot(keys_t, ds, 1, 0)
            return 0

        lax.fori_loop(0, tile.steps(side), visit, 0)
        att = (u_ref[side] * share).T.astype(jnp.bfloat16)
        dq = (dq_scr[...] * scale).T.astype(jnp.bfloat16)
        rows = pl.ds(pl.multiple_of(side * half, half), half)
        for whole, outs in ((att, (t0, t1, t2, t3)), (dq, (o0, o1, o2, o3))):
            for k, out in enumerate(outs):
                for h in range(heads):
                    at = k * cols + h * half
                    out[0, rows, h * width : (h + 1) * width] = whole[at : at + half]
        return 0

    lax.fori_loop(0, 2, one_side, 0)
    for b in range(2 * NZ):
        rows = slice((b // NZ) * half, (b // NZ + 1) * half)
        for out, part in ((dmine, slice(0, half)), (dother, slice(half, keys))):
            out[b % NZ, rows, :width] = (dacc[b, part, :width] * scale).astype(out.dtype)
            out[b % NZ, rows, width:] = dacc[b, part, width:].astype(out.dtype)


def combine_kernel(o0, o1, o2, o3, dkv, dq_ref, dkv_ref, sq_ref):
    parts = [o[0].astype(jnp.float32) for o in (o0, o1, o2, o3)]
    dq = (parts[0] + parts[1]) + (parts[2] + parts[3])
    dq_ref[0] = dq
    total = functools.reduce(jnp.add, [dkv[k].astype(jnp.float32) for k in range(NZ)])
    dkv_ref[0] = total
    squares = jnp.sum(dq * dq) + jnp.sum(total * total)
    sq_ref[...] = jnp.full(sq_ref.shape, squares, jnp.float32)


def attended_kernel(a0, a1, a2, a3, out):
    parts = [a[...].astype(jnp.float32) for a in (a0, a1, a2, a3)]
    out[...] = ((parts[0] + parts[1]) + (parts[2] + parts[3])).astype(out.dtype)


def fold_kernel(parts, out):
    total = functools.reduce(jnp.add, [parts[k] for k in range(parts.shape[0])])
    for k in range(out.shape[0]):
        out[k] = total


def scale_kernel(count, sums, dq, dkv, oq, ok, ov):
    lanes = sums.shape[2]
    total = sums[0]
    for k in range(1, sums.shape[0]):
        total = total + sums[k]
    factor = lax.rsqrt(total / count + 1e-06)
    for h in range(dq.shape[2] // lanes):
        at = slice(h * lanes, (h + 1) * lanes)
        oq[0, :, at] = (dq[0, :, at] * factor).astype(oq.dtype)
    width = ok.shape[2]
    ok[0] = (dkv[0, :, :width] * factor).astype(ok.dtype)
    ov[0] = (dkv[0, :, width:] * factor).astype(ov.dtype)


def run_copies(pairs, sems):
    copies = [pltpu.make_async_copy(a, b, sems.at[n]) for n, (a, b) in enumerate(pairs)]
    for copy in copies:
        copy.start()
    for copy in copies:
        copy.wait()


def spread_kernel(keys, values, order, copies, sems):
    del order
    width = keys.shape[2]
    sides = ((keys, slice(0, width)), (values, slice(width, 2 * width)))
    run_copies(
        [(x.at[0], copies.at[k, :, at]) for k in range(copies.shape[0]) for x, at in sides], sems
    )


def join_kernel(left, right, *refs):
    *outs, sems = refs
    wide = left.shape[2]
    sides = ((left, slice(0, wide)), (right, slice(wide, 2 * wide)))
    run_copies([(x, out.at[:, :, at]) for out in outs for x, at in sides], sems)


def turn(x, axis, size, by):
    return lax.ppermute(x, axis, [(i, (i + by) % size) for i in range(size)])


def per_device(queries, keys, values, grad_out, doc_starts):
    tok = queries.shape[1]
    wide = queries.shape[2]
    width = keys.shape[2]
    heads = wide // width
    half = tok // 2
    cols = heads * half
    z, y, c = (lax.axis_index(a) for a in ("z", "y", "core"))
    info = visits(doc_starts[0], tok, z, y, c)

    block = jax.ShapeDtypeStruct((1, tok, 2 * wide), keys.dtype)
    far = pl.pallas_call(
        join_kernel,
        out_shape=[block],
        in_specs=[FAR] * 2,
        out_specs=[VMEM],
        scratch_shapes=[pltpu.SemaphoreType.DMA((2,))],
        compiler_params=ALONE,
    )(queries, grad_out)
    copies = pl.pallas_call(
        spread_kernel,
        out_shape=jax.ShapeDtypeStruct((NZ, tok, 2 * width), keys.dtype),
        in_specs=[FAR] * 3,
        out_specs=VMEM,
        scratch_shapes=[pltpu.SemaphoreType.DMA((2 * NZ,))],
        compiler_params=ALONE,
    )(keys, values, far[0])
    asked, *near = pl.pallas_call(
        join_kernel,
        out_shape=[block] * (NY - 1),
        in_specs=[FAR] * 2,
        out_specs=[VMEM] * (NY - 1),
        scratch_shapes=[pltpu.SemaphoreType.DMA((2 * (NY - 1),))],
        compiler_params=ALONE,
    )(queries, grad_out)
    mine = lax.all_to_all(copies, "z", 0, 0, tiled=True)
    around = {0: asked, 1: turn(near[0], "y", NY, -1), 2: turn(far[0], "y", NY, -2), 3: turn(near[1], "y", NY, -3)}
    other = turn(mine, "core", NC, 1)

    f32, bf16 = jnp.float32, jnp.bfloat16
    shape = jax.ShapeDtypeStruct
    pairs, turned = pl.pallas_call(
        gather_kernel,
        out_shape=(shape((2 * NZ, tok, 2 * width), bf16), shape((2 * NZ, 2 * width, tok), bf16)),
        in_specs=[VMEM] * 2,
        out_specs=(VMEM,) * 2,
        compiler_params=PARAMS,
    )(mine, other)
    stat = (3, 2 * NY, cols)

    asks = [around[k] for k in range(NY)]
    u, stats = pl.pallas_call(
        functools.partial(forward_kernel, heads),
        out_shape=(shape((2, width, NY * cols), f32), shape((NY,) + stat, f32)),
        in_specs=[SMEM] + [VMEM] * (NY + 2),
        out_specs=(VMEM, VMEM),
        scratch_shapes=[pltpu.VMEM((NZ, 2 * tok, NY * cols), f32), pltpu.VMEM(stat, f32)],
        compiler_params=PARAMS,
    )(info, *asks, pairs, turned)
    stats = lax.all_to_all(stats, "y", 0, 0, tiled=True)
    *sent, dmine, dother = pl.pallas_call(
        functools.partial(backward_kernel, heads),
        out_shape=[shape(queries.shape, bf16)] * (2 * NY)
        + [shape(mine.shape, f32), shape(mine.shape, bf16)],
        in_specs=[SMEM] + [VMEM] * (NY + 4),
        out_specs=[VMEM] * (2 * NY + 2),
        scratch_shapes=[
            pltpu.VMEM((2 * NZ, tok, 2 * width), f32),
            pltpu.VMEM((width, NY * cols), f32),
            pltpu.VMEM(stat, f32),
        ],
        compiler_params=PARAMS,
    )(info, *asks, u, pairs, turned, stats)
    seen, sent = sent[:NY], sent[NY:]
    back = [sent[0]] + [turn(sent[k], "y", NY, k) for k in range(1, NY)]
    from_core = turn(dother, "core", NC, 1)
    pair = (dmine + from_core.astype(f32)).astype(bf16)
    pieces = lax.all_to_all(pair, "z", 0, 0, tiled=True)
    dq, dkv, squares = pl.pallas_call(
        combine_kernel,
        out_shape=[
            shape(queries.shape, f32),
            shape((1, tok, 2 * width), f32),
            shape((NZ * NC, 1, 128), f32),
        ],
        in_specs=[VMEM] * (NY + 1),
        out_specs=[VMEM] * 3,
        compiler_params=PARAMS,
    )(*back, pieces)
    squares = lax.all_to_all(squares, ("z", "core"), 0, 0, tiled=True)
    home = [seen[0]] + [turn(seen[k], "y", NY, k) for k in range(1, NY)]
    ndata = lax.axis_size("dp")
    squares = pl.pallas_call(
        fold_kernel,
        out_shape=shape((NY * ndata, 1, 128), f32),
        in_specs=[VMEM],
        out_specs=VMEM,
        compiler_params=PARAMS,
    )(squares)
    squares = lax.all_to_all(squares, ("y", "dp"), 0, 0, tiled=True)
    attended = pl.pallas_call(
        attended_kernel,
        out_shape=shape(queries.shape, bf16),
        in_specs=[VMEM] * NY,
        out_specs=VMEM,
        compiler_params=PARAMS,
    )(*home)
    count = float(ndata * NZ * NY * NC * tok * (wide + 2 * width))
    out_query, out_key, out_value = pl.pallas_call(
        functools.partial(scale_kernel, count),
        out_shape=(shape(queries.shape, bf16), shape(keys.shape, bf16), shape(values.shape, bf16)),
        in_specs=[VMEM] * 3,
        out_specs=(VMEM,) * 3,
        compiler_params=PARAMS,
    )(squares, dq, dkv)
    return attended, out_query, out_key, out_value


def solution(mesh):
    ndata = mesh.shape["dp"]
    fine = Mesh(mesh.devices.reshape(NZ, NY, NC, ndata), ("z", "y", "core", "dp"))
    spec = P("dp", ("z", "y", "core"), None)
    return jax.shard_map(
        per_device,
        mesh=fine,
        in_specs=(spec, spec, spec, spec, P("dp", None)),
        out_specs=(spec, spec, spec, spec),
        check_vma=False,
    )
```

```python
import functools
import math

import jax
import jax.numpy as jnp
from jax import lax
from jax.experimental import pallas as pl
from jax.experimental.pallas import tpu as pltpu
from jax.sharding import Mesh
from jax.sharding import PartitionSpec as P

FLOOR = -1e30
NZ, NY, NC = 8, 4, 2
FIELDS = 4
VMEM = pl.BlockSpec(memory_space=pltpu.VMEM)
FAR = pl.BlockSpec(memory_space=pl.ANY)
SMEM = pl.BlockSpec(memory_space=pltpu.SMEM)
ALONE = pltpu.CompilerParams(vmem_limit_bytes=62 * 1024 * 1024)
PARAMS = pltpu.CompilerParams(vmem_limit_bytes=40 * 1024 * 1024)


def dot(a, b, ca, cb):
    return lax.dot_general(a, b, (((ca,), (cb,)), ((), ())), preferred_element_type=jnp.float32)


FIELDS = 4
VMEM = pl.BlockSpec(memory_space=pltpu.VMEM)
FAR = pl.BlockSpec(memory_space=pl.ANY)
SMEM = pl.BlockSpec(memory_space=pltpu.SMEM)
ALONE = pltpu.CompilerParams(vmem_limit_bytes=62 * 1024 * 1024)
PARAMS = pltpu.CompilerParams(vmem_limit_bytes=40 * 1024 * 1024)


def dot(a, b, ca, cb):
    return lax.dot_general(a, b, (((ca,), (cb,)), ((), ())), preferred_element_type=jnp.float32)


def visits(doc_starts, tok, z, y, c):
    nctx = NZ * NY * NC
    half = tok // 2
    source = jnp.tile((y + jnp.arange(NY, dtype=jnp.int32)) % NY, 2)
    upper = jnp.repeat(jnp.arange(2, dtype=jnp.int32), NY)
    base = (z * NY + source) * NC + c
    run = jnp.where(upper == 1, 2 * nctx - 1 - base, base)
    starts = doc_starts // half
    begin = jnp.max(jnp.where(starts[None, :] <= run[:, None], starts[None, :], 0), axis=1)
    first = jnp.min(begin.reshape(2, NY), axis=1) // 2
    last = jnp.max(run.reshape(2, NY), axis=1) // 2
    low0 = (first - y + NY - 1) // NY
    high0 = jnp.minimum((last - y + NY) // NY, NZ)
    low1 = (nctx - 1 - y - last + NY - 1) // NY
    high1 = jnp.minimum((nctx - 1 - y - first + NY) // NY, NZ)
    count0 = jnp.maximum(high0 - low0, 0)
    count1 = jnp.maximum(high1 - low1, 0)
    sides = jnp.stack([low0, count0, low1, count1], axis=1).reshape(-1)
    runs = jnp.stack([run, begin, upper * NY + source], axis=1).reshape(-1)
    own = jnp.stack([y, c])
    return jnp.concatenate([sides, runs, own]).astype(jnp.int32)


class Tile:
    def __init__(self, info, pairs_ref, heads):
        self.info, self.pairs = info, pairs_ref
        self.keys = pairs_ref.shape[1]
        self.half = self.keys // 2
        self.width = pairs_ref.shape[2] // 2
        self.cols = heads * self.half
        self.runs = 2 * NZ * NY * NC
        own = 2 * FIELDS + 2 * NY * 3
        self.y = info[own]
        self.c = info[own + 1]
        row = lax.broadcasted_iota(jnp.int32, (self.keys, 1), 0)
        core = jnp.where(row < self.half, self.c, 1 - self.c)
        rest = row % self.half
        self.row_low = core * self.half + rest
        self.row_high = (self.runs - 1 - core) * self.half + rest
        self.col_rest = lax.broadcasted_iota(jnp.int32, (1, self.cols), 1) % self.half

    def field(self, side, n):
        return self.info[side * FIELDS + n]

    def run(self, side, k, n):
        return self.info[2 * FIELDS + (side * NY + k) * 3 + n]

    def row(self, side, k):
        return pl.ds(self.run(side, k, 2), 1)

    def count(self, side):
        return self.field(side, 1) + self.field(side, 3)

    def steps(self, side):
        return (self.count(side) + 1) // 2

    def columns(self, side):
        own = [self.run(side, k, 0) * self.half + self.col_rest for k in range(NY)]
        first = [jnp.full((1, self.cols), self.run(side, k, 1) * self.half) for k in range(NY)]
        return jnp.concatenate(own, axis=1), jnp.concatenate(first, axis=1)

    def blocks(self, side, i):
        def place(n):
            lower = self.field(side, 1)
            return jnp.where(
                n >= lower, self.field(side, 2) + NZ + n - lower, self.field(side, 0) + n
            )

        second = jnp.minimum(2 * i + 1, self.count(side) - 1)
        return place(2 * i), place(second)

    def positions(self, side, i, blocks):
        parts = []
        for n, b in enumerate(blocks):
            step = NY * NC * self.half
            low = b * step + self.y * NC * self.half + self.row_low
            high = self.row_high - (b - NZ) * step - self.y * NC * self.half
            at = jnp.where(b >= NZ, high, low)
            if n:
                at = jnp.where(2 * i + 1 < self.count(side), at, jnp.int32(2**30))
            parts.append(at)
        return jnp.concatenate(parts, axis=0)


def two(ref, blocks, lanes, axis):
    return jnp.concatenate([ref[b, :, lanes] for b in blocks], axis=axis)


def gather_kernel(mine, other, pairs, turned):
    half = mine.shape[1] // 2
    width = mine.shape[2] // 2
    for b in range(2 * NZ):
        rows = slice((b // NZ) * half, (b // NZ + 1) * half)
        block = jnp.concatenate([mine[b % NZ, rows], other[b % NZ, rows]], axis=0)
        pairs[b] = block
        turned[b] = block.astype(jnp.float32).T.astype(turned.dtype)


def queries_of(refs, side, second, half, width, heads):
    rows = pl.ds(pl.multiple_of(side * half, half), half)
    lanes = [(heads * second + h) * width for h in range(heads)]
    return jnp.concatenate([r[0, rows, at : at + width] for r in refs for at in lanes], axis=0)


def forward_kernel(heads, info, a0, a1, a2, a3, pairs, turned, u_ref, stats_ref, s_scr, st_scr):
    tile = Tile(info, pairs, heads)
    half, width, cols = tile.half, tile.width, tile.cols
    log2_scale = math.log2(math.e) / math.sqrt(width)
    groups = 2 * tile.keys // 8
    asked = (a0, a1, a2, a3)

    def one_side(side, _):
        queries = queries_of(asked, side, 0, half, width, heads)
        own, first = tile.columns(side)
        steps = tile.steps(side)

        def scores(i, biggest):
            blocks = tile.blocks(side, i)
            at = tile.positions(side, i, blocks)
            s = dot(two(pairs, blocks, slice(0, width), 0), queries, 1, 1)
            s = jnp.where((at <= own) & (at >= first), s, FLOOR)
            s_scr[i] = s
            return jnp.maximum(biggest, jnp.max(s.reshape(groups, 8, NY * cols), axis=0))

        biggest = lax.fori_loop(0, steps, scores, jnp.full((8, NY * cols), FLOOR, jnp.float32))
        top = jnp.max(biggest, axis=0, keepdims=True)
        u_ref[side] = jnp.zeros(u_ref.shape[1:], jnp.float32)

        def sums(i, total):
            e = jnp.exp2((s_scr[i] - top) * log2_scale)
            total = total + jnp.sum(e.reshape(groups, 8, NY * cols), axis=0)
            values_t = jnp.concatenate([turned[b, width:, :] for b in tile.blocks(side, i)], axis=1)
            u_ref[side] += dot(values_t, e.astype(jnp.bfloat16), 1, 0)
            return total

        total = lax.fori_loop(0, steps, sums, jnp.zeros((8, NY * cols), jnp.float32))
        total = jnp.sum(total, axis=0, keepdims=True)
        do_t = queries_of(asked, side, 1, half, width, heads).astype(jnp.float32).T
        seen = jnp.sum(u_ref[side] * do_t, axis=0, keepdims=True)
        for k in range(NY):
            for n, whole in enumerate((top, total, seen)):
                st_scr[n, tile.row(side, k), :] = whole[:, k * cols : (k + 1) * cols]
        return 0

    lax.fori_loop(0, 2, one_side, 0)
    for k in range(NY):
        stats_ref[k] = st_scr[...]


def backward_kernel(
    heads, info, a0, a1, a2, a3, u_ref, pairs, turned, stats,
    t0, t1, t2, t3, o0, o1, o2, o3, dmine, dother, dacc, dq_scr, st_scr,
):
    tile = Tile(info, pairs, heads)
    half, width, cols, keys = tile.half, tile.width, tile.cols, tile.keys
    scale = 1.0 / math.sqrt(width)
    log2_scale = scale * math.log2(math.e)
    asked = (a0, a1, a2, a3)
    dacc[...] = jnp.zeros_like(dacc)

    tops = [stats[k, 0] for k in range(NY)]
    top = functools.reduce(jnp.maximum, tops)
    weights = [jnp.exp2((t - top) * log2_scale) for t in tops]
    den = sum(w * stats[k, 1] for k, w in enumerate(weights))
    inverse = 1.0 / den
    st_scr[0] = top * log2_scale + jnp.log2(den)
    st_scr[1] = sum(w * stats[k, 2] for k, w in enumerate(weights)) * inverse
    st_scr[2] = jnp.exp2((stats[tile.y, 0] - top) * log2_scale) * inverse

    def one_side(side, _):
        queries = queries_of(asked, side, 0, half, width, heads)
        grads = queries_of(asked, side, 1, half, width, heads)
        own, first = tile.columns(side)
        lse2, delta, share = (
            jnp.concatenate([st_scr[n, tile.row(side, k), :] for k in range(NY)], axis=1)
            for n in range(3)
        )
        dq_scr[...] = jnp.zeros_like(dq_scr)

        def visit(i, _):
            blocks = tile.blocks(side, i)
            at = tile.positions(side, i, blocks)
            s = dot(two(pairs, blocks, slice(0, width), 0), queries, 1, 1)
            s = jnp.where((at <= own) & (at >= first), s, FLOOR)
            p = jnp.exp2(s * log2_scale - lse2)
            dp = dot(two(pairs, blocks, slice(width, 2 * width), 0), grads, 1, 1)
            ds = (p * (dp - delta)).astype(jnp.bfloat16)
            dk = dot(ds, queries, 1, 0)
            dv = dot(p.astype(jnp.bfloat16), grads, 1, 0)
            for m, b in enumerate(blocks):
                dacc[b, :, :width] += dk[m * keys : (m + 1) * keys]
                dacc[b, :, width:] += dv[m * keys : (m + 1) * keys]
            keys_t = jnp.concatenate([turned[b, :width, :] for b in blocks], axis=1)
            dq_scr[...] += dot(keys_t, ds, 1, 0)
            return 0

        lax.fori_loop(0, tile.steps(side), visit, 0)
        att = (u_ref[side] * share).T.astype(jnp.bfloat16)
        dq = (dq_scr[...] * scale).T.astype(jnp.bfloat16)
        rows = pl.ds(pl.multiple_of(side * half, half), half)
        for whole, outs in ((att, (t0, t1, t2, t3)), (dq, (o0, o1, o2, o3))):
            for k, out in enumerate(outs):
                for h in range(heads):
                    at = k * cols + h * half
                    out[0, rows, h * width : (h + 1) * width] = whole[at : at + half]
        return 0

    lax.fori_loop(0, 2, one_side, 0)
    for b in range(2 * NZ):
        rows = slice((b // NZ) * half, (b // NZ + 1) * half)
        for out, part in ((dmine, slice(0, half)), (dother, slice(half, keys))):
            out[b % NZ, rows, :width] = (dacc[b, part, :width] * scale).astype(out.dtype)
            out[b % NZ, rows, width:] = dacc[b, part, width:].astype(out.dtype)


def combine_kernel(o0, o1, o2, o3, dkv, dq_ref, dkv_ref, sq_ref):
    parts = [o[0].astype(jnp.float32) for o in (o0, o1, o2, o3)]
    dq = (parts[0] + parts[1]) + (parts[2] + parts[3])
    dq_ref[0] = dq
    total = functools.reduce(jnp.add, [dkv[k].astype(jnp.float32) for k in range(NZ)])
    dkv_ref[0] = total
    squares = jnp.sum(dq * dq) + jnp.sum(total * total)
    sq_ref[...] = jnp.full(sq_ref.shape, squares, jnp.float32)


def attended_kernel(order, a0, a1, a2, a3, out):
    del order
    parts = [a[...].astype(jnp.float32) for a in (a0, a1, a2, a3)]
    out[...] = ((parts[0] + parts[1]) + (parts[2] + parts[3])).astype(out.dtype)


def fold_kernel(parts, out):
    total = functools.reduce(jnp.add, [parts[k] for k in range(parts.shape[0])])
    for k in range(out.shape[0]):
        out[k] = total


def scale_kernel(count, sums, dq, dkv, oq, ok, ov, used):
    lanes = sums.shape[2]
    total = sums[0]
    for k in range(1, sums.shape[0]):
        total = total + sums[k]
    factor = lax.rsqrt(total / count + 1e-06)
    used[...] = factor
    for h in range(dq.shape[2] // lanes):
        at = slice(h * lanes, (h + 1) * lanes)
        oq[0, :, at] = (dq[0, :, at] * factor).astype(oq.dtype)
    width = ok.shape[2]
    ok[0] = (dkv[0, :, :width] * factor).astype(ok.dtype)
    ov[0] = (dkv[0, :, width:] * factor).astype(ov.dtype)


def spread_kernel(keys, values, order, copies):
    del order
    width = keys.shape[2]
    for k in range(copies.shape[0]):
        copies[k, :, :width] = keys[0]
        copies[k, :, width:] = values[0]


def join_kernel(left, right, *outs):
    wide = left.shape[2]
    for out in outs:
        out[:, :, :wide] = left[...]
        out[:, :, wide:] = right[...]


def far_kernel(left, right, out, sems):
    wide = left.shape[2]
    copies = [
        pltpu.make_async_copy(left, out.at[:, :, :wide], sems.at[0]),
        pltpu.make_async_copy(right, out.at[:, :, wide:], sems.at[1]),
    ]
    for copy in copies:
        copy.start()
    for copy in copies:
        copy.wait()


def turn(x, axis, size, by):
    return lax.ppermute(x, axis, [(i, (i + by) % size) for i in range(size)])


def per_device(queries, keys, values, grad_out, doc_starts):
    tok = queries.shape[1]
    wide = queries.shape[2]
    width = keys.shape[2]
    heads = wide // width
    half = tok // 2
    cols = heads * half
    z, y, c = (lax.axis_index(a) for a in ("z", "y", "core"))
    info = visits(doc_starts[0], tok, z, y, c)

    block = jax.ShapeDtypeStruct((1, tok, 2 * wide), keys.dtype)
    far = pl.pallas_call(
        far_kernel,
        out_shape=[block],
        in_specs=[FAR] * 2,
        out_specs=[VMEM],
        scratch_shapes=[pltpu.SemaphoreType.DMA((2,))],
        compiler_params=ALONE,
    )(queries, grad_out)
    copies = pl.pallas_call(
        spread_kernel,
        out_shape=jax.ShapeDtypeStruct((NZ, tok, 2 * width), keys.dtype),
        in_specs=[VMEM] * 3,
        out_specs=VMEM,
        compiler_params=PARAMS,
    )(keys, values, far[0])
    asked, *near = pl.pallas_call(
        join_kernel,
        out_shape=[block] * (NY - 1),
        in_specs=[VMEM] * 2,
        out_specs=[VMEM] * (NY - 1),
        compiler_params=PARAMS,
    )(queries, grad_out)
    mine = lax.all_to_all(copies, "z", 0, 0, tiled=True)
    around = {0: asked, 1: turn(near[0], "y", NY, -1), 2: turn(far[0], "y", NY, -2), 3: turn(near[1], "y", NY, -3)}
    other = turn(mine, "core", NC, 1)

    f32, bf16 = jnp.float32, jnp.bfloat16
    shape = jax.ShapeDtypeStruct
    pairs, turned = pl.pallas_call(
        gather_kernel,
        out_shape=(shape((2 * NZ, tok, 2 * width), bf16), shape((2 * NZ, 2 * width, tok), bf16)),
        in_specs=[VMEM] * 2,
        out_specs=(VMEM,) * 2,
        compiler_params=PARAMS,
    )(mine, other)
    stat = (3, 2 * NY, cols)

    asks = [around[k] for k in range(NY)]
    u, stats = pl.pallas_call(
        functools.partial(forward_kernel, heads),
        out_shape=(shape((2, width, NY * cols), f32), shape((NY,) + stat, f32)),
        in_specs=[SMEM] + [VMEM] * (NY + 2),
        out_specs=(VMEM, VMEM),
        scratch_shapes=[pltpu.VMEM((NZ, 2 * tok, NY * cols), f32), pltpu.VMEM(stat, f32)],
        compiler_params=PARAMS,
    )(info, *asks, pairs, turned)
    stats = lax.all_to_all(stats, "y", 0, 0, tiled=True)
    *sent, dmine, dother = pl.pallas_call(
        functools.partial(backward_kernel, heads),
        out_shape=[shape(queries.shape, bf16)] * (2 * NY)
        + [shape(mine.shape, f32), shape(mine.shape, bf16)],
        in_specs=[SMEM] + [VMEM] * (NY + 4),
        out_specs=[VMEM] * (2 * NY + 2),
        scratch_shapes=[
            pltpu.VMEM((2 * NZ, tok, 2 * width), f32),
            pltpu.VMEM((width, NY * cols), f32),
            pltpu.VMEM(stat, f32),
        ],
        compiler_params=PARAMS,
    )(info, *asks, u, pairs, turned, stats)
    seen, sent = sent[:NY], sent[NY:]
    back = [sent[0]] + [turn(sent[k], "y", NY, k) for k in range(1, NY)]
    from_core = turn(dother, "core", NC, 1)
    pair = (dmine + from_core.astype(f32)).astype(bf16)
    pieces = lax.all_to_all(pair, "z", 0, 0, tiled=True)
    dq, dkv, squares = pl.pallas_call(
        combine_kernel,
        out_shape=[
            shape(queries.shape, f32),
            shape((1, tok, 2 * width), f32),
            shape((NZ * NC, 1, 128), f32),
        ],
        in_specs=[VMEM] * (NY + 1),
        out_specs=[VMEM] * 3,
        compiler_params=PARAMS,
    )(*back, pieces)
    squares = lax.all_to_all(squares, ("z", "core"), 0, 0, tiled=True)
    home = [seen[0]] + [turn(seen[k], "y", NY, k) for k in range(1, NY)]
    ndata = lax.axis_size("dp")
    squares = pl.pallas_call(
        fold_kernel,
        out_shape=shape((NY * ndata, 1, 128), f32),
        in_specs=[VMEM],
        out_specs=VMEM,
        compiler_params=PARAMS,
    )(squares)
    squares = lax.all_to_all(squares, ("y", "dp"), 0, 0, tiled=True)
    count = float(ndata * NZ * NY * NC * tok * (wide + 2 * width))
    out_query, out_key, out_value, used = pl.pallas_call(
        functools.partial(scale_kernel, count),
        out_shape=(
            shape(queries.shape, bf16),
            shape(keys.shape, bf16),
            shape(values.shape, bf16),
            shape((1, 128), f32),
        ),
        in_specs=[VMEM] * 3,
        out_specs=(VMEM,) * 4,
        compiler_params=PARAMS,
    )(squares, dq, dkv)
    attended = pl.pallas_call(
        attended_kernel,
        out_shape=shape(queries.shape, bf16),
        in_specs=[VMEM] + [VMEM] * NY,
        out_specs=VMEM,
        compiler_params=PARAMS,
    )(used, *home)
    return attended, out_query, out_key, out_value


def solution(mesh):
    ndata = mesh.shape["dp"]
    fine = Mesh(mesh.devices.reshape(NZ, NY, NC, ndata), ("z", "y", "core", "dp"))
    spec = P("dp", ("z", "y", "core"), None)
    return jax.shard_map(
        per_device,
        mesh=fine,
        in_specs=(spec, spec, spec, spec, P("dp", None)),
        out_specs=(spec, spec, spec, spec),
        check_vma=False,
    )
```

```python
import functools
import math

import jax
import jax.numpy as jnp
from jax import lax
from jax.experimental import pallas as pl
from jax.experimental.pallas import tpu as pltpu
from jax.sharding import Mesh
from jax.sharding import PartitionSpec as P

FLOOR = -1e30
NZ, NY, NC = 8, 4, 2
FIELDS = 4
VMEM = pl.BlockSpec(memory_space=pltpu.VMEM)
FAR = pl.BlockSpec(memory_space=pl.ANY)
SMEM = pl.BlockSpec(memory_space=pltpu.SMEM)
ALONE = pltpu.CompilerParams(vmem_limit_bytes=62 * 1024 * 1024)
PARAMS = pltpu.CompilerParams(vmem_limit_bytes=40 * 1024 * 1024)


def dot(a, b, ca, cb):
    return lax.dot_general(a, b, (((ca,), (cb,)), ((), ())), preferred_element_type=jnp.float32)


FIELDS = 4
VMEM = pl.BlockSpec(memory_space=pltpu.VMEM)
FAR = pl.BlockSpec(memory_space=pl.ANY)
SMEM = pl.BlockSpec(memory_space=pltpu.SMEM)
ALONE = pltpu.CompilerParams(vmem_limit_bytes=62 * 1024 * 1024)
PARAMS = pltpu.CompilerParams(vmem_limit_bytes=40 * 1024 * 1024)


def dot(a, b, ca, cb):
    return lax.dot_general(a, b, (((ca,), (cb,)), ((), ())), preferred_element_type=jnp.float32)


def visits(doc_starts, tok, z, y, c):
    nctx = NZ * NY * NC
    half = tok // 2
    source = jnp.tile((y + jnp.arange(NY, dtype=jnp.int32)) % NY, 2)
    upper = jnp.repeat(jnp.arange(2, dtype=jnp.int32), NY)
    base = (z * NY + source) * NC + c
    run = jnp.where(upper == 1, 2 * nctx - 1 - base, base)
    starts = doc_starts // half
    begin = jnp.max(jnp.where(starts[None, :] <= run[:, None], starts[None, :], 0), axis=1)
    first = jnp.min(begin.reshape(2, NY), axis=1) // 2
    last = jnp.max(run.reshape(2, NY), axis=1) // 2
    low0 = (first - y + NY - 1) // NY
    high0 = jnp.minimum((last - y + NY) // NY, NZ)
    low1 = (nctx - 1 - y - last + NY - 1) // NY
    high1 = jnp.minimum((nctx - 1 - y - first + NY) // NY, NZ)
    count0 = jnp.maximum(high0 - low0, 0)
    count1 = jnp.maximum(high1 - low1, 0)
    sides = jnp.stack([low0, count0, low1, count1], axis=1).reshape(-1)
    runs = jnp.stack([run, begin, upper * NY + source], axis=1).reshape(-1)
    own = jnp.stack([y, c])
    return jnp.concatenate([sides, runs, own]).astype(jnp.int32)


class Tile:
    def __init__(self, info, pairs_ref, heads):
        self.info, self.pairs = info, pairs_ref
        self.keys = pairs_ref.shape[1]
        self.half = self.keys // 2
        self.width = pairs_ref.shape[2] // 2
        self.cols = heads * self.half
        self.runs = 2 * NZ * NY * NC
        own = 2 * FIELDS + 2 * NY * 3
        self.y = info[own]
        self.c = info[own + 1]
        row = lax.broadcasted_iota(jnp.int32, (self.keys, 1), 0)
        core = jnp.where(row < self.half, self.c, 1 - self.c)
        rest = row % self.half
        self.row_low = core * self.half + rest
        self.row_high = (self.runs - 1 - core) * self.half + rest
        self.col_rest = lax.broadcasted_iota(jnp.int32, (1, self.cols), 1) % self.half

    def field(self, side, n):
        return self.info[side * FIELDS + n]

    def run(self, side, k, n):
        return self.info[2 * FIELDS + (side * NY + k) * 3 + n]

    def row(self, side, k):
        return pl.ds(self.run(side, k, 2), 1)

    def count(self, side):
        return self.field(side, 1) + self.field(side, 3)

    def steps(self, side):
        return (self.count(side) + 1) // 2

    def columns(self, side):
        own = [self.run(side, k, 0) * self.half + self.col_rest for k in range(NY)]
        first = [jnp.full((1, self.cols), self.run(side, k, 1) * self.half) for k in range(NY)]
        return jnp.concatenate(own, axis=1), jnp.concatenate(first, axis=1)

    def blocks(self, side, i):
        def place(n):
            lower = self.field(side, 1)
            return jnp.where(
                n >= lower, self.field(side, 2) + NZ + n - lower, self.field(side, 0) + n
            )

        second = jnp.minimum(2 * i + 1, self.count(side) - 1)
        return place(2 * i), place(second)

    def positions(self, side, i, blocks):
        parts = []
        for n, b in enumerate(blocks):
            step = NY * NC * self.half
            low = b * step + self.y * NC * self.half + self.row_low
            high = self.row_high - (b - NZ) * step - self.y * NC * self.half
            at = jnp.where(b >= NZ, high, low)
            if n:
                at = jnp.where(2 * i + 1 < self.count(side), at, jnp.int32(2**30))
            parts.append(at)
        return jnp.concatenate(parts, axis=0)


def two(ref, blocks, lanes, axis):
    return jnp.concatenate([ref[b, :, lanes] for b in blocks], axis=axis)


def gather_kernel(mine, other, pairs, turned):
    half = mine.shape[1] // 2
    width = mine.shape[2] // 2
    for b in range(2 * NZ):
        rows = slice((b // NZ) * half, (b // NZ + 1) * half)
        block = jnp.concatenate([mine[b % NZ, rows], other[b % NZ, rows]], axis=0)
        pairs[b] = block
        turned[b] = block.astype(jnp.float32).T.astype(turned.dtype)


def queries_of(refs, side, second, half, width, heads):
    rows = pl.ds(pl.multiple_of(side * half, half), half)
    lanes = [(heads * second + h) * width for h in range(heads)]
    return jnp.concatenate([r[0, rows, at : at + width] for r in refs for at in lanes], axis=0)


def forward_kernel(heads, info, a0, a1, a2, a3, pairs, turned, u_ref, stats_ref, s_scr, st_scr):
    tile = Tile(info, pairs, heads)
    half, width, cols = tile.half, tile.width, tile.cols
    log2_scale = math.log2(math.e) / math.sqrt(width)
    groups = 2 * tile.keys // 8
    asked = (a0, a1, a2, a3)

    def one_side(side, _):
        queries = queries_of(asked, side, 0, half, width, heads)
        own, first = tile.columns(side)
        steps = tile.steps(side)

        def scores(i, biggest):
            blocks = tile.blocks(side, i)
            at = tile.positions(side, i, blocks)
            s = dot(two(pairs, blocks, slice(0, width), 0), queries, 1, 1)
            s = jnp.where((at <= own) & (at >= first), s, FLOOR)
            s_scr[i] = s
            return jnp.maximum(biggest, jnp.max(s.reshape(groups, 8, NY * cols), axis=0))

        biggest = lax.fori_loop(0, steps, scores, jnp.full((8, NY * cols), FLOOR, jnp.float32))
        top = jnp.max(biggest, axis=0, keepdims=True)
        u_ref[side] = jnp.zeros(u_ref.shape[1:], jnp.float32)

        def sums(i, total):
            e = jnp.exp2((s_scr[i] - top) * log2_scale)
            total = total + jnp.sum(e.reshape(groups, 8, NY * cols), axis=0)
            values_t = jnp.concatenate([turned[b, width:, :] for b in tile.blocks(side, i)], axis=1)
            u_ref[side] += dot(values_t, e.astype(jnp.bfloat16), 1, 0)
            return total

        total = lax.fori_loop(0, steps, sums, jnp.zeros((8, NY * cols), jnp.float32))
        total = jnp.sum(total, axis=0, keepdims=True)
        do_t = queries_of(asked, side, 1, half, width, heads).astype(jnp.float32).T
        seen = jnp.sum(u_ref[side] * do_t, axis=0, keepdims=True)
        for k in range(NY):
            for n, whole in enumerate((top, total, seen)):
                st_scr[n, tile.row(side, k), :] = whole[:, k * cols : (k + 1) * cols]
        return 0

    lax.fori_loop(0, 2, one_side, 0)
    for k in range(NY):
        stats_ref[k] = st_scr[...]


def backward_kernel(
    heads, info, a0, a1, a2, a3, u_ref, pairs, turned, stats,
    t0, t1, t3, o0, o1, o2, o3, dmine, dother, dacc, dq_scr, st_scr,
):
    tile = Tile(info, pairs, heads)
    half, width, cols, keys = tile.half, tile.width, tile.cols, tile.keys
    scale = 1.0 / math.sqrt(width)
    log2_scale = scale * math.log2(math.e)
    asked = (a0, a1, a2, a3)
    dacc[...] = jnp.zeros_like(dacc)

    tops = [stats[k, 0] for k in range(NY)]
    top = functools.reduce(jnp.maximum, tops)
    weights = [jnp.exp2((t - top) * log2_scale) for t in tops]
    den = sum(w * stats[k, 1] for k, w in enumerate(weights))
    inverse = 1.0 / den
    st_scr[0] = top * log2_scale + jnp.log2(den)
    st_scr[1] = sum(w * stats[k, 2] for k, w in enumerate(weights)) * inverse
    st_scr[2] = jnp.exp2((stats[tile.y, 0] - top) * log2_scale) * inverse

    def one_side(side, _):
        queries = queries_of(asked, side, 0, half, width, heads)
        grads = queries_of(asked, side, 1, half, width, heads)
        own, first = tile.columns(side)
        lse2, delta, share = (
            jnp.concatenate([st_scr[n, tile.row(side, k), :] for k in range(NY)], axis=1)
            for n in range(3)
        )
        dq_scr[...] = jnp.zeros_like(dq_scr)

        def visit(i, _):
            blocks = tile.blocks(side, i)
            at = tile.positions(side, i, blocks)
            s = dot(two(pairs, blocks, slice(0, width), 0), queries, 1, 1)
            s = jnp.where((at <= own) & (at >= first), s, FLOOR)
            p = jnp.exp2(s * log2_scale - lse2)
            dp = dot(two(pairs, blocks, slice(width, 2 * width), 0), grads, 1, 1)
            ds = (p * (dp - delta)).astype(jnp.bfloat16)
            dk = dot(ds, queries, 1, 0)
            dv = dot(p.astype(jnp.bfloat16), grads, 1, 0)
            for m, b in enumerate(blocks):
                dacc[b, :, :width] += dk[m * keys : (m + 1) * keys]
                dacc[b, :, width:] += dv[m * keys : (m + 1) * keys]
            keys_t = jnp.concatenate([turned[b, :width, :] for b in blocks], axis=1)
            dq_scr[...] += dot(keys_t, ds, 1, 0)
            return 0

        lax.fori_loop(0, tile.steps(side), visit, 0)
        att = (u_ref[side] * share).T.astype(jnp.bfloat16)
        dq = (dq_scr[...] * scale).T.astype(jnp.bfloat16)
        rows = pl.ds(pl.multiple_of(side * half, half), half)
        wide = heads * width
        for whole, outs in (
            (dq, ((o0, 0), (o1, 0), (o2, 0), (o3, 0))),
            (att, ((t0, 0), (t1, 0), (o2, wide), (t3, 0))),
        ):
            for k, (out, lane) in enumerate(outs):
                for h in range(heads):
                    at = k * cols + h * half
                    lanes = slice(lane + h * width, lane + (h + 1) * width)
                    out[0, rows, lanes] = whole[at : at + half]
        return 0

    lax.fori_loop(0, 2, one_side, 0)
    for b in range(2 * NZ):
        rows = slice((b // NZ) * half, (b // NZ + 1) * half)
        for out, part in ((dmine, slice(0, half)), (dother, slice(half, keys))):
            out[b % NZ, rows, :width] = (dacc[b, part, :width] * scale).astype(out.dtype)
            out[b % NZ, rows, width:] = dacc[b, part, width:].astype(out.dtype)


def combine_kernel(o0, o1, o2, o3, dkv, dq_ref, dkv_ref, sq_ref):
    wide = dq_ref.shape[2]
    parts = [o[0, :, :wide].astype(jnp.float32) for o in (o0, o1, o2, o3)]
    dq = (parts[0] + parts[1]) + (parts[2] + parts[3])
    dq_ref[0] = dq
    total = functools.reduce(jnp.add, [dkv[k].astype(jnp.float32) for k in range(NZ)])
    dkv_ref[0] = total
    squares = jnp.sum(dq * dq) + jnp.sum(total * total)
    sq_ref[...] = jnp.full(sq_ref.shape, squares, jnp.float32)


def attended_kernel(order, a0, a1, a2, a3, out):
    del order
    wide = out.shape[2]
    parts = [a[...].astype(jnp.float32) for a in (a0, a1, a2)]
    parts.append(a3[:, :, wide:].astype(jnp.float32))
    out[...] = ((parts[0] + parts[1]) + (parts[2] + parts[3])).astype(out.dtype)


def fold_kernel(parts, out):
    total = functools.reduce(jnp.add, [parts[k] for k in range(parts.shape[0])])
    for k in range(out.shape[0]):
        out[k] = total


def scale_kernel(count, sums, dq, dkv, oq, ok, ov, used):
    lanes = sums.shape[2]
    total = sums[0]
    for k in range(1, sums.shape[0]):
        total = total + sums[k]
    factor = lax.rsqrt(total / count + 1e-06)
    used[...] = factor
    for h in range(dq.shape[2] // lanes):
        at = slice(h * lanes, (h + 1) * lanes)
        oq[0, :, at] = (dq[0, :, at] * factor).astype(oq.dtype)
    width = ok.shape[2]
    ok[0] = (dkv[0, :, :width] * factor).astype(ok.dtype)
    ov[0] = (dkv[0, :, width:] * factor).astype(ov.dtype)


def spread_kernel(keys, values, order, copies):
    del order
    width = keys.shape[2]
    for k in range(copies.shape[0]):
        copies[k, :, :width] = keys[0]
        copies[k, :, width:] = values[0]


def join_kernel(left, right, *outs):
    wide = left.shape[2]
    for out in outs:
        out[:, :, :wide] = left[...]
        out[:, :, wide:] = right[...]


def far_kernel(left, right, out, done, sems):
    wide = left.shape[2]
    copies = [
        pltpu.make_async_copy(left, out.at[:, :, :wide], sems.at[0]),
        pltpu.make_async_copy(right, out.at[:, :, wide:], sems.at[1]),
    ]
    for copy in copies:
        copy.start()
    done[...] = jnp.zeros_like(done)
    for copy in copies:
        copy.wait()


def turn(x, axis, size, by):
    return lax.ppermute(x, axis, [(i, (i + by) % size) for i in range(size)])


def per_device(queries, keys, values, grad_out, doc_starts):
    tok = queries.shape[1]
    wide = queries.shape[2]
    width = keys.shape[2]
    heads = wide // width
    half = tok // 2
    cols = heads * half
    z, y, c = (lax.axis_index(a) for a in ("z", "y", "core"))
    info = visits(doc_starts[0], tok, z, y, c)

    block = jax.ShapeDtypeStruct((1, tok, 2 * wide), keys.dtype)
    far = pl.pallas_call(
        far_kernel,
        out_shape=[block, jax.ShapeDtypeStruct((8, 128), jnp.float32)],
        in_specs=[FAR] * 2,
        out_specs=[VMEM] * 2,
        scratch_shapes=[pltpu.SemaphoreType.DMA((2,))],
        compiler_params=ALONE,
    )(queries, grad_out)
    copies = pl.pallas_call(
        spread_kernel,
        out_shape=jax.ShapeDtypeStruct((NZ, tok, 2 * width), keys.dtype),
        in_specs=[VMEM] * 3,
        out_specs=VMEM,
        compiler_params=PARAMS,
    )(keys, values, far[1])
    asked, *near = pl.pallas_call(
        join_kernel,
        out_shape=[block] * (NY - 1),
        in_specs=[VMEM] * 2,
        out_specs=[VMEM] * (NY - 1),
        compiler_params=PARAMS,
    )(queries, grad_out)
    mine = lax.all_to_all(copies, "z", 0, 0, tiled=True)
    around = {0: asked, 1: turn(near[0], "y", NY, -1), 2: turn(far[0], "y", NY, -2), 3: turn(near[1], "y", NY, -3)}
    other = turn(mine, "core", NC, 1)

    f32, bf16 = jnp.float32, jnp.bfloat16
    shape = jax.ShapeDtypeStruct
    pairs, turned = pl.pallas_call(
        gather_kernel,
        out_shape=(shape((2 * NZ, tok, 2 * width), bf16), shape((2 * NZ, 2 * width, tok), bf16)),
        in_specs=[VMEM] * 2,
        out_specs=(VMEM,) * 2,
        compiler_params=PARAMS,
    )(mine, other)
    stat = (3, 2 * NY, cols)

    asks = [around[k] for k in range(NY)]
    u, stats = pl.pallas_call(
        functools.partial(forward_kernel, heads),
        out_shape=(shape((2, width, NY * cols), f32), shape((NY,) + stat, f32)),
        in_specs=[SMEM] + [VMEM] * (NY + 2),
        out_specs=(VMEM, VMEM),
        scratch_shapes=[pltpu.VMEM((NZ, 2 * tok, NY * cols), f32), pltpu.VMEM(stat, f32)],
        compiler_params=PARAMS,
    )(info, *asks, pairs, turned)
    stats = lax.all_to_all(stats, "y", 0, 0, tiled=True)
    *sent, dmine, dother = pl.pallas_call(
        functools.partial(backward_kernel, heads),
        out_shape=[shape(queries.shape, bf16)] * (NY + 1)
        + [shape(asked.shape, bf16), shape(queries.shape, bf16)]
        + [shape(mine.shape, f32), shape(mine.shape, bf16)],
        in_specs=[SMEM] + [VMEM] * (NY + 4),
        out_specs=[VMEM] * (2 * NY + 1),
        scratch_shapes=[
            pltpu.VMEM((2 * NZ, tok, 2 * width), f32),
            pltpu.VMEM((width, NY * cols), f32),
            pltpu.VMEM(stat, f32),
        ],
        compiler_params=PARAMS,
    )(info, *asks, u, pairs, turned, stats)
    seen, sent = {0: sent[0], 1: sent[1], 3: sent[2]}, sent[3:]
    back = [sent[0]] + [turn(sent[k], "y", NY, k) for k in range(1, NY)]
    from_core = turn(dother, "core", NC, 1)
    pair = (dmine + from_core.astype(f32)).astype(bf16)
    pieces = lax.all_to_all(pair, "z", 0, 0, tiled=True)
    dq, dkv, squares = pl.pallas_call(
        combine_kernel,
        out_shape=[
            shape(queries.shape, f32),
            shape((1, tok, 2 * width), f32),
            shape((NZ * NC, 1, 128), f32),
        ],
        in_specs=[VMEM] * (NY + 1),
        out_specs=[VMEM] * 3,
        compiler_params=PARAMS,
    )(*back, pieces)
    squares = lax.all_to_all(squares, ("z", "core"), 0, 0, tiled=True)
    home = [seen[0]] + [turn(seen[k], "y", NY, k) for k in (1, 3)] + [back[2]]
    ndata = lax.axis_size("dp")
    squares = pl.pallas_call(
        fold_kernel,
        out_shape=shape((NY * ndata, 1, 128), f32),
        in_specs=[VMEM],
        out_specs=VMEM,
        compiler_params=PARAMS,
    )(squares)
    squares = lax.all_to_all(squares, ("y", "dp"), 0, 0, tiled=True)
    count = float(ndata * NZ * NY * NC * tok * (wide + 2 * width))
    out_query, out_key, out_value, used = pl.pallas_call(
        functools.partial(scale_kernel, count),
        out_shape=(
            shape(queries.shape, bf16),
            shape(keys.shape, bf16),
            shape(values.shape, bf16),
            shape((1, 128), f32),
        ),
        in_specs=[VMEM] * 3,
        out_specs=(VMEM,) * 4,
        compiler_params=PARAMS,
    )(squares, dq, dkv)
    attended = pl.pallas_call(
        attended_kernel,
        out_shape=shape(queries.shape, bf16),
        in_specs=[VMEM] + [VMEM] * NY,
        out_specs=VMEM,
        compiler_params=PARAMS,
    )(used, *home)
    return attended, out_query, out_key, out_value


def solution(mesh):
    ndata = mesh.shape["dp"]
    fine = Mesh(mesh.devices.reshape(NZ, NY, NC, ndata), ("z", "y", "core", "dp"))
    spec = P("dp", ("z", "y", "core"), None)
    return jax.shard_map(
        per_device,
        mesh=fine,
        in_specs=(spec, spec, spec, spec, P("dp", None)),
        out_specs=(spec, spec, spec, spec),
        check_vma=False,
    )
```

```python
import functools
import math

import jax
import jax.numpy as jnp
from jax import lax
from jax.experimental import pallas as pl
from jax.experimental.pallas import tpu as pltpu
from jax.sharding import Mesh
from jax.sharding import PartitionSpec as P

FLOOR = -1e30
NZ, NY, NC = 8, 4, 2
FIELDS = 4
VMEM = pl.BlockSpec(memory_space=pltpu.VMEM)
FAR = pl.BlockSpec(memory_space=pl.ANY)
SMEM = pl.BlockSpec(memory_space=pltpu.SMEM)
ALONE = pltpu.CompilerParams(vmem_limit_bytes=62 * 1024 * 1024)
PARAMS = pltpu.CompilerParams(vmem_limit_bytes=40 * 1024 * 1024)


def dot(a, b, ca, cb):
    return lax.dot_general(a, b, (((ca,), (cb,)), ((), ())), preferred_element_type=jnp.float32)


FIELDS = 4
VMEM = pl.BlockSpec(memory_space=pltpu.VMEM)
FAR = pl.BlockSpec(memory_space=pl.ANY)
SMEM = pl.BlockSpec(memory_space=pltpu.SMEM)
ALONE = pltpu.CompilerParams(vmem_limit_bytes=62 * 1024 * 1024)
PARAMS = pltpu.CompilerParams(vmem_limit_bytes=40 * 1024 * 1024)


def dot(a, b, ca, cb):
    return lax.dot_general(a, b, (((ca,), (cb,)), ((), ())), preferred_element_type=jnp.float32)


def visits(doc_starts, tok, z, y, c):
    nctx = NZ * NY * NC
    half = tok // 2
    source = jnp.tile((y + jnp.arange(NY, dtype=jnp.int32)) % NY, 2)
    upper = jnp.repeat(jnp.arange(2, dtype=jnp.int32), NY)
    base = (z * NY + source) * NC + c
    run = jnp.where(upper == 1, 2 * nctx - 1 - base, base)
    starts = doc_starts // half
    begin = jnp.max(jnp.where(starts[None, :] <= run[:, None], starts[None, :], 0), axis=1)
    first = jnp.min(begin.reshape(2, NY), axis=1) // 2
    last = jnp.max(run.reshape(2, NY), axis=1) // 2
    low0 = (first - y + NY - 1) // NY
    high0 = jnp.minimum((last - y + NY) // NY, NZ)
    low1 = (nctx - 1 - y - last + NY - 1) // NY
    high1 = jnp.minimum((nctx - 1 - y - first + NY) // NY, NZ)
    count0 = jnp.maximum(high0 - low0, 0)
    count1 = jnp.maximum(high1 - low1, 0)
    sides = jnp.stack([low0, count0, low1, count1], axis=1).reshape(-1)
    runs = jnp.stack([run, begin, upper * NY + source], axis=1).reshape(-1)
    own = jnp.stack([y, c])
    return jnp.concatenate([sides, runs, own]).astype(jnp.int32)


class Tile:
    def __init__(self, info, pairs_ref, heads):
        self.info, self.pairs = info, pairs_ref
        self.keys = pairs_ref.shape[1]
        self.half = self.keys // 2
        self.width = pairs_ref.shape[2] // 2
        self.cols = heads * self.half
        self.runs = 2 * NZ * NY * NC
        own = 2 * FIELDS + 2 * NY * 3
        self.y = info[own]
        self.c = info[own + 1]
        row = lax.broadcasted_iota(jnp.int32, (self.keys, 1), 0)
        core = jnp.where(row < self.half, self.c, 1 - self.c)
        rest = row % self.half
        self.row_low = core * self.half + rest
        self.row_high = (self.runs - 1 - core) * self.half + rest
        self.col_rest = lax.broadcasted_iota(jnp.int32, (1, self.cols), 1) % self.half

    def field(self, side, n):
        return self.info[side * FIELDS + n]

    def run(self, side, k, n):
        return self.info[2 * FIELDS + (side * NY + k) * 3 + n]

    def row(self, side, k):
        return pl.ds(self.run(side, k, 2), 1)

    def count(self, side):
        return self.field(side, 1) + self.field(side, 3)

    def steps(self, side):
        return (self.count(side) + 1) // 2

    def columns(self, side):
        own = [self.run(side, k, 0) * self.half + self.col_rest for k in range(NY)]
        first = [jnp.full((1, self.cols), self.run(side, k, 1) * self.half) for k in range(NY)]
        return jnp.concatenate(own, axis=1), jnp.concatenate(first, axis=1)

    def blocks(self, side, i):
        def place(n):
            lower = self.field(side, 1)
            return jnp.where(
                n >= lower, self.field(side, 2) + NZ + n - lower, self.field(side, 0) + n
            )

        second = jnp.minimum(2 * i + 1, self.count(side) - 1)
        return place(2 * i), place(second)

    def positions(self, side, i, blocks):
        parts = []
        for n, b in enumerate(blocks):
            step = NY * NC * self.half
            low = b * step + self.y * NC * self.half + self.row_low
            high = self.row_high - (b - NZ) * step - self.y * NC * self.half
            at = jnp.where(b >= NZ, high, low)
            if n:
                at = jnp.where(2 * i + 1 < self.count(side), at, jnp.int32(2**30))
            parts.append(at)
        return jnp.concatenate(parts, axis=0)


def two(ref, blocks, lanes, axis):
    return jnp.concatenate([ref[b, :, lanes] for b in blocks], axis=axis)


def gather_kernel(mine, other, pairs, turned):
    half = mine.shape[1] // 2
    width = mine.shape[2] // 2
    for b in range(2 * NZ):
        rows = slice((b // NZ) * half, (b // NZ + 1) * half)
        block = jnp.concatenate([mine[b % NZ, rows], other[b % NZ, rows]], axis=0)
        pairs[b] = block
        turned[b] = block.astype(jnp.float32).T.astype(turned.dtype)


def queries_of(refs, side, second, half, width, heads):
    rows = pl.ds(pl.multiple_of(side * half, half), half)
    lanes = [(heads * second + h) * width for h in range(heads)]
    return jnp.concatenate([r[0, rows, at : at + width] for r in refs for at in lanes], axis=0)


def forward_kernel(heads, info, a0, a1, a2, a3, pairs, turned, u_ref, stats_ref, s_scr, st_scr):
    tile = Tile(info, pairs, heads)
    half, width, cols = tile.half, tile.width, tile.cols
    log2_scale = math.log2(math.e) / math.sqrt(width)
    groups = 2 * tile.keys // 8
    asked = (a0, a1, a2, a3)

    def one_side(side, _):
        queries = queries_of(asked, side, 0, half, width, heads)
        own, first = tile.columns(side)
        steps = tile.steps(side)

        def scores(i, biggest):
            blocks = tile.blocks(side, i)
            at = tile.positions(side, i, blocks)
            s = dot(two(pairs, blocks, slice(0, width), 0), queries, 1, 1)
            s = jnp.where((at <= own) & (at >= first), s, FLOOR)
            s_scr[i] = s
            return jnp.maximum(biggest, jnp.max(s.reshape(groups, 8, NY * cols), axis=0))

        biggest = lax.fori_loop(0, steps, scores, jnp.full((8, NY * cols), FLOOR, jnp.float32))
        top = jnp.max(biggest, axis=0, keepdims=True)
        u_ref[side] = jnp.zeros(u_ref.shape[1:], jnp.float32)

        def sums(i, total):
            e = jnp.exp2((s_scr[i] - top) * log2_scale)
            total = total + jnp.sum(e.reshape(groups, 8, NY * cols), axis=0)
            values_t = jnp.concatenate([turned[b, width:, :] for b in tile.blocks(side, i)], axis=1)
            u_ref[side] += dot(values_t, e.astype(jnp.bfloat16), 1, 0)
            return total

        total = lax.fori_loop(0, steps, sums, jnp.zeros((8, NY * cols), jnp.float32))
        total = jnp.sum(total, axis=0, keepdims=True)
        do_t = queries_of(asked, side, 1, half, width, heads).astype(jnp.float32).T
        seen = jnp.sum(u_ref[side] * do_t, axis=0, keepdims=True)
        for k in range(NY):
            for n, whole in enumerate((top, total, seen)):
                st_scr[n, tile.row(side, k), :] = whole[:, k * cols : (k + 1) * cols]
        return 0

    lax.fori_loop(0, 2, one_side, 0)
    for k in range(NY):
        stats_ref[k] = st_scr[...]


def backward_kernel(
    heads, info, a0, a1, a2, a3, u_ref, pairs, turned, stats,
    t0, t1, t3, o0, o1, o2, o3, dmine, dother, dacc, dq_scr, st_scr,
):
    tile = Tile(info, pairs, heads)
    half, width, cols, keys = tile.half, tile.width, tile.cols, tile.keys
    scale = 1.0 / math.sqrt(width)
    log2_scale = scale * math.log2(math.e)
    asked = (a0, a1, a2, a3)
    dacc[...] = jnp.zeros_like(dacc)

    tops = [stats[k, 0] for k in range(NY)]
    top = functools.reduce(jnp.maximum, tops)
    weights = [jnp.exp2((t - top) * log2_scale) for t in tops]
    den = sum(w * stats[k, 1] for k, w in enumerate(weights))
    inverse = 1.0 / den
    st_scr[0] = top * log2_scale + jnp.log2(den)
    st_scr[1] = sum(w * stats[k, 2] for k, w in enumerate(weights)) * inverse
    st_scr[2] = jnp.exp2((stats[tile.y, 0] - top) * log2_scale) * inverse

    def one_side(side, _):
        queries = queries_of(asked, side, 0, half, width, heads)
        grads = queries_of(asked, side, 1, half, width, heads)
        own, first = tile.columns(side)
        lse2, delta, share = (
            jnp.concatenate([st_scr[n, tile.row(side, k), :] for k in range(NY)], axis=1)
            for n in range(3)
        )
        dq_scr[...] = jnp.zeros_like(dq_scr)

        def visit(i, _):
            blocks = tile.blocks(side, i)
            at = tile.positions(side, i, blocks)
            s = dot(two(pairs, blocks, slice(0, width), 0), queries, 1, 1)
            s = jnp.where((at <= own) & (at >= first), s, FLOOR)
            p = jnp.exp2(s * log2_scale - lse2)
            dp = dot(two(pairs, blocks, slice(width, 2 * width), 0), grads, 1, 1)
            ds = (p * (dp - delta)).astype(jnp.bfloat16)
            dk = dot(ds, queries, 1, 0)
            dv = dot(p.astype(jnp.bfloat16), grads, 1, 0)
            for m, b in enumerate(blocks):
                dacc[b, :, :width] += dk[m * keys : (m + 1) * keys]
                dacc[b, :, width:] += dv[m * keys : (m + 1) * keys]
            keys_t = jnp.concatenate([turned[b, :width, :] for b in blocks], axis=1)
            dq_scr[...] += dot(keys_t, ds, 1, 0)
            return 0

        lax.fori_loop(0, tile.steps(side), visit, 0)
        att = (u_ref[side] * share).T.astype(jnp.bfloat16)
        dq = (dq_scr[...] * scale).T.astype(jnp.bfloat16)
        rows = pl.ds(pl.multiple_of(side * half, half), half)
        wide = heads * width
        for whole, outs in (
            (dq, ((o0, 0), (o1, 0), (o2, 0), (o3, 0))),
            (att, ((t0, 0), (t1, 0), (o2, wide), (t3, 0))),
        ):
            for k, (out, lane) in enumerate(outs):
                for h in range(heads):
                    at = k * cols + h * half
                    lanes = slice(lane + h * width, lane + (h + 1) * width)
                    out[0, rows, lanes] = whole[at : at + half]
        return 0

    lax.fori_loop(0, 2, one_side, 0)
    for b in range(2 * NZ):
        rows = slice((b // NZ) * half, (b // NZ + 1) * half)
        for out, part in ((dmine, slice(0, half)), (dother, slice(half, keys))):
            out[b % NZ, rows, :width] = (dacc[b, part, :width] * scale).astype(out.dtype)
            out[b % NZ, rows, width:] = dacc[b, part, width:].astype(out.dtype)


def combine_kernel(o0, o1, o2, o3, dkv, dq_ref, dkv_ref, sq_ref):
    wide = dq_ref.shape[2]
    parts = [o[0, :, :wide].astype(jnp.float32) for o in (o0, o1, o2, o3)]
    dq = (parts[0] + parts[1]) + (parts[2] + parts[3])
    dq_ref[0] = dq
    total = functools.reduce(jnp.add, [dkv[k].astype(jnp.float32) for k in range(NZ)])
    dkv_ref[0] = total
    squares = jnp.sum(dq * dq) + jnp.sum(total * total)
    sq_ref[...] = jnp.full(sq_ref.shape, squares, jnp.float32)


def release_kernel(order, a1, a3, b1, b3):
    del order
    b1[...] = a1[...]
    b3[...] = a3[...]


def attended_kernel(order, a0, a1, a2, a3, out):
    del order
    wide = out.shape[2]
    parts = [a[...].astype(jnp.float32) for a in (a0, a1, a2)]
    parts.append(a3[:, :, wide:].astype(jnp.float32))
    out[...] = ((parts[0] + parts[1]) + (parts[2] + parts[3])).astype(out.dtype)


def fold_kernel(parts, out):
    total = functools.reduce(jnp.add, [parts[k] for k in range(parts.shape[0])])
    for k in range(out.shape[0]):
        out[k] = total


def scale_kernel(count, sums, dq, dkv, oq, ok, ov, used):
    lanes = sums.shape[2]
    total = sums[0]
    for k in range(1, sums.shape[0]):
        total = total + sums[k]
    factor = lax.rsqrt(total / count + 1e-06)
    used[...] = factor
    for h in range(dq.shape[2] // lanes):
        at = slice(h * lanes, (h + 1) * lanes)
        oq[0, :, at] = (dq[0, :, at] * factor).astype(oq.dtype)
    width = ok.shape[2]
    ok[0] = (dkv[0, :, :width] * factor).astype(ok.dtype)
    ov[0] = (dkv[0, :, width:] * factor).astype(ov.dtype)


def spread_kernel(keys, values, order, copies):
    del order
    width = keys.shape[2]
    for k in range(copies.shape[0]):
        copies[k, :, :width] = keys[0]
        copies[k, :, width:] = values[0]


def join_kernel(left, right, *outs):
    wide = left.shape[2]
    for out in outs:
        out[:, :, :wide] = left[...]
        out[:, :, wide:] = right[...]


def far_kernel(left, right, out, done, sems):
    wide = left.shape[2]
    copies = [
        pltpu.make_async_copy(left, out.at[:, :, :wide], sems.at[0]),
        pltpu.make_async_copy(right, out.at[:, :, wide:], sems.at[1]),
    ]
    for copy in copies:
        copy.start()
    done[...] = jnp.zeros_like(done)
    for copy in copies:
        copy.wait()


def turn(x, axis, size, by):
    return lax.ppermute(x, axis, [(i, (i + by) % size) for i in range(size)])


def per_device(queries, keys, values, grad_out, doc_starts):
    tok = queries.shape[1]
    wide = queries.shape[2]
    width = keys.shape[2]
    heads = wide // width
    half = tok // 2
    cols = heads * half
    z, y, c = (lax.axis_index(a) for a in ("z", "y", "core"))
    info = visits(doc_starts[0], tok, z, y, c)

    block = jax.ShapeDtypeStruct((1, tok, 2 * wide), keys.dtype)
    far = pl.pallas_call(
        far_kernel,
        out_shape=[block, jax.ShapeDtypeStruct((8, 128), jnp.float32)],
        in_specs=[FAR] * 2,
        out_specs=[VMEM] * 2,
        scratch_shapes=[pltpu.SemaphoreType.DMA((2,))],
        compiler_params=ALONE,
    )(queries, grad_out)
    copies = pl.pallas_call(
        spread_kernel,
        out_shape=jax.ShapeDtypeStruct((NZ, tok, 2 * width), keys.dtype),
        in_specs=[VMEM] * 3,
        out_specs=VMEM,
        compiler_params=PARAMS,
    )(keys, values, far[1])
    asked, *near = pl.pallas_call(
        join_kernel,
        out_shape=[block] * (NY - 1),
        in_specs=[VMEM] * 2,
        out_specs=[VMEM] * (NY - 1),
        compiler_params=PARAMS,
    )(queries, grad_out)
    mine = lax.all_to_all(copies, "z", 0, 0, tiled=True)
    around = {0: asked, 1: turn(near[0], "y", NY, -1), 2: turn(far[0], "y", NY, -2), 3: turn(near[1], "y", NY, -3)}
    other = turn(mine, "core", NC, 1)

    f32, bf16 = jnp.float32, jnp.bfloat16
    shape = jax.ShapeDtypeStruct
    pairs, turned = pl.pallas_call(
        gather_kernel,
        out_shape=(shape((2 * NZ, tok, 2 * width), bf16), shape((2 * NZ, 2 * width, tok), bf16)),
        in_specs=[VMEM] * 2,
        out_specs=(VMEM,) * 2,
        compiler_params=PARAMS,
    )(mine, other)
    stat = (3, 2 * NY, cols)

    asks = [around[k] for k in range(NY)]
    u, stats = pl.pallas_call(
        functools.partial(forward_kernel, heads),
        out_shape=(shape((2, width, NY * cols), f32), shape((NY,) + stat, f32)),
        in_specs=[SMEM] + [VMEM] * (NY + 2),
        out_specs=(VMEM, VMEM),
        scratch_shapes=[pltpu.VMEM((NZ, 2 * tok, NY * cols), f32), pltpu.VMEM(stat, f32)],
        compiler_params=PARAMS,
    )(info, *asks, pairs, turned)
    stats = lax.all_to_all(stats, "y", 0, 0, tiled=True)
    *sent, dmine, dother = pl.pallas_call(
        functools.partial(backward_kernel, heads),
        out_shape=[shape(queries.shape, bf16)] * (NY + 1)
        + [shape(asked.shape, bf16), shape(queries.shape, bf16)]
        + [shape(mine.shape, f32), shape(mine.shape, bf16)],
        in_specs=[SMEM] + [VMEM] * (NY + 4),
        out_specs=[VMEM] * (2 * NY + 1),
        scratch_shapes=[
            pltpu.VMEM((2 * NZ, tok, 2 * width), f32),
            pltpu.VMEM((width, NY * cols), f32),
            pltpu.VMEM(stat, f32),
        ],
        compiler_params=PARAMS,
    )(info, *asks, u, pairs, turned, stats)
    seen, sent = {0: sent[0], 1: sent[1], 3: sent[2]}, sent[3:]
    back = [sent[0]] + [turn(sent[k], "y", NY, k) for k in range(1, NY)]
    from_core = turn(dother, "core", NC, 1)
    pair = (dmine + from_core.astype(f32)).astype(bf16)
    pieces = lax.all_to_all(pair, "z", 0, 0, tiled=True)
    dq, dkv, squares = pl.pallas_call(
        combine_kernel,
        out_shape=[
            shape(queries.shape, f32),
            shape((1, tok, 2 * width), f32),
            shape((NZ * NC, 1, 128), f32),
        ],
        in_specs=[VMEM] * (NY + 1),
        out_specs=[VMEM] * 3,
        compiler_params=PARAMS,
    )(*back, pieces)
    near1, near3 = pl.pallas_call(
        release_kernel,
        out_shape=[shape(queries.shape, bf16)] * 2,
        in_specs=[VMEM] * 3,
        out_specs=[VMEM] * 2,
        compiler_params=PARAMS,
    )(squares, seen[1], seen[3])
    squares = lax.all_to_all(squares, ("z", "core"), 0, 0, tiled=True)
    home = [seen[0], turn(near1, "y", NY, 1), turn(near3, "y", NY, 3), back[2]]
    ndata = lax.axis_size("dp")
    squares = pl.pallas_call(
        fold_kernel,
        out_shape=shape((NY * ndata, 1, 128), f32),
        in_specs=[VMEM],
        out_specs=VMEM,
        compiler_params=PARAMS,
        cost_estimate=pl.CostEstimate(flops=10**9, transcendentals=0, bytes_accessed=0),
    )(squares)
    squares = lax.all_to_all(squares, ("y", "dp"), 0, 0, tiled=True)
    count = float(ndata * NZ * NY * NC * tok * (wide + 2 * width))
    out_query, out_key, out_value, used = pl.pallas_call(
        functools.partial(scale_kernel, count),
        out_shape=(
            shape(queries.shape, bf16),
            shape(keys.shape, bf16),
            shape(values.shape, bf16),
            shape((1, 128), f32),
        ),
        in_specs=[VMEM] * 3,
        out_specs=(VMEM,) * 4,
        compiler_params=PARAMS,
    )(squares, dq, dkv)
    attended = pl.pallas_call(
        attended_kernel,
        out_shape=shape(queries.shape, bf16),
        in_specs=[VMEM] + [VMEM] * NY,
        out_specs=VMEM,
        compiler_params=PARAMS,
    )(used, *home)
    return attended, out_query, out_key, out_value


def solution(mesh):
    ndata = mesh.shape["dp"]
    fine = Mesh(mesh.devices.reshape(NZ, NY, NC, ndata), ("z", "y", "core", "dp"))
    spec = P("dp", ("z", "y", "core"), None)
    return jax.shard_map(
        per_device,
        mesh=fine,
        in_specs=(spec, spec, spec, spec, P("dp", None)),
        out_specs=(spec, spec, spec, spec),
        check_vma=False,
    )
```

```python
import functools
import math

import jax
import jax.numpy as jnp
from jax import lax
from jax.experimental import pallas as pl
from jax.experimental.pallas import tpu as pltpu
from jax.sharding import Mesh
from jax.sharding import PartitionSpec as P

FLOOR = -1e30
NZ, NY, NC = 8, 4, 2
FIELDS = 4
VMEM = pl.BlockSpec(memory_space=pltpu.VMEM)
FAR = pl.BlockSpec(memory_space=pl.ANY)
SMEM = pl.BlockSpec(memory_space=pltpu.SMEM)
ALONE = pltpu.CompilerParams(vmem_limit_bytes=62 * 1024 * 1024)
PARAMS = pltpu.CompilerParams(vmem_limit_bytes=40 * 1024 * 1024)


def dot(a, b, ca, cb):
    return lax.dot_general(a, b, (((ca,), (cb,)), ((), ())), preferred_element_type=jnp.float32)


FIELDS = 4
VMEM = pl.BlockSpec(memory_space=pltpu.VMEM)
FAR = pl.BlockSpec(memory_space=pl.ANY)
SMEM = pl.BlockSpec(memory_space=pltpu.SMEM)
ALONE = pltpu.CompilerParams(vmem_limit_bytes=62 * 1024 * 1024)
PARAMS = pltpu.CompilerParams(vmem_limit_bytes=40 * 1024 * 1024)


def dot(a, b, ca, cb):
    return lax.dot_general(a, b, (((ca,), (cb,)), ((), ())), preferred_element_type=jnp.float32)


def visits(doc_starts, tok, z, y, c):
    nctx = NZ * NY * NC
    half = tok // 2
    source = jnp.tile((y + jnp.arange(NY, dtype=jnp.int32)) % NY, 2)
    upper = jnp.repeat(jnp.arange(2, dtype=jnp.int32), NY)
    base = (z * NY + source) * NC + c
    run = jnp.where(upper == 1, 2 * nctx - 1 - base, base)
    starts = doc_starts // half
    begin = jnp.max(jnp.where(starts[None, :] <= run[:, None], starts[None, :], 0), axis=1)
    first = jnp.min(begin.reshape(2, NY), axis=1) // 2
    last = jnp.max(run.reshape(2, NY), axis=1) // 2
    low0 = (first - y + NY - 1) // NY
    high0 = jnp.minimum((last - y + NY) // NY, NZ)
    low1 = (nctx - 1 - y - last + NY - 1) // NY
    high1 = jnp.minimum((nctx - 1 - y - first + NY) // NY, NZ)
    count0 = jnp.maximum(high0 - low0, 0)
    count1 = jnp.maximum(high1 - low1, 0)
    sides = jnp.stack([low0, count0, low1, count1], axis=1).reshape(-1)
    runs = jnp.stack([run, begin, upper * NY + source], axis=1).reshape(-1)
    own = jnp.stack([y, c])
    return jnp.concatenate([sides, runs, own]).astype(jnp.int32)


class Tile:
    def __init__(self, info, pairs_ref, heads):
        self.info, self.pairs = info, pairs_ref
        self.keys = pairs_ref.shape[1]
        self.half = self.keys // 2
        self.width = pairs_ref.shape[2] // 2
        self.cols = heads * self.half
        self.runs = 2 * NZ * NY * NC
        own = 2 * FIELDS + 2 * NY * 3
        self.y = info[own]
        self.c = info[own + 1]
        row = lax.broadcasted_iota(jnp.int32, (self.keys, 1), 0)
        core = jnp.where(row < self.half, self.c, 1 - self.c)
        rest = row % self.half
        self.row_low = core * self.half + rest
        self.row_high = (self.runs - 1 - core) * self.half + rest
        self.col_rest = lax.broadcasted_iota(jnp.int32, (1, self.cols), 1) % self.half

    def field(self, side, n):
        return self.info[side * FIELDS + n]

    def run(self, side, k, n):
        return self.info[2 * FIELDS + (side * NY + k) * 3 + n]

    def row(self, side, k):
        return pl.ds(self.run(side, k, 2), 1)

    def count(self, side):
        return self.field(side, 1) + self.field(side, 3)

    def steps(self, side):
        return (self.count(side) + 1) // 2

    def columns(self, side):
        own = [self.run(side, k, 0) * self.half + self.col_rest for k in range(NY)]
        first = [jnp.full((1, self.cols), self.run(side, k, 1) * self.half) for k in range(NY)]
        return jnp.concatenate(own, axis=1), jnp.concatenate(first, axis=1)

    def blocks(self, side, i):
        def place(n):
            lower = self.field(side, 1)
            return jnp.where(
                n >= lower, self.field(side, 2) + NZ + n - lower, self.field(side, 0) + n
            )

        second = jnp.minimum(2 * i + 1, self.count(side) - 1)
        return place(2 * i), place(second)

    def positions(self, side, i, blocks):
        parts = []
        for n, b in enumerate(blocks):
            step = NY * NC * self.half
            low = b * step + self.y * NC * self.half + self.row_low
            high = self.row_high - (b - NZ) * step - self.y * NC * self.half
            at = jnp.where(b >= NZ, high, low)
            if n:
                at = jnp.where(2 * i + 1 < self.count(side), at, jnp.int32(2**30))
            parts.append(at)
        return jnp.concatenate(parts, axis=0)


def two(ref, blocks, lanes, axis):
    return jnp.concatenate([ref[b, :, lanes] for b in blocks], axis=axis)


def gather_kernel(mine, other, pairs, turned):
    half = mine.shape[1] // 2
    width = mine.shape[2] // 2
    for b in range(2 * NZ):
        rows = slice((b // NZ) * half, (b // NZ + 1) * half)
        block = jnp.concatenate([mine[b % NZ, rows], other[b % NZ, rows]], axis=0)
        pairs[b] = block
        turned[b] = block.astype(jnp.float32).T.astype(turned.dtype)


def queries_of(refs, side, second, half, width, heads):
    rows = pl.ds(pl.multiple_of(side * half, half), half)
    lanes = [(heads * second + h) * width for h in range(heads)]
    return jnp.concatenate([r[0, rows, at : at + width] for r in refs for at in lanes], axis=0)


def forward_kernel(heads, info, a0, a1, a2, a3, pairs, turned, u_ref, stats_ref, s_scr, st_scr):
    tile = Tile(info, pairs, heads)
    half, width, cols = tile.half, tile.width, tile.cols
    log2_scale = math.log2(math.e) / math.sqrt(width)
    groups = 2 * tile.keys // 8
    asked = (a0, a1, a2, a3)

    def one_side(side, _):
        queries = queries_of(asked, side, 0, half, width, heads)
        own, first = tile.columns(side)
        steps = tile.steps(side)

        def scores(i, biggest):
            blocks = tile.blocks(side, i)
            at = tile.positions(side, i, blocks)
            s = dot(two(pairs, blocks, slice(0, width), 0), queries, 1, 1)
            s = jnp.where((at <= own) & (at >= first), s, FLOOR)
            s_scr[i] = s
            return jnp.maximum(biggest, jnp.max(s.reshape(groups, 8, NY * cols), axis=0))

        biggest = lax.fori_loop(0, steps, scores, jnp.full((8, NY * cols), FLOOR, jnp.float32))
        top = jnp.max(biggest, axis=0, keepdims=True)
        u_ref[side] = jnp.zeros(u_ref.shape[1:], jnp.float32)

        def sums(i, total):
            e = jnp.exp2((s_scr[i] - top) * log2_scale)
            total = total + jnp.sum(e.reshape(groups, 8, NY * cols), axis=0)
            values_t = jnp.concatenate([turned[b, width:, :] for b in tile.blocks(side, i)], axis=1)
            u_ref[side] += dot(values_t, e.astype(jnp.bfloat16), 1, 0)
            return total

        total = lax.fori_loop(0, steps, sums, jnp.zeros((8, NY * cols), jnp.float32))
        total = jnp.sum(total, axis=0, keepdims=True)
        do_t = queries_of(asked, side, 1, half, width, heads).astype(jnp.float32).T
        seen = jnp.sum(u_ref[side] * do_t, axis=0, keepdims=True)
        for k in range(NY):
            for n, whole in enumerate((top, total, seen)):
                st_scr[n, tile.row(side, k), :] = whole[:, k * cols : (k + 1) * cols]
        return 0

    lax.fori_loop(0, 2, one_side, 0)
    for k in range(NY):
        stats_ref[k] = st_scr[...]


def backward_kernel(
    heads, info, a0, a1, a2, a3, u_ref, pairs, turned, stats,
    t0, t1, t3, o0, o1, o2, o3, dmine, dother, dacc, dq_scr, st_scr,
):
    tile = Tile(info, pairs, heads)
    half, width, cols, keys = tile.half, tile.width, tile.cols, tile.keys
    scale = 1.0 / math.sqrt(width)
    log2_scale = scale * math.log2(math.e)
    asked = (a0, a1, a2, a3)
    dacc[...] = jnp.zeros_like(dacc)

    tops = [stats[k, 0] for k in range(NY)]
    top = functools.reduce(jnp.maximum, tops)
    weights = [jnp.exp2((t - top) * log2_scale) for t in tops]
    den = sum(w * stats[k, 1] for k, w in enumerate(weights))
    inverse = 1.0 / den
    st_scr[0] = top * log2_scale + jnp.log2(den)
    st_scr[1] = sum(w * stats[k, 2] for k, w in enumerate(weights)) * inverse
    st_scr[2] = jnp.exp2((stats[tile.y, 0] - top) * log2_scale) * inverse

    def one_side(side, _):
        queries = queries_of(asked, side, 0, half, width, heads)
        grads = queries_of(asked, side, 1, half, width, heads)
        own, first = tile.columns(side)
        lse2, delta, share = (
            jnp.concatenate([st_scr[n, tile.row(side, k), :] for k in range(NY)], axis=1)
            for n in range(3)
        )
        dq_scr[...] = jnp.zeros_like(dq_scr)

        def visit(i, _):
            blocks = tile.blocks(side, i)
            at = tile.positions(side, i, blocks)
            s = dot(two(pairs, blocks, slice(0, width), 0), queries, 1, 1)
            s = jnp.where((at <= own) & (at >= first), s, FLOOR)
            p = jnp.exp2(s * log2_scale - lse2)
            dp = dot(two(pairs, blocks, slice(width, 2 * width), 0), grads, 1, 1)
            ds = (p * (dp - delta)).astype(jnp.bfloat16)
            dk = dot(ds, queries, 1, 0)
            dv = dot(p.astype(jnp.bfloat16), grads, 1, 0)
            for m, b in enumerate(blocks):
                dacc[b, :, :width] += dk[m * keys : (m + 1) * keys]
                dacc[b, :, width:] += dv[m * keys : (m + 1) * keys]
            keys_t = jnp.concatenate([turned[b, :width, :] for b in blocks], axis=1)
            dq_scr[...] += dot(keys_t, ds, 1, 0)
            return 0

        lax.fori_loop(0, tile.steps(side), visit, 0)
        att = (u_ref[side] * share).T.astype(jnp.bfloat16)
        dq = (dq_scr[...] * scale).T.astype(jnp.bfloat16)
        rows = pl.ds(pl.multiple_of(side * half, half), half)
        wide = heads * width
        for whole, outs in (
            (dq, ((o0, 0), (o1, 0), (o2, 0), (o3, 0))),
            (att, ((t0, 0), (t1, 0), (o2, wide), (t3, 0))),
        ):
            for k, (out, lane) in enumerate(outs):
                for h in range(heads):
                    at = k * cols + h * half
                    lanes = slice(lane + h * width, lane + (h + 1) * width)
                    out[0, rows, lanes] = whole[at : at + half]
        return 0

    lax.fori_loop(0, 2, one_side, 0)
    for b in range(2 * NZ):
        rows = slice((b // NZ) * half, (b // NZ + 1) * half)
        for out, part in ((dmine, slice(0, half)), (dother, slice(half, keys))):
            out[b % NZ, rows, :width] = (dacc[b, part, :width] * scale).astype(out.dtype)
            out[b % NZ, rows, width:] = dacc[b, part, width:].astype(out.dtype)


def combine_kernel(o0, o1, o2, o3, dkv, dq_ref, dkv_ref, sq_ref):
    wide = dq_ref.shape[2]
    parts = [o[0, :, :wide].astype(jnp.float32) for o in (o0, o1, o2, o3)]
    dq = (parts[0] + parts[1]) + (parts[2] + parts[3])
    dq_ref[0] = dq
    total = functools.reduce(jnp.add, [dkv[k].astype(jnp.float32) for k in range(NZ)])
    dkv_ref[0] = total
    squares = jnp.sum(dq * dq) + jnp.sum(total * total)
    sq_ref[...] = jnp.full(sq_ref.shape, squares, jnp.float32)


def attended_kernel(a0, a1, a2, a3, out):
    wide = out.shape[2]
    parts = [a[...].astype(jnp.float32) for a in (a0, a1, a2)]
    parts.append(a3[:, :, wide:].astype(jnp.float32))
    out[...] = ((parts[0] + parts[1]) + (parts[2] + parts[3])).astype(out.dtype)


def fold_kernel(parts, out):
    total = functools.reduce(jnp.add, [parts[k] for k in range(parts.shape[0])])
    for k in range(out.shape[0]):
        out[k] = total


def scale_kernel(count, sums, dq, dkv, oq, ok, ov):
    lanes = sums.shape[2]
    total = sums[0]
    for k in range(1, sums.shape[0]):
        total = total + sums[k]
    factor = lax.rsqrt(total / count + 1e-06)
    for h in range(dq.shape[2] // lanes):
        at = slice(h * lanes, (h + 1) * lanes)
        oq[0, :, at] = (dq[0, :, at] * factor).astype(oq.dtype)
    width = ok.shape[2]
    ok[0] = (dkv[0, :, :width] * factor).astype(ok.dtype)
    ov[0] = (dkv[0, :, width:] * factor).astype(ov.dtype)


def spread_kernel(keys, values, order, copies):
    del order
    width = keys.shape[2]
    for k in range(copies.shape[0]):
        copies[k, :, :width] = keys[0]
        copies[k, :, width:] = values[0]


def join_kernel(left, right, *outs):
    wide = left.shape[2]
    for out in outs:
        out[:, :, :wide] = left[...]
        out[:, :, wide:] = right[...]


def far_kernel(left, right, out, done, sems):
    wide = left.shape[2]
    copies = [
        pltpu.make_async_copy(left, out.at[:, :, :wide], sems.at[0]),
        pltpu.make_async_copy(right, out.at[:, :, wide:], sems.at[1]),
    ]
    for copy in copies:
        copy.start()
    done[0, 0] = 0
    for copy in copies:
        copy.wait()


def turn(x, axis, size, by):
    return lax.ppermute(x, axis, [(i, (i + by) % size) for i in range(size)])


def per_device(queries, keys, values, grad_out, doc_starts):
    tok = queries.shape[1]
    wide = queries.shape[2]
    width = keys.shape[2]
    heads = wide // width
    half = tok // 2
    cols = heads * half
    z, y, c = (lax.axis_index(a) for a in ("z", "y", "core"))
    info = visits(doc_starts[0], tok, z, y, c)

    block = jax.ShapeDtypeStruct((1, tok, 2 * wide), keys.dtype)
    far = pl.pallas_call(
        far_kernel,
        out_shape=[block, jax.ShapeDtypeStruct((1, 1), jnp.int32)],
        in_specs=[FAR] * 2,
        out_specs=[VMEM, SMEM],
        scratch_shapes=[pltpu.SemaphoreType.DMA((2,))],
        compiler_params=ALONE,
    )(queries, grad_out)
    copies = pl.pallas_call(
        spread_kernel,
        out_shape=jax.ShapeDtypeStruct((NZ, tok, 2 * width), keys.dtype),
        in_specs=[VMEM] * 2 + [SMEM],
        out_specs=VMEM,
        compiler_params=PARAMS,
    )(keys, values, far[1])
    asked, *near = pl.pallas_call(
        join_kernel,
        out_shape=[block] * (NY - 1),
        in_specs=[VMEM] * 2,
        out_specs=[VMEM] * (NY - 1),
        compiler_params=PARAMS,
    )(queries, grad_out)
    mine = lax.all_to_all(copies, "z", 0, 0, tiled=True)
    around = {0: asked, 1: turn(near[0], "y", NY, -1), 2: turn(far[0], "y", NY, -2), 3: turn(near[1], "y", NY, -3)}
    other = turn(mine, "core", NC, 1)

    f32, bf16 = jnp.float32, jnp.bfloat16
    shape = jax.ShapeDtypeStruct
    pairs, turned = pl.pallas_call(
        gather_kernel,
        out_shape=(shape((2 * NZ, tok, 2 * width), bf16), shape((2 * NZ, 2 * width, tok), bf16)),
        in_specs=[VMEM] * 2,
        out_specs=(VMEM,) * 2,
        compiler_params=PARAMS,
    )(mine, other)
    stat = (3, 2 * NY, cols)

    asks = [around[k] for k in range(NY)]
    u, stats = pl.pallas_call(
        functools.partial(forward_kernel, heads),
        out_shape=(shape((2, width, NY * cols), f32), shape((NY,) + stat, f32)),
        in_specs=[SMEM] + [VMEM] * (NY + 2),
        out_specs=(VMEM, VMEM),
        scratch_shapes=[pltpu.VMEM((NZ, 2 * tok, NY * cols), f32), pltpu.VMEM(stat, f32)],
        compiler_params=PARAMS,
    )(info, *asks, pairs, turned)
    stats = lax.all_to_all(stats, "y", 0, 0, tiled=True)
    *sent, dmine, dother = pl.pallas_call(
        functools.partial(backward_kernel, heads),
        out_shape=[shape(queries.shape, bf16)] * (NY + 1)
        + [shape(asked.shape, bf16), shape(queries.shape, bf16)]
        + [shape(mine.shape, f32), shape(mine.shape, bf16)],
        in_specs=[SMEM] + [VMEM] * (NY + 4),
        out_specs=[VMEM] * (2 * NY + 1),
        scratch_shapes=[
            pltpu.VMEM((2 * NZ, tok, 2 * width), f32),
            pltpu.VMEM((width, NY * cols), f32),
            pltpu.VMEM(stat, f32),
        ],
        compiler_params=PARAMS,
    )(info, *asks, u, pairs, turned, stats)
    seen, sent = {0: sent[0], 1: sent[1], 3: sent[2]}, sent[3:]
    back = [sent[0]] + [turn(sent[k], "y", NY, k) for k in range(1, NY)]
    from_core = turn(dother, "core", NC, 1)
    pair = (dmine + from_core.astype(f32)).astype(bf16)
    pieces = lax.all_to_all(pair, "z", 0, 0, tiled=True)
    dq, dkv, squares = pl.pallas_call(
        combine_kernel,
        out_shape=[
            shape(queries.shape, f32),
            shape((1, tok, 2 * width), f32),
            shape((NZ * NC, 1, 128), f32),
        ],
        in_specs=[VMEM] * (NY + 1),
        out_specs=[VMEM] * 3,
        compiler_params=PARAMS,
    )(*back, pieces)
    squares = lax.all_to_all(squares, ("z", "core"), 0, 0, tiled=True)
    home = [seen[0]] + [turn(seen[k], "y", NY, k) for k in (1, 3)] + [back[2]]
    ndata = lax.axis_size("dp")
    squares = pl.pallas_call(
        fold_kernel,
        out_shape=shape((NY * ndata, 1, 128), f32),
        in_specs=[VMEM],
        out_specs=VMEM,
        compiler_params=PARAMS,
    )(squares)
    squares = lax.all_to_all(squares, ("y", "dp"), 0, 0, tiled=True)
    count = float(ndata * NZ * NY * NC * tok * (wide + 2 * width))
    out_query, out_key, out_value = pl.pallas_call(
        functools.partial(scale_kernel, count),
        out_shape=(
            shape(queries.shape, bf16),
            shape(keys.shape, bf16),
            shape(values.shape, bf16),
        ),
        in_specs=[VMEM] * 3,
        out_specs=(VMEM,) * 3,
        compiler_params=PARAMS,
    )(squares, dq, dkv)
    attended = pl.pallas_call(
        attended_kernel,
        out_shape=shape(queries.shape, bf16),
        in_specs=[VMEM] * NY,
        out_specs=VMEM,
        compiler_params=PARAMS,
    )(*home)
    return attended, out_query, out_key, out_value


def solution(mesh):
    ndata = mesh.shape["dp"]
    fine = Mesh(mesh.devices.reshape(NZ, NY, NC, ndata), ("z", "y", "core", "dp"))
    spec = P("dp", ("z", "y", "core"), None)
    return jax.shard_map(
        per_device,
        mesh=fine,
        in_specs=(spec, spec, spec, spec, P("dp", None)),
        out_specs=(spec, spec, spec, spec),
        check_vma=False,
    )
```

```python
import functools
import math

import jax
import jax.numpy as jnp
from jax import lax
from jax.experimental import pallas as pl
from jax.experimental.pallas import tpu as pltpu
from jax.sharding import Mesh
from jax.sharding import PartitionSpec as P

FLOOR = -1e30
NZ, NY, NC = 8, 4, 2
FIELDS = 4
VMEM = pl.BlockSpec(memory_space=pltpu.VMEM)
FAR = pl.BlockSpec(memory_space=pl.ANY)
SMEM = pl.BlockSpec(memory_space=pltpu.SMEM)
ALONE = pltpu.CompilerParams(vmem_limit_bytes=62 * 1024 * 1024)
PARAMS = pltpu.CompilerParams(vmem_limit_bytes=40 * 1024 * 1024)


def dot(a, b, ca, cb):
    return lax.dot_general(a, b, (((ca,), (cb,)), ((), ())), preferred_element_type=jnp.float32)


FIELDS = 4
VMEM = pl.BlockSpec(memory_space=pltpu.VMEM)
FAR = pl.BlockSpec(memory_space=pl.ANY)
SMEM = pl.BlockSpec(memory_space=pltpu.SMEM)
ALONE = pltpu.CompilerParams(vmem_limit_bytes=62 * 1024 * 1024)
PARAMS = pltpu.CompilerParams(vmem_limit_bytes=40 * 1024 * 1024)


def dot(a, b, ca, cb):
    return lax.dot_general(a, b, (((ca,), (cb,)), ((), ())), preferred_element_type=jnp.float32)


def visits(doc_starts, tok, z, y, c):
    nctx = NZ * NY * NC
    half = tok // 2
    source = jnp.tile((y + jnp.arange(NY, dtype=jnp.int32)) % NY, 2)
    upper = jnp.repeat(jnp.arange(2, dtype=jnp.int32), NY)
    base = (z * NY + source) * NC + c
    run = jnp.where(upper == 1, 2 * nctx - 1 - base, base)
    starts = doc_starts // half
    begin = jnp.max(jnp.where(starts[None, :] <= run[:, None], starts[None, :], 0), axis=1)
    first = jnp.min(begin.reshape(2, NY), axis=1) // 2
    last = jnp.max(run.reshape(2, NY), axis=1) // 2
    low0 = (first - y + NY - 1) // NY
    high0 = jnp.minimum((last - y + NY) // NY, NZ)
    low1 = (nctx - 1 - y - last + NY - 1) // NY
    high1 = jnp.minimum((nctx - 1 - y - first + NY) // NY, NZ)
    count0 = jnp.maximum(high0 - low0, 0)
    count1 = jnp.maximum(high1 - low1, 0)
    sides = jnp.stack([low0, count0, low1, count1], axis=1).reshape(-1)
    runs = jnp.stack([run, begin, upper * NY + source], axis=1).reshape(-1)
    own = jnp.stack([y, c])
    return jnp.concatenate([sides, runs, own]).astype(jnp.int32)


class Tile:
    def __init__(self, info, pairs_ref, heads):
        self.info, self.pairs = info, pairs_ref
        self.keys = pairs_ref.shape[1]
        self.half = self.keys // 2
        self.width = pairs_ref.shape[2] // 2
        self.cols = heads * self.half
        self.runs = 2 * NZ * NY * NC
        own = 2 * FIELDS + 2 * NY * 3
        self.y = info[own]
        self.c = info[own + 1]
        row = lax.broadcasted_iota(jnp.int32, (self.keys, 1), 0)
        core = jnp.where(row < self.half, self.c, 1 - self.c)
        rest = row % self.half
        self.row_low = core * self.half + rest
        self.row_high = (self.runs - 1 - core) * self.half + rest
        self.col_rest = lax.broadcasted_iota(jnp.int32, (1, self.cols), 1) % self.half

    def field(self, side, n):
        return self.info[side * FIELDS + n]

    def run(self, side, k, n):
        return self.info[2 * FIELDS + (side * NY + k) * 3 + n]

    def row(self, side, k):
        return pl.ds(self.run(side, k, 2), 1)

    def count(self, side):
        return self.field(side, 1) + self.field(side, 3)

    def steps(self, side):
        return (self.count(side) + 1) // 2

    def columns(self, side):
        own = [self.run(side, k, 0) * self.half + self.col_rest for k in range(NY)]
        first = [jnp.full((1, self.cols), self.run(side, k, 1) * self.half) for k in range(NY)]
        return jnp.concatenate(own, axis=1), jnp.concatenate(first, axis=1)

    def blocks(self, side, i):
        def place(n):
            lower = self.field(side, 1)
            return jnp.where(
                n >= lower, self.field(side, 2) + NZ + n - lower, self.field(side, 0) + n
            )

        second = jnp.minimum(2 * i + 1, self.count(side) - 1)
        return place(2 * i), place(second)

    def positions(self, side, i, blocks):
        parts = []
        for n, b in enumerate(blocks):
            step = NY * NC * self.half
            low = b * step + self.y * NC * self.half + self.row_low
            high = self.row_high - (b - NZ) * step - self.y * NC * self.half
            at = jnp.where(b >= NZ, high, low)
            if n:
                at = jnp.where(2 * i + 1 < self.count(side), at, jnp.int32(2**30))
            parts.append(at)
        return jnp.concatenate(parts, axis=0)


def two(ref, blocks, lanes, axis):
    return jnp.concatenate([ref[b, :, lanes] for b in blocks], axis=axis)


def gather_kernel(mine, other, pairs, turned):
    half = mine.shape[1] // 2
    width = mine.shape[2] // 2
    for b in range(2 * NZ):
        rows = slice((b // NZ) * half, (b // NZ + 1) * half)
        block = jnp.concatenate([mine[b % NZ, rows], other[b % NZ, rows]], axis=0)
        pairs[b] = block
        turned[b] = block.astype(jnp.float32).T.astype(turned.dtype)


def queries_of(refs, side, second, half, width, heads):
    rows = pl.ds(pl.multiple_of(side * half, half), half)
    lanes = [(heads * second + h) * width for h in range(heads)]
    return jnp.concatenate([r[0, rows, at : at + width] for r in refs for at in lanes], axis=0)


def forward_kernel(heads, info, a0, a1, a2, a3, pairs, turned, u_ref, stats_ref, s_scr, st_scr):
    tile = Tile(info, pairs, heads)
    half, width, cols = tile.half, tile.width, tile.cols
    log2_scale = math.log2(math.e) / math.sqrt(width)
    groups = 2 * tile.keys // 8
    asked = (a0, a1, a2, a3)

    def one_side(side, _):
        queries = queries_of(asked, side, 0, half, width, heads)
        own, first = tile.columns(side)
        steps = tile.steps(side)

        def scores(i, biggest):
            blocks = tile.blocks(side, i)
            at = tile.positions(side, i, blocks)
            s = dot(two(pairs, blocks, slice(0, width), 0), queries, 1, 1)
            s = jnp.where((at <= own) & (at >= first), s, FLOOR)
            s_scr[i] = s
            return jnp.maximum(biggest, jnp.max(s.reshape(groups, 8, NY * cols), axis=0))

        biggest = lax.fori_loop(0, steps, scores, jnp.full((8, NY * cols), FLOOR, jnp.float32))
        top = jnp.max(biggest, axis=0, keepdims=True)
        u_ref[side] = jnp.zeros(u_ref.shape[1:], jnp.float32)

        def sums(i, total):
            e = jnp.exp2((s_scr[i] - top) * log2_scale)
            total = total + jnp.sum(e.reshape(groups, 8, NY * cols), axis=0)
            values_t = jnp.concatenate([turned[b, width:, :] for b in tile.blocks(side, i)], axis=1)
            u_ref[side] += dot(values_t, e.astype(jnp.bfloat16), 1, 0)
            return total

        total = lax.fori_loop(0, steps, sums, jnp.zeros((8, NY * cols), jnp.float32))
        total = jnp.sum(total, axis=0, keepdims=True)
        do_t = queries_of(asked, side, 1, half, width, heads).astype(jnp.float32).T
        seen = jnp.sum(u_ref[side] * do_t, axis=0, keepdims=True)
        for k in range(NY):
            for n, whole in enumerate((top, total, seen)):
                st_scr[n, tile.row(side, k), :] = whole[:, k * cols : (k + 1) * cols]
        return 0

    lax.fori_loop(0, 2, one_side, 0)
    for k in range(NY):
        stats_ref[k] = st_scr[...]


def backward_kernel(
    heads, info, a0, a1, a2, a3, u_ref, pairs, turned, stats,
    t0, t1, t3, o0, o1, o2, o3, dmine, dother, dacc, dq_scr, st_scr,
):
    tile = Tile(info, pairs, heads)
    half, width, cols, keys = tile.half, tile.width, tile.cols, tile.keys
    scale = 1.0 / math.sqrt(width)
    log2_scale = scale * math.log2(math.e)
    asked = (a0, a1, a2, a3)
    dacc[...] = jnp.zeros_like(dacc)

    tops = [stats[k, 0] for k in range(NY)]
    top = functools.reduce(jnp.maximum, tops)
    weights = [jnp.exp2((t - top) * log2_scale) for t in tops]
    den = sum(w * stats[k, 1] for k, w in enumerate(weights))
    inverse = 1.0 / den
    st_scr[0] = top * log2_scale + jnp.log2(den)
    st_scr[1] = sum(w * stats[k, 2] for k, w in enumerate(weights)) * inverse
    st_scr[2] = jnp.exp2((stats[tile.y, 0] - top) * log2_scale) * inverse

    def one_side(side, _):
        queries = queries_of(asked, side, 0, half, width, heads)
        grads = queries_of(asked, side, 1, half, width, heads)
        own, first = tile.columns(side)
        lse2, delta, share = (
            jnp.concatenate([st_scr[n, tile.row(side, k), :] for k in range(NY)], axis=1)
            for n in range(3)
        )
        dq_scr[...] = jnp.zeros_like(dq_scr)

        def visit(i, _):
            blocks = tile.blocks(side, i)
            at = tile.positions(side, i, blocks)
            s = dot(two(pairs, blocks, slice(0, width), 0), queries, 1, 1)
            s = jnp.where((at <= own) & (at >= first), s, FLOOR)
            p = jnp.exp2(s * log2_scale - lse2)
            dp = dot(two(pairs, blocks, slice(width, 2 * width), 0), grads, 1, 1)
            ds = (p * (dp - delta)).astype(jnp.bfloat16)
            dk = dot(ds, queries, 1, 0)
            dv = dot(p.astype(jnp.bfloat16), grads, 1, 0)
            for m, b in enumerate(blocks):
                dacc[b, :, :width] += dk[m * keys : (m + 1) * keys]
                dacc[b, :, width:] += dv[m * keys : (m + 1) * keys]
            keys_t = jnp.concatenate([turned[b, :width, :] for b in blocks], axis=1)
            dq_scr[...] += dot(keys_t, ds, 1, 0)
            return 0

        lax.fori_loop(0, tile.steps(side), visit, 0)
        att = (u_ref[side] * share).T.astype(jnp.bfloat16)
        dq = (dq_scr[...] * scale).T.astype(jnp.bfloat16)
        rows = pl.ds(pl.multiple_of(side * half, half), half)
        wide = heads * width
        for whole, outs in (
            (dq, ((o0, 0), (o1, 0), (o2, 0), (o3, 0))),
            (att, ((t0, 0), (t1, 0), (o2, wide), (t3, 0))),
        ):
            for k, (out, lane) in enumerate(outs):
                for h in range(heads):
                    at = k * cols + h * half
                    lanes = slice(lane + h * width, lane + (h + 1) * width)
                    out[0, rows, lanes] = whole[at : at + half]
        return 0

    lax.fori_loop(0, 2, one_side, 0)
    for b in range(2 * NZ):
        rows = slice((b // NZ) * half, (b // NZ + 1) * half)
        for out, part in ((dmine, slice(0, half)), (dother, slice(half, keys))):
            out[b % NZ, rows, :width] = (dacc[b, part, :width] * scale).astype(out.dtype)
            out[b % NZ, rows, width:] = dacc[b, part, width:].astype(out.dtype)


def combine_kernel(o0, o1, o2, o3, dkv, dq_ref, dkv_ref, sq_ref):
    wide = dq_ref.shape[2]
    parts = [o[0, :, :wide].astype(jnp.float32) for o in (o0, o1, o2, o3)]
    dq = (parts[0] + parts[1]) + (parts[2] + parts[3])
    dq_ref[0] = dq
    total = functools.reduce(jnp.add, [dkv[k].astype(jnp.float32) for k in range(NZ)])
    dkv_ref[0] = total
    squares = jnp.sum(dq * dq) + jnp.sum(total * total)
    sq_ref[...] = jnp.full(sq_ref.shape, squares, jnp.float32)


def attended_kernel(a0, a1, a2, a3, out):
    wide = out.shape[2]
    parts = [a[...].astype(jnp.float32) for a in (a0, a1, a2)]
    parts.append(a3[:, :, wide:].astype(jnp.float32))
    out[...] = ((parts[0] + parts[1]) + (parts[2] + parts[3])).astype(out.dtype)


def fold_kernel(parts, out):
    total = functools.reduce(jnp.add, [parts[k] for k in range(parts.shape[0])])
    for k in range(out.shape[0]):
        out[k] = total


def scale_kernel(count, sums, dq, dkv, oq, ok, ov):
    lanes = sums.shape[2]
    total = sums[0]
    for k in range(1, sums.shape[0]):
        total = total + sums[k]
    factor = lax.rsqrt(total / count + 1e-06)
    for h in range(dq.shape[2] // lanes):
        at = slice(h * lanes, (h + 1) * lanes)
        oq[0, :, at] = (dq[0, :, at] * factor).astype(oq.dtype)
    width = ok.shape[2]
    ok[0] = (dkv[0, :, :width] * factor).astype(ok.dtype)
    ov[0] = (dkv[0, :, width:] * factor).astype(ov.dtype)


def spread_kernel(keys, values, copies):
    width = keys.shape[2]
    for k in range(copies.shape[0]):
        copies[k, :, :width] = keys[0]
        copies[k, :, width:] = values[0]


def join_kernel(left, right, *outs):
    wide = left.shape[2]
    for out in outs:
        out[:, :, :wide] = left[...]
        out[:, :, wide:] = right[...]


def far_kernel(left, right, out, sems):
    wide = left.shape[2]
    copies = [
        pltpu.make_async_copy(left, out.at[:, :, :wide], sems.at[0]),
        pltpu.make_async_copy(right, out.at[:, :, wide:], sems.at[1]),
    ]
    for copy in copies:
        copy.start()
    for copy in copies:
        copy.wait()


def turn(x, axis, size, by):
    return lax.ppermute(x, axis, [(i, (i + by) % size) for i in range(size)])


def per_device(queries, keys, values, grad_out, doc_starts):
    tok = queries.shape[1]
    wide = queries.shape[2]
    width = keys.shape[2]
    heads = wide // width
    half = tok // 2
    cols = heads * half
    z, y, c = (lax.axis_index(a) for a in ("z", "y", "core"))
    info = visits(doc_starts[0], tok, z, y, c)

    block = jax.ShapeDtypeStruct((1, tok, 2 * wide), keys.dtype)
    far = pl.pallas_call(
        far_kernel,
        out_shape=[block],
        in_specs=[FAR] * 2,
        out_specs=[VMEM],
        scratch_shapes=[pltpu.SemaphoreType.DMA((2,))],
        compiler_params=ALONE,
    )(queries, grad_out)
    copies = pl.pallas_call(
        spread_kernel,
        out_shape=jax.ShapeDtypeStruct((NZ, tok, 2 * width), keys.dtype),
        in_specs=[VMEM] * 2,
        out_specs=VMEM,
        compiler_params=PARAMS,
    )(keys, values)
    asked, *near = pl.pallas_call(
        join_kernel,
        out_shape=[block] * (NY - 1),
        in_specs=[VMEM] * 2,
        out_specs=[VMEM] * (NY - 1),
        compiler_params=PARAMS,
    )(queries, grad_out)
    mine = lax.all_to_all(copies, "z", 0, 0, tiled=True)
    around = {0: asked, 1: turn(near[0], "y", NY, -1), 2: turn(far[0], "y", NY, -2), 3: turn(near[1], "y", NY, -3)}
    other = turn(mine, "core", NC, 1)

    f32, bf16 = jnp.float32, jnp.bfloat16
    shape = jax.ShapeDtypeStruct
    pairs, turned = pl.pallas_call(
        gather_kernel,
        out_shape=(shape((2 * NZ, tok, 2 * width), bf16), shape((2 * NZ, 2 * width, tok), bf16)),
        in_specs=[VMEM] * 2,
        out_specs=(VMEM,) * 2,
        compiler_params=PARAMS,
    )(mine, other)
    stat = (3, 2 * NY, cols)

    asks = [around[k] for k in range(NY)]
    u, stats = pl.pallas_call(
        functools.partial(forward_kernel, heads),
        out_shape=(shape((2, width, NY * cols), f32), shape((NY,) + stat, f32)),
        in_specs=[SMEM] + [VMEM] * (NY + 2),
        out_specs=(VMEM, VMEM),
        scratch_shapes=[pltpu.VMEM((NZ, 2 * tok, NY * cols), f32), pltpu.VMEM(stat, f32)],
        compiler_params=PARAMS,
    )(info, *asks, pairs, turned)
    stats = lax.all_to_all(stats, "y", 0, 0, tiled=True)
    *sent, dmine, dother = pl.pallas_call(
        functools.partial(backward_kernel, heads),
        out_shape=[shape(queries.shape, bf16)] * (NY + 1)
        + [shape(asked.shape, bf16), shape(queries.shape, bf16)]
        + [shape(mine.shape, f32), shape(mine.shape, bf16)],
        in_specs=[SMEM] + [VMEM] * (NY + 4),
        out_specs=[VMEM] * (2 * NY + 1),
        scratch_shapes=[
            pltpu.VMEM((2 * NZ, tok, 2 * width), f32),
            pltpu.VMEM((width, NY * cols), f32),
            pltpu.VMEM(stat, f32),
        ],
        compiler_params=PARAMS,
    )(info, *asks, u, pairs, turned, stats)
    seen, sent = {0: sent[0], 1: sent[1], 3: sent[2]}, sent[3:]
    back = [sent[0]] + [turn(sent[k], "y", NY, k) for k in range(1, NY)]
    from_core = turn(dother, "core", NC, 1)
    pair = (dmine + from_core.astype(f32)).astype(bf16)
    pieces = lax.all_to_all(pair, "z", 0, 0, tiled=True)
    dq, dkv, squares = pl.pallas_call(
        combine_kernel,
        out_shape=[
            shape(queries.shape, f32),
            shape((1, tok, 2 * width), f32),
            shape((NZ * NC, 1, 128), f32),
        ],
        in_specs=[VMEM] * (NY + 1),
        out_specs=[VMEM] * 3,
        compiler_params=PARAMS,
    )(*back, pieces)
    squares = lax.all_to_all(squares, ("z", "core"), 0, 0, tiled=True)
    home = [seen[0]] + [turn(seen[k], "y", NY, k) for k in (1, 3)] + [back[2]]
    ndata = lax.axis_size("dp")
    squares = pl.pallas_call(
        fold_kernel,
        out_shape=shape((NY * ndata, 1, 128), f32),
        in_specs=[VMEM],
        out_specs=VMEM,
        compiler_params=PARAMS,
    )(squares)
    squares = lax.all_to_all(squares, ("y", "dp"), 0, 0, tiled=True)
    count = float(ndata * NZ * NY * NC * tok * (wide + 2 * width))
    out_query, out_key, out_value = pl.pallas_call(
        functools.partial(scale_kernel, count),
        out_shape=(
            shape(queries.shape, bf16),
            shape(keys.shape, bf16),
            shape(values.shape, bf16),
        ),
        in_specs=[VMEM] * 3,
        out_specs=(VMEM,) * 3,
        compiler_params=PARAMS,
    )(squares, dq, dkv)
    attended = pl.pallas_call(
        attended_kernel,
        out_shape=shape(queries.shape, bf16),
        in_specs=[VMEM] * NY,
        out_specs=VMEM,
        compiler_params=PARAMS,
    )(*home)
    return attended, out_query, out_key, out_value


def solution(mesh):
    ndata = mesh.shape["dp"]
    fine = Mesh(mesh.devices.reshape(NZ, NY, NC, ndata), ("z", "y", "core", "dp"))
    spec = P("dp", ("z", "y", "core"), None)
    return jax.shard_map(
        per_device,
        mesh=fine,
        in_specs=(spec, spec, spec, spec, P("dp", None)),
        out_specs=(spec, spec, spec, spec),
        check_vma=False,
    )
```

```python
import functools
import math

import jax
import jax.numpy as jnp
from jax import lax
from jax.experimental import pallas as pl
from jax.experimental.pallas import tpu as pltpu
from jax.sharding import Mesh
from jax.sharding import PartitionSpec as P

FLOOR = -1e30
NZ, NY, NC = 8, 4, 2
FIELDS = 4
VMEM = pl.BlockSpec(memory_space=pltpu.VMEM)
FAR = pl.BlockSpec(memory_space=pl.ANY)
SMEM = pl.BlockSpec(memory_space=pltpu.SMEM)
ALONE = pltpu.CompilerParams(vmem_limit_bytes=62 * 1024 * 1024)
PARAMS = pltpu.CompilerParams(vmem_limit_bytes=40 * 1024 * 1024)


def dot(a, b, ca, cb):
    return lax.dot_general(a, b, (((ca,), (cb,)), ((), ())), preferred_element_type=jnp.float32)


FIELDS = 4
VMEM = pl.BlockSpec(memory_space=pltpu.VMEM)
FAR = pl.BlockSpec(memory_space=pl.ANY)
SMEM = pl.BlockSpec(memory_space=pltpu.SMEM)
ALONE = pltpu.CompilerParams(vmem_limit_bytes=62 * 1024 * 1024)
PARAMS = pltpu.CompilerParams(vmem_limit_bytes=40 * 1024 * 1024)


def dot(a, b, ca, cb):
    return lax.dot_general(a, b, (((ca,), (cb,)), ((), ())), preferred_element_type=jnp.float32)


def visits(doc_starts, tok, z, y, c):
    nctx = NZ * NY * NC
    half = tok // 2
    source = jnp.tile((y + jnp.arange(NY, dtype=jnp.int32)) % NY, 2)
    upper = jnp.repeat(jnp.arange(2, dtype=jnp.int32), NY)
    base = (z * NY + source) * NC + c
    run = jnp.where(upper == 1, 2 * nctx - 1 - base, base)
    starts = doc_starts // half
    begin = jnp.max(jnp.where(starts[None, :] <= run[:, None], starts[None, :], 0), axis=1)
    first = jnp.min(begin.reshape(2, NY), axis=1) // 2
    last = jnp.max(run.reshape(2, NY), axis=1) // 2
    low0 = (first - y + NY - 1) // NY
    high0 = jnp.minimum((last - y + NY) // NY, NZ)
    low1 = (nctx - 1 - y - last + NY - 1) // NY
    high1 = jnp.minimum((nctx - 1 - y - first + NY) // NY, NZ)
    count0 = jnp.maximum(high0 - low0, 0)
    count1 = jnp.maximum(high1 - low1, 0)
    sides = jnp.stack([low0, count0, low1, count1], axis=1).reshape(-1)
    runs = jnp.stack([run, begin, upper * NY + source], axis=1).reshape(-1)
    own = jnp.stack([y, c])
    return jnp.concatenate([sides, runs, own]).astype(jnp.int32)


class Tile:
    def __init__(self, info, pairs_ref, heads):
        self.info, self.pairs = info, pairs_ref
        self.keys = pairs_ref.shape[1]
        self.half = self.keys // 2
        self.width = pairs_ref.shape[2] // 2
        self.cols = heads * self.half
        self.runs = 2 * NZ * NY * NC
        own = 2 * FIELDS + 2 * NY * 3
        self.y = info[own]
        self.c = info[own + 1]
        row = lax.broadcasted_iota(jnp.int32, (self.keys, 1), 0)
        core = jnp.where(row < self.half, self.c, 1 - self.c)
        rest = row % self.half
        self.row_low = core * self.half + rest
        self.row_high = (self.runs - 1 - core) * self.half + rest
        self.col_rest = lax.broadcasted_iota(jnp.int32, (1, self.cols), 1) % self.half

    def field(self, side, n):
        return self.info[side * FIELDS + n]

    def run(self, side, k, n):
        return self.info[2 * FIELDS + (side * NY + k) * 3 + n]

    def row(self, side, k):
        return pl.ds(self.run(side, k, 2), 1)

    def count(self, side):
        return self.field(side, 1) + self.field(side, 3)

    def steps(self, side):
        return (self.count(side) + 1) // 2

    def columns(self, side):
        own = [self.run(side, k, 0) * self.half + self.col_rest for k in range(NY)]
        first = [jnp.full((1, self.cols), self.run(side, k, 1) * self.half) for k in range(NY)]
        return jnp.concatenate(own, axis=1), jnp.concatenate(first, axis=1)

    def blocks(self, side, i):
        def place(n):
            lower = self.field(side, 1)
            return jnp.where(
                n >= lower, self.field(side, 2) + NZ + n - lower, self.field(side, 0) + n
            )

        second = jnp.minimum(2 * i + 1, self.count(side) - 1)
        return place(2 * i), place(second)

    def positions(self, side, i, blocks):
        parts = []
        for n, b in enumerate(blocks):
            step = NY * NC * self.half
            low = b * step + self.y * NC * self.half + self.row_low
            high = self.row_high - (b - NZ) * step - self.y * NC * self.half
            at = jnp.where(b >= NZ, high, low)
            if n:
                at = jnp.where(2 * i + 1 < self.count(side), at, jnp.int32(2**30))
            parts.append(at)
        return jnp.concatenate(parts, axis=0)


def two(ref, blocks, lanes, axis):
    return jnp.concatenate([ref[b, :, lanes] for b in blocks], axis=axis)


def gather_kernel(mine, other, pairs, turned):
    half = mine.shape[1] // 2
    width = mine.shape[2] // 2
    for b in range(2 * NZ):
        rows = slice((b // NZ) * half, (b // NZ + 1) * half)
        block = jnp.concatenate([mine[b % NZ, rows], other[b % NZ, rows]], axis=0)
        pairs[b] = block
        turned[b] = block.astype(jnp.float32).T.astype(turned.dtype)


def queries_of(refs, side, second, half, width, heads):
    rows = pl.ds(pl.multiple_of(side * half, half), half)
    lanes = [(heads * second + h) * width for h in range(heads)]
    return jnp.concatenate([r[0, rows, at : at + width] for r in refs for at in lanes], axis=0)


def forward_kernel(heads, info, a0, a1, a2, a3, pairs, turned, u_ref, stats_ref, s_scr, st_scr):
    tile = Tile(info, pairs, heads)
    half, width, cols = tile.half, tile.width, tile.cols
    log2_scale = math.log2(math.e) / math.sqrt(width)
    groups = 2 * tile.keys // 8
    asked = (a0, a1, a2, a3)

    def one_side(side, _):
        queries = queries_of(asked, side, 0, half, width, heads)
        own, first = tile.columns(side)
        steps = tile.steps(side)

        def scores(i, biggest):
            blocks = tile.blocks(side, i)
            at = tile.positions(side, i, blocks)
            s = dot(two(pairs, blocks, slice(0, width), 0), queries, 1, 1)
            s = jnp.where((at <= own) & (at >= first), s, FLOOR)
            s_scr[i] = s
            return jnp.maximum(biggest, jnp.max(s.reshape(groups, 8, NY * cols), axis=0))

        biggest = lax.fori_loop(0, steps, scores, jnp.full((8, NY * cols), FLOOR, jnp.float32))
        top = jnp.max(biggest, axis=0, keepdims=True)
        u_ref[side] = jnp.zeros(u_ref.shape[1:], jnp.float32)

        def sums(i, total):
            e = jnp.exp2((s_scr[i] - top) * log2_scale)
            total = total + jnp.sum(e.reshape(groups, 8, NY * cols), axis=0)
            values_t = jnp.concatenate([turned[b, width:, :] for b in tile.blocks(side, i)], axis=1)
            u_ref[side] += dot(values_t, e.astype(jnp.bfloat16), 1, 0)
            return total

        total = lax.fori_loop(0, steps, sums, jnp.zeros((8, NY * cols), jnp.float32))
        total = jnp.sum(total, axis=0, keepdims=True)
        do_t = queries_of(asked, side, 1, half, width, heads).astype(jnp.float32).T
        seen = jnp.sum(u_ref[side] * do_t, axis=0, keepdims=True)
        for k in range(NY):
            for n, whole in enumerate((top, total, seen)):
                st_scr[n, tile.row(side, k), :] = whole[:, k * cols : (k + 1) * cols]
        return 0

    lax.fori_loop(0, 2, one_side, 0)
    for k in range(NY):
        stats_ref[k] = st_scr[...]


def backward_kernel(
    heads, info, a0, a1, a2, a3, u_ref, pairs, turned, stats,
    t0, t1, t3, o0, o1, o2, o3, dmine, dother, dacc, dq_scr, st_scr,
):
    tile = Tile(info, pairs, heads)
    half, width, cols, keys = tile.half, tile.width, tile.cols, tile.keys
    scale = 1.0 / math.sqrt(width)
    log2_scale = scale * math.log2(math.e)
    asked = (a0, a1, a2, a3)
    dacc[...] = jnp.zeros_like(dacc)

    tops = [stats[k, 0] for k in range(NY)]
    top = functools.reduce(jnp.maximum, tops)
    weights = [jnp.exp2((t - top) * log2_scale) for t in tops]
    den = sum(w * stats[k, 1] for k, w in enumerate(weights))
    inverse = 1.0 / den
    st_scr[0] = top * log2_scale + jnp.log2(den)
    st_scr[1] = sum(w * stats[k, 2] for k, w in enumerate(weights)) * inverse
    st_scr[2] = jnp.exp2((stats[tile.y, 0] - top) * log2_scale) * inverse

    def one_side(side, _):
        queries = queries_of(asked, side, 0, half, width, heads)
        grads = queries_of(asked, side, 1, half, width, heads)
        own, first = tile.columns(side)
        lse2, delta, share = (
            jnp.concatenate([st_scr[n, tile.row(side, k), :] for k in range(NY)], axis=1)
            for n in range(3)
        )
        dq_scr[...] = jnp.zeros_like(dq_scr)

        def visit(i, _):
            blocks = tile.blocks(side, i)
            at = tile.positions(side, i, blocks)
            s = dot(two(pairs, blocks, slice(0, width), 0), queries, 1, 1)
            s = jnp.where((at <= own) & (at >= first), s, FLOOR)
            p = jnp.exp2(s * log2_scale - lse2)
            dp = dot(two(pairs, blocks, slice(width, 2 * width), 0), grads, 1, 1)
            ds = (p * (dp - delta)).astype(jnp.bfloat16)
            dk = dot(ds, queries, 1, 0)
            dv = dot(p.astype(jnp.bfloat16), grads, 1, 0)
            for m, b in enumerate(blocks):
                dacc[b, :, :width] += dk[m * keys : (m + 1) * keys]
                dacc[b, :, width:] += dv[m * keys : (m + 1) * keys]
            keys_t = jnp.concatenate([turned[b, :width, :] for b in blocks], axis=1)
            dq_scr[...] += dot(keys_t, ds, 1, 0)
            return 0

        lax.fori_loop(0, tile.steps(side), visit, 0)
        att = (u_ref[side] * share).T.astype(jnp.bfloat16)
        dq = (dq_scr[...] * scale).T.astype(jnp.bfloat16)
        rows = pl.ds(pl.multiple_of(side * half, half), half)
        wide = heads * width
        for whole, outs in (
            (dq, ((o0, 0), (o1, 0), (o2, 0), (o3, 0))),
            (att, ((t0, 0), (t1, 0), (o2, wide), (t3, 0))),
        ):
            for k, (out, lane) in enumerate(outs):
                for h in range(heads):
                    at = k * cols + h * half
                    lanes = slice(lane + h * width, lane + (h + 1) * width)
                    out[0, rows, lanes] = whole[at : at + half]
        return 0

    lax.fori_loop(0, 2, one_side, 0)
    for b in range(2 * NZ):
        rows = slice((b // NZ) * half, (b // NZ + 1) * half)
        for out, part in ((dmine, slice(0, half)), (dother, slice(half, keys))):
            out[b % NZ, rows, :width] = (dacc[b, part, :width] * scale).astype(out.dtype)
            out[b % NZ, rows, width:] = dacc[b, part, width:].astype(out.dtype)


def combine_kernel(o0, o1, o2, o3, dkv, dq_ref, dkv_ref, sq_ref):
    wide = dq_ref.shape[2]
    parts = [o[0, :, :wide].astype(jnp.float32) for o in (o0, o1, o2, o3)]
    dq = (parts[0] + parts[1]) + (parts[2] + parts[3])
    dq_ref[0] = dq
    total = functools.reduce(jnp.add, [dkv[k].astype(jnp.float32) for k in range(NZ)])
    dkv_ref[0] = total
    squares = jnp.sum(dq * dq) + jnp.sum(total * total)
    sq_ref[...] = jnp.full(sq_ref.shape, squares, jnp.float32)


def attended_kernel(a0, a1, a2, a3, out):
    wide = out.shape[2]
    parts = [a[...].astype(jnp.float32) for a in (a0, a1, a2)]
    parts.append(a3[:, :, wide:].astype(jnp.float32))
    out[...] = ((parts[0] + parts[1]) + (parts[2] + parts[3])).astype(out.dtype)


def fold_kernel(parts, out):
    total = functools.reduce(jnp.add, [parts[k] for k in range(parts.shape[0])])
    for k in range(out.shape[0]):
        out[k] = total


def scale_kernel(count, sums, dq, dkv, oq, ok, ov):
    lanes = sums.shape[2]
    total = sums[0]
    for k in range(1, sums.shape[0]):
        total = total + sums[k]
    factor = lax.rsqrt(total / count + 1e-06)
    for h in range(dq.shape[2] // lanes):
        at = slice(h * lanes, (h + 1) * lanes)
        oq[0, :, at] = (dq[0, :, at] * factor).astype(oq.dtype)
    width = ok.shape[2]
    ok[0] = (dkv[0, :, :width] * factor).astype(ok.dtype)
    ov[0] = (dkv[0, :, width:] * factor).astype(ov.dtype)


def spread_kernel(keys, values, copies):
    width = keys.shape[2]
    for k in range(copies.shape[0]):
        copies[k, :, :width] = keys[0]
        copies[k, :, width:] = values[0]


def join_kernel(left, right, *outs):
    wide = left.shape[2]
    for out in outs:
        out[:, :, :wide] = left[...]
        out[:, :, wide:] = right[...]


def far_kernel(left, right, out, sems):
    wide = left.shape[2]
    copies = [
        pltpu.make_async_copy(left, out.at[:, :, :wide], sems.at[0]),
        pltpu.make_async_copy(right, out.at[:, :, wide:], sems.at[1]),
    ]
    for copy in copies:
        copy.start()
    for copy in copies:
        copy.wait()


def turn(x, axis, size, by):
    return lax.ppermute(x, axis, [(i, (i + by) % size) for i in range(size)])


def per_device(queries, keys, values, grad_out, doc_starts):
    tok = queries.shape[1]
    wide = queries.shape[2]
    width = keys.shape[2]
    heads = wide // width
    half = tok // 2
    cols = heads * half
    z, y, c = (lax.axis_index(a) for a in ("z", "y", "core"))
    info = visits(doc_starts[0], tok, z, y, c)

    block = jax.ShapeDtypeStruct((1, tok, 2 * wide), keys.dtype)
    far = pl.pallas_call(
        far_kernel,
        out_shape=[block],
        in_specs=[FAR] * 2,
        out_specs=[VMEM],
        scratch_shapes=[pltpu.SemaphoreType.DMA((2,))],
        compiler_params=ALONE,
    )(queries, grad_out)
    copies = pl.pallas_call(
        spread_kernel,
        out_shape=jax.ShapeDtypeStruct((NZ, tok, 2 * width), keys.dtype),
        in_specs=[VMEM] * 2,
        out_specs=VMEM,
        compiler_params=PARAMS,
    )(keys, values)
    asked, *near = pl.pallas_call(
        join_kernel,
        out_shape=[block] * (NY - 1),
        in_specs=[VMEM] * 2,
        out_specs=[VMEM] * (NY - 1),
        compiler_params=PARAMS,
    )(queries, grad_out)
    mine = lax.all_to_all(copies, "z", 0, 0, tiled=True)
    around = {0: asked, 1: turn(near[0], "y", NY, -1), 2: turn(far[0], "y", NY, -2), 3: turn(near[1], "y", NY, -3)}
    other = turn(mine, "core", NC, 1)

    f32, bf16 = jnp.float32, jnp.bfloat16
    shape = jax.ShapeDtypeStruct
    pairs, turned = pl.pallas_call(
        gather_kernel,
        out_shape=(shape((2 * NZ, tok, 2 * width), bf16), shape((2 * NZ, 2 * width, tok), bf16)),
        in_specs=[VMEM] * 2,
        out_specs=(VMEM,) * 2,
        compiler_params=PARAMS,
    )(mine, other)
    stat = (3, 2 * NY, cols)

    asks = [around[k] for k in range(NY)]
    u, stats = pl.pallas_call(
        functools.partial(forward_kernel, heads),
        out_shape=(shape((2, width, NY * cols), f32), shape((NY,) + stat, f32)),
        in_specs=[SMEM] + [VMEM] * (NY + 2),
        out_specs=(VMEM, VMEM),
        scratch_shapes=[pltpu.VMEM((NZ, 2 * tok, NY * cols), f32), pltpu.VMEM(stat, f32)],
        compiler_params=PARAMS,
    )(info, *asks, pairs, turned)
    stats = lax.all_to_all(stats, "y", 0, 0, tiled=True)
    *sent, dmine, dother = pl.pallas_call(
        functools.partial(backward_kernel, heads),
        out_shape=[shape(queries.shape, bf16)] * (NY + 1)
        + [shape(asked.shape, bf16), shape(queries.shape, bf16)]
        + [shape(mine.shape, bf16)] * 2,
        in_specs=[SMEM] + [VMEM] * (NY + 4),
        out_specs=[VMEM] * (2 * NY + 1),
        scratch_shapes=[
            pltpu.VMEM((2 * NZ, tok, 2 * width), f32),
            pltpu.VMEM((width, NY * cols), f32),
            pltpu.VMEM(stat, f32),
        ],
        compiler_params=PARAMS,
    )(info, *asks, u, pairs, turned, stats)
    seen, sent = {0: sent[0], 1: sent[1], 3: sent[2]}, sent[3:]
    back = [sent[0]] + [turn(sent[k], "y", NY, k) for k in range(1, NY)]
    from_core = turn(dother, "core", NC, 1)
    pair = (dmine.astype(f32) + from_core.astype(f32)).astype(bf16)
    pieces = lax.all_to_all(pair, "z", 0, 0, tiled=True)
    dq, dkv, squares = pl.pallas_call(
        combine_kernel,
        out_shape=[
            shape(queries.shape, f32),
            shape((1, tok, 2 * width), f32),
            shape((NZ * NC, 1, 128), f32),
        ],
        in_specs=[VMEM] * (NY + 1),
        out_specs=[VMEM] * 3,
        compiler_params=PARAMS,
    )(*back, pieces)
    squares = lax.all_to_all(squares, ("z", "core"), 0, 0, tiled=True)
    home = [seen[0]] + [turn(seen[k], "y", NY, k) for k in (1, 3)] + [back[2]]
    ndata = lax.axis_size("dp")
    squares = pl.pallas_call(
        fold_kernel,
        out_shape=shape((NY * ndata, 1, 128), f32),
        in_specs=[VMEM],
        out_specs=VMEM,
        compiler_params=PARAMS,
    )(squares)
    squares = lax.all_to_all(squares, ("y", "dp"), 0, 0, tiled=True)
    count = float(ndata * NZ * NY * NC * tok * (wide + 2 * width))
    out_query, out_key, out_value = pl.pallas_call(
        functools.partial(scale_kernel, count),
        out_shape=(
            shape(queries.shape, bf16),
            shape(keys.shape, bf16),
            shape(values.shape, bf16),
        ),
        in_specs=[VMEM] * 3,
        out_specs=(VMEM,) * 3,
        compiler_params=PARAMS,
    )(squares, dq, dkv)
    attended = pl.pallas_call(
        attended_kernel,
        out_shape=shape(queries.shape, bf16),
        in_specs=[VMEM] * NY,
        out_specs=VMEM,
        compiler_params=PARAMS,
    )(*home)
    return attended, out_query, out_key, out_value


def solution(mesh):
    ndata = mesh.shape["dp"]
    fine = Mesh(mesh.devices.reshape(NZ, NY, NC, ndata), ("z", "y", "core", "dp"))
    spec = P("dp", ("z", "y", "core"), None)
    return jax.shard_map(
        per_device,
        mesh=fine,
        in_specs=(spec, spec, spec, spec, P("dp", None)),
        out_specs=(spec, spec, spec, spec),
        check_vma=False,
    )
```
